32 devices in a mesh: img: 8 (over z, y), patch: 4 (over x, core).
Axes of the slice: x: 2, y: 2, z: 4, core: 2. Of those that a mesh axis runs over, the one named last changes fastest.
Arguments:
- media: bfloat16 [80, 256, 1024], P('img', 'patch'), may hold values from -6 to 6
- latents: bfloat16 [80, 64, 1024], P('img', 'patch'), may hold values from -6 to 6
- counts: int32 [16], P('img'), may hold values from 1 to 5
- gains: float32 [3, 1024], replicated, may hold values from 0.1 to 1.9
- biases: float32 [3, 1024], replicated, may hold values from -3 to 3
- w_query: bfloat16 [1024, 512], replicated, may hold values from -0.1875 to 0.1875
- w_keyval: bfloat16 [1024, 1024], replicated, may hold values from -0.1875 to 0.1875
- w_out: bfloat16 [512, 1024], replicated, may hold values from -2 to 2
- w_up: bfloat16 [1024, 4096], replicated, may hold values from -0.1875 to 0.1875
- w_down: bfloat16 [4096, 1024], replicated, may hold values from -0.09375 to 0.09375
- out_grad: bfloat16 [80, 64, 1024], P('img', 'patch'), may hold values from -6 to 6
Outputs:
- latents_out: bfloat16 [80, 64, 1024], P('img', 'patch')
- media_grad: bfloat16 [80, 256, 1024], P('img', 'patch')
- latent_grad: bfloat16 [80, 64, 1024], P('img', 'patch')
- query_wgrad: float32 [1024, 512], P(None, ('img', 'patch'))
- keyval_wgrad: float32 [1024, 1024], P(None, ('img', 'patch'))
- out_wgrad: float32 [512, 1024], P(None, ('img', 'patch'))
- up_wgrad: float32 [1024, 4096], P(None, ('img', 'patch'))
- down_wgrad: float32 [4096, 1024], P(None, ('img', 'patch'))
- gain_grad: float32 [3, 1024], P(None, ('img', 'patch'))
- bias_grad: float32 [3, 1024], P(None, ('img', 'patch'))
The draws below stay inside these ranges and needn't reach their ends.
All inputs are finite; a program needn't handle non-finite values.
Results may differ from the reference program's by a relative error of at most 0.015.
Values may be sent and summed in bfloat16 or wider, within the bound.
No kernel may reach another device: no remote copies, remote signals or barrier semaphores. Data moves between devices by JAX's collectives and lax.ppermute only.
A program may use at most 192 MiB of HBM per device.

```python
import math
from functools import partial
import jax
import jax.numpy as jnp
from jax import lax

D = 1024
HEADS = 8
LAT = 64
FF = 4096
PATCHES = 256
SLOTS_PER = 5
INNER = 512
SAMPLES = 16
SLOTS = 80


def set_ends(entries, stream_key, least, largest):
    index_at = [jax.random.randint(jax.random.fold_in(stream_key, axis), (), 0, length) for axis, length in enumerate(entries.shape)]
    main_axis = entries.shape.index(max(entries.shape))
    beside = index_at[:main_axis] + [(index_at[main_axis] + 1) % entries.shape[main_axis]] + index_at[main_axis + 1:]
    return entries.at[tuple(index_at)].set(least).at[tuple(beside)].set(largest)


def spiked(values, own_key, source, target, blocks, factor):
    def block_of(position):
        return (jnp.arange(values.shape[position]) // (values.shape[position] // blocks)).reshape((-1,) + (1,) * (values.ndim - 1 - position))

    first = jax.random.permutation(own_key, blocks)[block_of(target)]
    second = (block_of(target) + blocks // 2) % blocks
    return jnp.where((block_of(source) == first) | (block_of(source) == second), factor * values, values)


def level_of(stream_key, shape, cuts, low, largest):
    def one(position, blocks):
        heights = jax.random.uniform(jax.random.fold_in(jax.random.fold_in(stream_key, 6), position), (blocks,), jnp.float32, low / len(cuts), largest / len(cuts))
        return jnp.repeat(jnp.exp(heights), shape[position] // blocks).reshape((-1,) + (1,) * (len(shape) - position - 1))

    level = one(*cuts[0])
    for cut in cuts[1:]:
        level = level * one(*cut)
    return level


def normal_values(own_key, dims, scale, most, split=(), kind=jnp.bfloat16):
    factor_of = level_of(own_key, dims, split, -0.22, 0.18) if split else 1.0
    drawn = jax.random.normal(own_key, dims, jnp.float32) * scale * factor_of
    return jnp.minimum(jnp.maximum(drawn, -most), most).astype(kind)


def noise_with(own_key, dims, width, bound, shards, heavy, kind=jnp.bfloat16):
    drawn = width * jax.random.normal(own_key, dims, jnp.float32)
    if shards:
        drawn = drawn * level_of(own_key, dims, shards, -0.22, 0.18)
    return jnp.clip(spiked(drawn, jax.random.fold_in(own_key, 3), *heavy), -bound, bound).astype(kind)


def setup_inputs(seed: int = 0) -> dict:
    key_of = jax.random.split(jax.random.key(seed), 12)
    return {
        "media": normal_values(key_of[0], (SLOTS, PATCHES, D), 1.0, 6.0, ((0, 8), (1, 4))),
        "latents": normal_values(key_of[1], (SLOTS, LAT, D), 1.0, 6.0, ((0, 8), (1, 4))),
        "counts": set_ends(jax.random.randint(key_of[2], (SAMPLES,), 1, 6), jax.random.fold_in(key_of[2], 1), 1, 5).astype(jnp.int32),
        "gains": jnp.clip(1.0 + 0.18 * jax.random.normal(key_of[3], (3, D), jnp.float32), 0.1, 1.9),
        "biases": normal_values(key_of[4], (3, D), 0.5, 3.0, (), jnp.float32),
        "w_query": normal_values(key_of[5], (D, INNER), D ** -0.5, 0.1875),
        "w_keyval": normal_values(key_of[6], (D, 2 * INNER), D ** -0.5, 0.1875),
        "w_out": normal_values(key_of[7], (INNER, D), (INNER // 64) ** -0.5, 2.0),
        "w_up": normal_values(key_of[8], (D, FF), D ** -0.5, 0.1875),
        "w_down": normal_values(key_of[9], (FF, D), FF ** -0.5, 0.09375),
        "out_grad": noise_with(key_of[10], (SLOTS, LAT, D), 1.0, 6.0, ((0, 8), (1, 4)), (0, 2, 8, 2.0)),
    }


HIGH = lax.Precision.HIGHEST

@jax.custom_vjp
def low(v):
    return lax.optimization_barrier(v.astype(jnp.bfloat16)).astype(jnp.float32)

@jax.custom_vjp
def low_back(v):
    return v

def low_keep(v):
    return (low(v), None)

def low_pass(kept, grad):
    return (grad,)

def back_keep(v):
    return (v, None)

def back_low(kept, grad):
    return (low(grad),)
low.defvjp(low_keep, low_pass)
low_back.defvjp(back_keep, back_low)

def norm_rows(values, norm_gain, norm_bias):
    average = lax.optimization_barrier(jnp.mean(values, axis=-1, keepdims=True))
    centred = values - average
    spread = lax.optimization_barrier(jnp.mean(centred * centred, axis=-1, keepdims=True))
    return centred * lax.rsqrt(spread + 1e-05) * norm_gain + norm_bias

def project(values, weight):
    return jnp.einsum('...c,cd->...d', values, weight, precision=HIGH)

def split_heads(values):
    return values.reshape(values.shape[0], values.shape[1], HEADS, values.shape[2] // HEADS)

def sample_layer(params, group):
    gains, biases, w_query, w_keyval, w_out, w_up, w_down = params
    media_rows, latent_rows, live_mask = group
    inner_width = w_query.shape[1]
    scale_factor = 1.0 / math.sqrt(inner_width // HEADS)
    media_norm = low(norm_rows(media_rows, gains[0], biases[0]))
    latent_norm = low(norm_rows(latent_rows, gains[1], biases[1]))
    queries = low(low_back(project(latent_norm, w_query)))
    key_input = jnp.concatenate([media_norm, latent_norm], axis=1)
    keyval = project(key_input, w_keyval)
    keys = low(low_back(keyval[..., :inner_width]))
    values = low(low_back(keyval[..., inner_width:]))
    scores = low_back(jnp.einsum('gqhd,gkhd->ghqk', split_heads(queries), split_heads(keys), precision=HIGH) * scale_factor)
    probs = jax.nn.softmax(scores, axis=-1)
    attended = jnp.einsum('ghqk,gkhd->gqhd', low(probs), split_heads(values), precision=HIGH).reshape(latent_rows.shape[0], latent_rows.shape[1], inner_width)
    attended = low(low_back(attended))
    hidden_state = latent_rows + low_back(project(attended, w_out))
    ff_norm = low(norm_rows(hidden_state, gains[2], biases[2]))
    pre_act = low_back(project(ff_norm, w_up))
    activated = low(jax.nn.gelu(pre_act, approximate=False))
    return live_mask[:, None, None] * (hidden_state + low_back(project(activated, w_down)))

def reference(media, latents, counts, gains, biases, w_query, w_keyval, w_out, w_up, w_down, out_grad):
    slot_ids = jnp.arange(SLOTS, dtype=jnp.int32)
    repeated = jnp.repeat(counts.astype(jnp.int32), SLOTS_PER)
    live = (slot_ids % SLOTS_PER < repeated).astype(jnp.float32)
    params = (gains.astype(jnp.float32), biases.astype(jnp.float32), w_query.astype(jnp.float32), w_keyval.astype(jnp.float32), w_out.astype(jnp.float32), w_up.astype(jnp.float32), w_down.astype(jnp.float32))
    media_f = media.astype(jnp.float32)
    latent_f = latents.astype(jnp.float32)

    def forward(params_f, media_in, latent_in):
        group_fn = jax.checkpoint(partial(sample_layer, params_f))
        outputs = lax.map(group_fn, (media_in.reshape(SAMPLES, SLOTS_PER, PATCHES, D), latent_in.reshape(SAMPLES, SLOTS_PER, LAT, D), live.reshape(SAMPLES, SLOTS_PER)))
        return outputs.reshape(SLOTS, LAT, D)
    result, pull = jax.vjp(forward, params, media_f, latent_f)
    param_grads, media_back, latent_back = pull(out_grad.astype(jnp.float32))
    gain_back, bias_back, query_back, keyval_back, out_back, up_back, down_back = param_grads
    return (result.astype(jnp.bfloat16), media_back.astype(jnp.bfloat16), latent_back.astype(jnp.bfloat16), query_back, keyval_back, out_back, up_back, down_back, gain_back, bias_back)
```

```python
import math

import jax
import jax.numpy as jnp
from jax import lax
from jax.sharding import PartitionSpec as P

HEADS = 8
SLOTS_PER = 5
EPS = 1e-05
F32 = jnp.float32
BF16 = jnp.bfloat16


def swap(values, axis, bit):
    n = lax.axis_size(axis)
    return lax.ppermute(values, axis, [(k, k ^ bit) for k in range(n)])


def bits_of(axis):
    return [1 << k for k in range(lax.axis_size(axis).bit_length() - 1)]


def halve(pieces, axis, bit):
    mine = (lax.axis_index(axis) // bit) % 2 == 1
    kept, sent = [], []
    for piece in pieces:
        half = piece.shape[0] // 2
        low, high = piece[:half], piece[half:]
        kept.append(jnp.where(mine, high, low))
        sent.append(jnp.where(mine, low, high))
    got = [swap(s, axis, bit) for s in sent]
    return [(k.astype(F32) + g.astype(F32)).astype(k.dtype) for k, g in zip(kept, got)]


def gather_rows(values, axis):
    blocks = values[None]
    for bit in bits_of(axis):
        blocks = jnp.concatenate([blocks, swap(blocks, axis, bit)], axis=0)
    return blocks


def stats(values):
    average = jnp.mean(values, axis=-1, keepdims=True)
    centred = values - average
    spread = jnp.mean(centred * centred, axis=-1, keepdims=True)
    return average, lax.rsqrt(spread + EPS)


def pull(hat, inverse, grad, gain):
    scaled = grad * gain
    first = jnp.mean(scaled, axis=-1, keepdims=True)
    second = jnp.mean(scaled * hat, axis=-1, keepdims=True)
    return inverse * (scaled - first - hat * second)


def gelu_parts(values):
    cdf = 0.5 * (1.0 + lax.erf(values * (1.0 / math.sqrt(2.0))))
    density = jnp.exp(-0.5 * values * values) * (1.0 / math.sqrt(2.0 * math.pi))
    return values * cdf, cdf + values * density


def dot(a, b, dims):
    return lax.dot_general(a, b, (dims, ((), ())), preferred_element_type=F32)


def on_device(
    media, latents, counts, gains, biases, w_query, w_keyval, w_out, w_up, w_down, out_grad
):
    slots, patch_rows, width = media.shape
    latent_rows = latents.shape[1]
    inner = w_query.shape[1]
    head = inner // HEADS
    ff = w_up.shape[1]
    n_img, n_patch = lax.axis_size("img"), lax.axis_size("patch")
    own = lax.axis_index("patch")
    scale = 1.0 / math.sqrt(head)
    rows = slots * latent_rows

    live = (jnp.arange(slots, dtype=jnp.int32) % SLOTS_PER < jnp.repeat(counts, SLOTS_PER)).astype(F32)
    live_rows = jnp.repeat(live, latent_rows)[:, None]
    lat = latents.reshape(rows, width).astype(F32)
    dy = (live_rows * out_grad.reshape(rows, width).astype(F32)).astype(BF16)

    lat_avg, lat_inv = stats(lat)
    lat_hat = (lat - lat_avg) * lat_inv
    lat_low = (lat_hat * gains[1] + biases[1]).astype(BF16)
    q_low = dot(lat_low, w_query, ((1,), (0,))).astype(BF16).reshape(slots, latent_rows, inner)
    q_blocks = gather_rows(q_low, "patch")
    q_all = jnp.concatenate(list(q_blocks), axis=1)
    dy_blocks = gather_rows(dy, "patch").reshape(n_patch * rows, width)

    med = media.astype(F32)
    med_avg, med_inv = stats(med)
    med_hat = (med - med_avg) * med_inv
    med_low = (med_hat * gains[0] + biases[0]).astype(BF16)
    key_input = jnp.concatenate([med_low, lat_low.reshape(slots, latent_rows, width)], axis=1)
    keyval = jnp.einsum("rkc,cd->rkd", key_input, w_keyval, preferred_element_type=F32).astype(BF16)
    keys = keyval[..., :inner].reshape(slots, -1, HEADS, head)
    vals = keyval[..., inner:].reshape(slots, -1, HEADS, head)

    q_heads = q_all.reshape(slots, -1, HEADS, head)
    scores = jnp.einsum("rqhd,rkhd->rhqk", q_heads, keys, preferred_element_type=F32) * scale
    top = jnp.max(scores, axis=-1)
    expd = jnp.exp(scores - top[..., None])
    total = jnp.sum(expd, axis=-1)
    part_low = (expd / total[..., None]).astype(BF16)
    part_out = jnp.einsum("rhqk,rkhd->rqhd", part_low, vals, preferred_element_type=F32).astype(BF16)
    lse = top + jnp.log(total)
    lse_blocks = gather_rows(lse, "patch")
    lse_rows = lse_blocks.reshape(n_patch, slots, HEADS, n_patch, latent_rows)
    per_owner = jnp.stack(
        [jnp.stack([lse_rows[j, :, :, i ^ j] for j in range(n_patch)]) for i in range(n_patch)], axis=3
    )
    lse_top = jnp.max(per_owner, axis=0)
    lse_all = lse_top + jnp.log(jnp.sum(jnp.exp(per_owner - lse_top), axis=0))
    lse_all = lse_all.reshape(slots, HEADS, n_patch * latent_rows)

    part_blocks = part_out.reshape(slots, n_patch, latent_rows, inner)
    attended = 0.0
    for j in range(n_patch):
        block = part_blocks[:, j]
        got = block if j == 0 else swap(block, "patch", j)
        weight = jnp.exp(per_owner[j, :, :, 0] - lse_all[:, :, :latent_rows])
        weight = jnp.repeat(weight.transpose(0, 2, 1), head, axis=-1)
        attended = attended + weight * got.astype(F32)
    attended = attended.reshape(rows, inner)
    att_low = attended.astype(BF16)

    hidden = lat + dot(att_low, w_out, ((1,), (0,)))
    hid_avg, hid_inv = stats(hidden)
    hid_hat = (hidden - hid_avg) * hid_inv
    ff_low = (hid_hat * gains[2] + biases[2]).astype(BF16)
    ff_blocks = gather_rows(ff_low, "patch").reshape(n_patch * rows, width)
    pre = dot(ff_low, w_up, ((1,), (0,)))
    act, slope = gelu_parts(pre)
    act_low = act.astype(BF16)
    result = live_rows * (hidden + dot(act_low, w_down, ((1,), (0,))))
    dpre_low = (slope * dot(dy, w_down, ((1,), (1,)))).astype(BF16)

    def column_blocks(values):
        split = values.reshape(rows, n_img, n_patch, ff // (n_img * n_patch)).transpose(2, 0, 1, 3)
        split = split.reshape(n_patch, rows, ff // n_patch)
        order = jnp.arange(n_patch) ^ own
        moved = lax.all_to_all(split, "patch", 0, 0, tiled=True)
        return jnp.take(moved, order, axis=0).reshape(n_patch * rows, ff // n_patch)

    act_blocks = column_blocks(act_low)
    dpre_blocks = column_blocks(dpre_low)
    up_part = dot(dpre_blocks, ff_blocks, ((0,), (0,))).astype(BF16)
    down_part = dot(dy_blocks, act_blocks, ((0,), (0,))).astype(BF16)
    up_part = up_part.reshape(n_img, -1, width)
    down_part = down_part.reshape(n_img, -1, ff // n_patch)
    ff_parts = [up_part, down_part]
    for bit in reversed(bits_of("img")):
        ff_parts = halve(ff_parts, "img", bit)
    up_grad = ff_parts[0][0].astype(F32).T
    down_piece = ff_parts[1][0].reshape(n_patch, -1, ff // n_patch)
    down_piece = lax.all_to_all(down_piece, "patch", 0, 0, tiled=True)
    down_piece = down_piece.reshape(n_patch, -1, n_img, ff // (n_img * n_patch))
    down_grad = down_piece.transpose(2, 0, 3, 1).reshape(ff, -1).astype(F32)

    dff = dot(dpre_low, w_up, ((1,), (1,)))
    gain_ff = jnp.sum(dff * hid_hat, axis=0)
    bias_ff = jnp.sum(dff, axis=0)
    dhidden = dy.astype(F32) + pull(hid_hat, hid_inv, dff, gains[2])
    dhid_low = dhidden.astype(BF16)
    datt_low = dot(dhid_low, w_out, ((1,), (1,))).astype(BF16)

    delta = jnp.sum(
        (datt_low.astype(F32) * attended).reshape(slots, latent_rows, HEADS, head), axis=-1
    )
    datt_blocks = gather_rows(datt_low.reshape(slots, latent_rows, inner), "patch")
    delta_blocks = gather_rows(delta.transpose(0, 2, 1), "patch")
    datt_all = jnp.concatenate(list(datt_blocks), axis=1).reshape(slots, -1, HEADS, head)
    delta_all = jnp.concatenate(list(delta_blocks), axis=2)
    scores = jnp.einsum("rqhd,rkhd->rhqk", q_heads, keys, preferred_element_type=F32) * scale
    probs = jnp.exp(scores - lse_all[..., None])
    probs_low = probs.astype(BF16)
    dprobs = jnp.einsum("rqhd,rkhd->rhqk", datt_all, vals, preferred_element_type=F32)
    dscores = (probs * (dprobs - delta_all[..., None])).astype(BF16)
    dq_part = jnp.einsum("rhqk,rkhd->rqhd", dscores, keys, preferred_element_type=F32) * scale
    dkeys = jnp.einsum("rhqk,rqhd->rkhd", dscores, q_heads, preferred_element_type=F32) * scale
    dvals = jnp.einsum("rhqk,rqhd->rkhd", probs_low, datt_all, preferred_element_type=F32)
    dkv_low = jnp.concatenate(
        [dkeys.reshape(slots, -1, inner).astype(BF16), dvals.reshape(slots, -1, inner).astype(BF16)], axis=-1
    )
    dq_blocks = dq_part.astype(BF16).reshape(slots, n_patch, latent_rows, inner)
    dq = dq_blocks[:, 0].astype(F32)
    for j in range(1, n_patch):
        dq = dq + swap(dq_blocks[:, j], "patch", j).astype(F32)
    dq_low = dq.reshape(rows, inner).astype(BF16)

    shards = n_img * n_patch
    kv_t = dot(dkv_low.reshape(-1, 2 * inner), key_input.reshape(-1, width), ((0,), (0,))).astype(BF16)
    q_t = dot(dq_low, lat_low, ((0,), (0,))).astype(BF16)
    out_t = dot(dhid_low, att_low, ((0,), (0,))).astype(BF16)

    dinput = jnp.einsum("rkd,cd->rkc", dkv_low, w_keyval, preferred_element_type=F32)
    dmed = dinput[:, :patch_rows]
    dlat = dot(dq_low, w_query, ((1,), (1,))) + dinput[:, patch_rows:].reshape(rows, width)
    media_grad = pull(med_hat, med_inv, dmed, gains[0])
    latent_grad = dhidden + pull(lat_hat, lat_inv, dlat, gains[1])
    gain_media = jnp.sum(dmed * med_hat, axis=(0, 1))
    bias_media = jnp.sum(dmed, axis=(0, 1))
    gain_lat = jnp.sum(dlat * lat_hat, axis=0)
    bias_lat = jnp.sum(dlat, axis=0)

    small = jnp.stack([gain_media, gain_lat, gain_ff, bias_media, bias_lat, bias_ff])
    small = small.reshape(6, shards, width // shards).transpose(1, 0, 2)
    parts = [a.reshape(n_img, n_patch, -1, a.shape[-1]) for a in (kv_t, q_t, out_t)]
    parts.append(small.reshape(n_img, n_patch, 6, width // shards))
    parts = [a.swapaxes(0, 1) for a in parts]
    for bit in reversed(bits_of("patch")):
        parts = halve(parts, "patch", bit)
    parts = [a[0] for a in parts]
    for bit in reversed(bits_of("img")):
        parts = halve(parts, "img", bit)
    kv_grad, q_grad, out_grad_w, small = [a[0] for a in parts]
    return (
        result.reshape(slots, latent_rows, width).astype(BF16),
        media_grad.astype(BF16),
        latent_grad.reshape(slots, latent_rows, width).astype(BF16),
        q_grad.astype(F32).T,
        kv_grad.astype(F32).T,
        out_grad_w.astype(F32).T,
        up_grad,
        down_grad,
        small[:3],
        small[3:],
    )


def solution(mesh):
    rows = P("img", "patch", None)
    shard = P(None, ("img", "patch"))
    return jax.shard_map(
        on_device,
        mesh=mesh,
        in_specs=(rows, rows, P("img"), P(), P(), P(), P(), P(), P(), P(), rows),
        out_specs=(rows, rows, rows) + (shard,) * 7,
        check_vma=False,
    )
```

```python
import functools
import math

import jax
import jax.numpy as jnp
from jax import lax
from jax.experimental import pallas as pl
from jax.experimental.pallas import tpu as pltpu
from jax.sharding import PartitionSpec as P

HEADS = 8
SLOTS_PER = 5
EPS = 1e-05
LANES = 128
F32 = jnp.float32
BF16 = jnp.bfloat16
MIB = 1024 * 1024


def swap(values, axis, bit):
    n = lax.axis_size(axis)
    return lax.ppermute(values, axis, [(k, k ^ bit) for k in range(n)])


def log2(n):
    return n.bit_length() - 1


def gather(values, axis):
    n = lax.axis_size(axis)
    blocks = {0: values}
    bit = n // 2
    while bit:
        for j in list(blocks):
            blocks[j ^ bit] = swap(blocks[j], axis, bit)
        bit //= 2
    return [blocks[j] for j in range(n)]


class Piece:
    def __init__(self, values, digits):
        self.digits = list(digits)
        count = math.prod(size for _, size in digits)
        self.values = values.reshape((count, -1) + values.shape[-1:])

    def step(self, axis, bit):
        at = [name for name, _ in self.digits].index((axis, bit))
        before = math.prod(s for _, s in self.digits[:at])
        after = math.prod(s for _, s in self.digits[at + 1 :])
        inner = self.values.shape[1:]
        split = self.values.reshape((before, 2, after * inner[0]) + inner[1:])
        mine = (lax.axis_index(axis) // bit) % 2 == 1
        low, high = split[:, 0], split[:, 1]
        kept = jnp.where(mine, high, low)
        sent = jnp.where(mine, low, high)
        del self.digits[at]
        shape = (before * after,) + inner
        return kept.reshape(shape), sent.reshape(shape)


def scatter_sum(pieces, order):
    for axis, bit in order:
        both = [piece.step(axis, bit) for piece in pieces]
        got = [swap(sent, axis, bit) for _, sent in both]
        for piece, (kept, _), other in zip(pieces, both, got):
            piece.values = (kept.astype(F32) + other.astype(F32)).astype(kept.dtype)
    return [piece.values[0] for piece in pieces]


def digits_of(axis):
    n = lax.axis_size(axis)
    return [((axis, 1 << k), 2) for k in reversed(range(log2(n)))]


def stats(values):
    average = jnp.mean(values, axis=-1, keepdims=True)
    centred = values - average
    spread = jnp.mean(centred * centred, axis=-1, keepdims=True)
    inverse = lax.rsqrt(spread + EPS)
    return centred * inverse, inverse


def pull(hat, inverse, grad, gain):
    scaled = grad * gain
    first = jnp.mean(scaled, axis=-1, keepdims=True)
    second = jnp.mean(scaled * hat, axis=-1, keepdims=True)
    return inverse * (scaled - first - hat * second)


def gelu_parts(values):
    cdf = 0.5 + 0.5 * lax.erf(values * (1.0 / math.sqrt(2.0)))
    density = jnp.exp(-0.5 * values * values) * (1.0 / math.sqrt(2.0 * math.pi))
    return values * cdf, cdf + values * density


def dot(a, b, dims=((1,), (0,))):
    return lax.dot_general(a, b, (dims, ((), ())), preferred_element_type=F32)


NT = ((1,), (1,))
TN = ((0,), (0,))


def low_lanes(shape):
    return lax.broadcasted_iota(jnp.int32, shape, len(shape) - 1) < LANES // 2


def live_rows(counts_ref, rows, per_slot):
    row = lax.broadcasted_iota(jnp.int32, (rows, 1), 0)
    live = jnp.zeros((rows, 1), F32)
    for sample in range(rows // (per_slot * SLOTS_PER)):
        start = sample * SLOTS_PER * per_slot
        inside = jnp.logical_and(row >= start, row < start + counts_ref[sample] * per_slot)
        live = jnp.where(inside, 1.0, live)
    return live


def paired(block):
    low = low_lanes(block.shape)
    zero = jnp.zeros_like(block)
    return jnp.concatenate([jnp.where(low, block, zero), jnp.where(low, zero, block)], axis=0)


def unpaired(block):
    half = block.shape[0] // 2
    return jnp.where(low_lanes((half, block.shape[1])), block[:half], block[half:])


def flipped(values):
    a, b = values.shape
    tall, wide = -a % LANES, -b % LANES
    if wide:
        values = jnp.concatenate([values, jnp.zeros((a, wide), F32)], axis=1)
    if tall:
        values = jnp.concatenate([values, jnp.zeros((tall, b + wide), F32)], axis=0)
    return values.T[:b, :a]


def call(kernel, grid, ins, outs, scratch=(), vmem=40, flops=0, moved=0, prefetch=0, name=None):
    return pl.pallas_call(
        kernel,
        grid_spec=pltpu.PrefetchScalarGridSpec(
            num_scalar_prefetch=prefetch,
            grid=grid,
            in_specs=ins,
            out_specs=[spec for spec, _ in outs],
            scratch_shapes=list(scratch),
        ),
        out_shape=[shape for _, shape in outs],
        compiler_params=pltpu.CompilerParams(
            vmem_limit_bytes=vmem * MIB, dimension_semantics=("arbitrary",) * len(grid)
        ),
        cost_estimate=pl.CostEstimate(flops=int(flops), bytes_accessed=int(moved), transcendentals=0),
        name=name,
    )


def whole(shape):
    zeros = (0,) * len(shape)
    return pl.BlockSpec(tuple(shape), lambda *_: zeros)


def leading(shape):
    zeros = (0,) * (len(shape) - 1)
    return pl.BlockSpec(tuple(shape), lambda g, *_: (g,) + zeros)


def out(shape, dtype):
    return jax.ShapeDtypeStruct(tuple(shape), dtype)


SMEM = pl.BlockSpec(memory_space=pltpu.SMEM)


def latent_kernel(per_slot, counts, lat, grad, gain, bias, w_query, lat_low, q_low, dy):
    hat, _ = stats(lat[...].astype(F32))
    low = (hat * gain[1:2] + bias[1:2]).astype(BF16)
    lat_low[...] = low
    q_low[...] = dot(low, w_query[...]).astype(BF16)
    live = live_rows(counts, lat.shape[0], per_slot)
    dy[...] = (live * grad[...].astype(F32)).astype(BF16)


def media_kernel(media, lat_low, gain, bias, w_keyval, key_input, keyval):
    n, rows, width = media.shape
    hat, _ = stats(media[...].reshape(n * rows, width).astype(F32))
    low = (hat * gain[0:1] + bias[0:1]).astype(BF16)
    key_input[:, :rows, :] = low.reshape(n, rows, width)
    key_input[:, rows:, :] = lat_low[...].reshape(n, -1, width)
    every = key_input[...].reshape(-1, width)
    keyval[...] = dot(every, w_keyval[...]).astype(BF16).reshape(keyval.shape)


def attend_kernel(peers, scale, *refs):
    qs, (kv,), parts, lses, (held,) = (
        refs[:peers], refs[peers : peers + 1], refs[peers + 1 : 2 * peers + 1],
        refs[2 * peers + 1 : 3 * peers + 1], refs[3 * peers + 1 :],
    )
    n, per_slot, inner = qs[0].shape
    step = pl.program_id(0)
    for s in range(n):
        lane = lax.broadcasted_iota(jnp.int32, (peers * per_slot, LANES), 1)
        logs = jnp.zeros((peers * per_slot, LANES), F32)
        for t in range(inner // LANES):
            cut = slice(t * LANES, (t + 1) * LANES)
            q = paired(jnp.concatenate([ref[s, :, cut] for ref in qs], axis=0))
            k = kv[s, :, cut]
            v = kv[s, :, inner + t * LANES : inner + (t + 1) * LANES]
            scores = dot(q, k, NT) * scale
            top = jnp.max(scores, axis=-1, keepdims=True)
            expd = jnp.exp(scores - top)
            total = jnp.sum(expd, axis=-1, keepdims=True)
            probs = (expd * (1.0 / total)).astype(BF16)
            o = unpaired(dot(probs, v)).astype(BF16)
            lse = top + jnp.log(total)
            half = lse.shape[0] // 2
            logs = jnp.where(lane == 2 * t, lse[:half], logs)
            logs = jnp.where(lane == 2 * t + 1, lse[half:], logs)
            for i in range(peers):
                parts[i][s, :, cut] = o[i * per_slot : (i + 1) * per_slot]
        row = pl.multiple_of((step * n + s) * per_slot, per_slot)
        for i in range(peers):
            held[i, pl.ds(row, per_slot), :] = logs[i * per_slot : (i + 1) * per_slot]

    @pl.when(step == pl.num_programs(0) - 1)
    def _():
        for i in range(peers):
            lses[i][...] = held[i].T[: lses[i].shape[0], : lses[i].shape[1]]


def mix_kernel(peers, *refs):
    parts, lses = refs[:peers], refs[peers : 2 * peers]
    lat, w_out, gain, bias, attended, att_low, hidden, ff_low, lse_out = refs[2 * peers :]
    rows, inner = attended.shape
    logs = [ref[...] for ref in lses]
    top = functools.reduce(jnp.maximum, logs)
    lse = top + jnp.log(sum(jnp.exp(v - top) for v in logs))
    lse_out[...] = lse
    weights = flipped(jnp.concatenate([jnp.exp(v - lse) for v in logs], axis=0))
    low = low_lanes((rows, LANES))
    for t in range(inner // LANES):
        cut = slice(t * LANES, (t + 1) * LANES)
        total = jnp.zeros((rows, LANES), F32)
        for j in range(peers):
            at = j * HEADS + 2 * t
            weight = jnp.where(low, weights[:, at : at + 1], weights[:, at + 1 : at + 2])
            total = total + weight * parts[j][:, cut].astype(F32)
        attended[:, cut] = total
        att_low[:, cut] = total.astype(BF16)
    state = lat[...].astype(F32) + dot(att_low[...], w_out[...])
    hidden[...] = state
    hat, _ = stats(state)
    ff_low[...] = (hat * gain[2:3] + bias[2:3]).astype(BF16)


def feed_kernel(per_slot, halves, blocks, own, counts, *refs):
    count = halves * blocks
    ff_low, dy, hidden, attended, lse, w_out, gain = refs[:7]
    ups, downs = refs[7 : 7 + count], refs[7 + count : 7 + 2 * count]
    act, dpre, result, dhidden, dhid_low, datt_low, stat, sums, res, dff = refs[7 + 2 * count :]
    step = pl.program_id(0)

    @pl.when(step == 0)
    def _():
        res[...] = jnp.zeros_like(res)
        dff[...] = jnp.zeros_like(dff)

    for a in range(halves):
        up = jnp.concatenate([ref[...] for ref in ups[a * blocks : (a + 1) * blocks]], axis=1)
        down = jnp.concatenate([ref[...] for ref in downs[a * blocks : (a + 1) * blocks]], axis=0)
        value, slope = gelu_parts(dot(ff_low[...], up))
        value = value.astype(BF16)
        act[0, a] = value
        back = (slope * dot(dy[...], down, NT)).astype(BF16)
        dpre[0, a] = back
        res[...] += dot(value, down)
        dff[...] += dot(back, up, NT)

    @pl.when(step == pl.num_programs(0) - 1)
    def _():
        rows, inner = attended.shape
        live = live_rows(counts, rows, per_slot)
        state = hidden[...]
        result[...] = (live * (state + res[...])).astype(BF16)
        hat, inverse = stats(state)
        grad = dff[...]
        sums[0:1] = jnp.sum(grad * hat, axis=0, keepdims=True)
        sums[1:2] = jnp.sum(grad, axis=0, keepdims=True)
        back = dy[...].astype(F32) + pull(hat, inverse, grad, gain[2:3])
        dhidden[...] = back
        dhid_low[...] = back.astype(BF16)
        datt = dot(dhid_low[...], w_out[...], NT).astype(BF16)
        datt_low[...] = datt
        product = datt.astype(F32) * attended[...]
        low = low_lanes((rows, LANES))
        lane = lax.broadcasted_iota(jnp.int32, (rows, LANES), 1)
        delta = jnp.zeros((rows, LANES), F32)
        for t in range(inner // LANES):
            both = product[:, t * LANES : (t + 1) * LANES]
            first = jnp.sum(jnp.where(low, both, 0.0), axis=-1, keepdims=True)
            second = jnp.sum(jnp.where(low, 0.0, both), axis=-1, keepdims=True)
            delta = jnp.where(lane == 2 * t, first, delta)
            delta = jnp.where(lane == 2 * t + 1, second, delta)
        stat[:HEADS] = lse[...]
        stat[HEADS:] = flipped(delta)[:HEADS]


def attend_back_kernel(peers, scale, *refs):
    qs, das, sts = refs[:peers], refs[peers : 2 * peers], refs[2 * peers : 3 * peers]
    kv, dkv = refs[3 * peers], refs[3 * peers + 1]
    dqs, held = refs[3 * peers + 2 : 4 * peers + 2], refs[4 * peers + 2]
    n, per_slot, inner = qs[0].shape
    step = pl.program_id(0)

    @pl.when(step == 0)
    def _():
        for i in range(peers):
            rows = sts[i].shape[1]
            held[i, :rows, : 2 * HEADS] = flipped(sts[i][...])

    for s in range(n):
        row = pl.multiple_of((step * n + s) * per_slot, per_slot)
        st = jnp.concatenate([held[i, pl.ds(row, per_slot), :] for i in range(peers)], axis=0)
        for t in range(inner // LANES):
            cut = slice(t * LANES, (t + 1) * LANES)
            after = slice(inner + t * LANES, inner + (t + 1) * LANES)
            q = paired(jnp.concatenate([ref[s, :, cut] for ref in qs], axis=0))
            da = paired(jnp.concatenate([ref[s, :, cut] for ref in das], axis=0))
            k, v = kv[s, :, cut], kv[s, :, after]
            h = 2 * t
            lse = jnp.concatenate([st[:, h : h + 1], st[:, h + 1 : h + 2]], axis=0)
            h = HEADS + 2 * t
            delta = jnp.concatenate([st[:, h : h + 1], st[:, h + 1 : h + 2]], axis=0)
            probs = jnp.exp(dot(q, k, NT) * scale - lse)
            dprobs = dot(da, v, NT)
            dscores = (probs * (dprobs - delta)).astype(BF16)
            dq = (unpaired(dot(dscores, k)) * scale).astype(BF16)
            for i in range(peers):
                dqs[i][s, :, cut] = dq[i * per_slot : (i + 1) * per_slot]
            dkv[s, :, cut] = (dot(dscores, q, TN) * scale).astype(BF16)
            dkv[s, :, after] = dot(probs.astype(BF16), da, TN).astype(BF16)


def keyval_back_kernel(media, dkv, w_keyval, gain, media_grad, dlat, sums):
    n, rows, width = media.shape
    grad = dot(dkv[...].reshape(-1, dkv.shape[2]), w_keyval[...], NT).reshape(n, -1, width)
    dlat[...] = grad[:, rows:].reshape(dlat.shape)
    grad = grad[:, :rows].reshape(n * rows, width)
    hat, inverse = stats(media[...].reshape(n * rows, width).astype(F32))
    media_grad[...] = pull(hat, inverse, grad, gain[0:1]).astype(BF16).reshape(media_grad.shape)

    @pl.when(pl.program_id(0) == 0)
    def _():
        sums[...] = jnp.zeros_like(sums)

    sums[0:1] += jnp.sum(grad * hat, axis=0, keepdims=True)
    sums[1:2] += jnp.sum(grad, axis=0, keepdims=True)


def latent_back_kernel(peers, *refs):
    dqs = refs[:peers]
    dlat, lat, dhidden, w_query, gain, sums_media, sums_ff, dq_low, latent_grad, sums = refs[peers:]
    dq = sum(ref[...].astype(F32) for ref in dqs).astype(BF16)
    dq_low[...] = dq
    grad = dlat[...] + dot(dq, w_query[...], NT)
    hat, inverse = stats(lat[...].astype(F32))
    latent_grad[...] = (dhidden[...] + pull(hat, inverse, grad, gain[1:2])).astype(BF16)
    sums[0:1] = sums_media[0:1]
    sums[1:2] = jnp.sum(grad * hat, axis=0, keepdims=True)
    sums[2:3] = sums_ff[0:1]
    sums[3:4] = sums_media[1:2]
    sums[4:5] = jnp.sum(grad, axis=0, keepdims=True)
    sums[5:6] = sums_ff[1:2]


def outer_kernel(count, *refs):
    lefts, rights, result = refs[:count], refs[count : 2 * count], refs[2 * count]
    left = jnp.concatenate([ref[...] for ref in lefts], axis=0)
    right = jnp.concatenate([ref[...] for ref in rights], axis=0)
    result[...] = dot(left, right, TN).astype(BF16)


def outer(lefts, rights, tile, name):
    count = len(lefts)
    rows, a = lefts[0].shape
    b = rights[0].shape[1]
    return call(
        functools.partial(outer_kernel, count),
        (a // tile,),
        [pl.BlockSpec((rows, tile), lambda g: (0, g))] * count + [whole((rows, b))] * count,
        [(pl.BlockSpec((tile, b), lambda g: (g, 0)), out((a, b), BF16))],
        flops=2 * count * rows * a * b,
        moved=count * rows * (a + b) * 2 + a * b * 2,
        name=name,
    )(*lefts, *rights)[0]


def on_device(
    media, latents, counts, gains, biases, w_query, w_keyval, w_out, w_up, w_down, out_grad
):
    slots, patch_rows, width = media.shape
    per_slot = latents.shape[1]
    inner = w_query.shape[1]
    ff = w_up.shape[1]
    n_img, peers = lax.axis_size("img"), lax.axis_size("patch")
    shards = n_img * peers
    scale = 1.0 / math.sqrt(inner // HEADS)
    rows = slots * per_slot
    keys = patch_rows + per_slot
    padded = -(-rows // LANES) * LANES
    gain_spec = whole(gains.shape)
    lat = latents.reshape(rows, width)

    lat_low, q_low, dy = call(
        functools.partial(latent_kernel, per_slot),
        (1,),
        [SMEM, whole((rows, width)), whole((rows, width)), gain_spec, gain_spec, whole(w_query.shape)],
        [
            (whole((rows, width)), out((rows, width), BF16)),
            (whole((rows, inner)), out((rows, inner), BF16)),
            (whole((rows, width)), out((rows, width), BF16)),
        ],
        flops=2 * rows * width * inner, moved=2 * width * inner + 8 * rows * width, name="latent",
    )(counts, lat, out_grad.reshape(rows, width), gains, biases, w_query)
    qs = gather(q_low, "patch")
    qs = [q.reshape(slots, per_slot, inner) for q in qs]

    group = slots // 2
    key_input, keyval = call(
        media_kernel,
        (slots // group,),
        [
            leading((group, patch_rows, width)), leading((group * per_slot, width)),
            gain_spec, gain_spec, whole(w_keyval.shape),
        ],
        [
            (leading((group, keys, width)), out((slots, keys, width), BF16)),
            (leading((group, keys, 2 * inner)), out((slots, keys, 2 * inner), BF16)),
        ],
        flops=4 * slots * keys * width * inner, moved=8 * slots * keys * width, name="media",
    )(media, lat_low, gains, biases, w_keyval)

    pair = 2
    row_block = leading((pair, per_slot, inner))
    kv_block = leading((pair, keys, 2 * inner))
    row_out = (row_block, out((slots, per_slot, inner), BF16))
    stat_out = (whole((HEADS, rows)), out((HEADS, rows), F32))
    attention = 4 * slots * keys * peers * per_slot * inner
    got = call(
        functools.partial(attend_kernel, peers, scale),
        (slots // pair,),
        [row_block] * peers + [kv_block],
        [row_out] * peers + [stat_out] * peers,
        scratch=[pltpu.VMEM((peers, padded, LANES), F32)],
        flops=attention, moved=4 * slots * keys * inner + 4 * peers * rows * inner, name="attend",
    )(*qs, keyval)
    parts, lses = got[:peers], got[peers:]
    parts = [part.reshape(rows, inner) for part in parts]
    parts = [parts[0]] + [swap(parts[j], "patch", j) for j in range(1, peers)]
    lses = [lses[0]] + [swap(lses[j], "patch", j) for j in range(1, peers)]

    attended, att_low, hidden, ff_low, lse = call(
        functools.partial(mix_kernel, peers),
        (1,),
        [whole((rows, inner))] * peers + [whole((HEADS, rows))] * peers
        + [whole((rows, width)), whole(w_out.shape), gain_spec, gain_spec],
        [
            (whole((rows, inner)), out((rows, inner), F32)),
            (whole((rows, inner)), out((rows, inner), BF16)),
            (whole((rows, width)), out((rows, width), F32)),
            (whole((rows, width)), out((rows, width), BF16)),
            stat_out,
        ],
        flops=2 * rows * width * inner, moved=2 * width * inner + 8 * rows * width, name="mix",
    )(*parts, *lses, lat, w_out, gains, biases)

    halves = 2
    blocks = ff // (peers * halves * LANES)
    chunk = ff // shards
    strided = chunk % LANES == 0

    def column(own, j, a, k):
        p, y = own[0] ^ j, own[1] ^ a
        if strided:
            return (((k // (chunk // LANES)) * halves + y) * peers + p) * (chunk // LANES) + k % (chunk // LANES)
        return (p * halves + y) * blocks + k

    places = [(a, k) for a in range(halves) for k in range(blocks)]
    ups = [pl.BlockSpec((width, LANES), lambda j, own, a=a, k=k: (0, column(own, j, a, k))) for a, k in places]
    downs = [pl.BlockSpec((LANES, width), lambda j, own, a=a, k=k: (column(own, j, a, k), 0)) for a, k in places]
    own = jnp.stack([lax.axis_index("patch"), lax.axis_index("img") % halves]).astype(jnp.int32)
    part = ff // (peers * halves)
    tall = pl.BlockSpec((1, halves, rows, part), lambda j, *_: (j, 0, 0, 0))
    act, dpre, result, dhidden, dhid_low, datt_low, stat, sums_ff = call(
        functools.partial(feed_kernel, per_slot, halves, blocks),
        (peers,),
        [SMEM, whole((rows, width)), whole((rows, width)), whole((rows, width)), whole((rows, inner)),
         whole((HEADS, rows)), whole(w_out.shape), gain_spec] + ups + downs,
        [
            (tall, out((peers, halves, rows, part), BF16)),
            (tall, out((peers, halves, rows, part), BF16)),
            (whole((rows, width)), out((rows, width), BF16)),
            (whole((rows, width)), out((rows, width), F32)),
            (whole((rows, width)), out((rows, width), BF16)),
            (whole((rows, inner)), out((rows, inner), BF16)),
            (whole((2 * HEADS, rows)), out((2 * HEADS, rows), F32)),
            (whole((2, width)), out((2, width), F32)),
        ],
        scratch=[pltpu.VMEM((rows, width), F32), pltpu.VMEM((rows, width), F32)],
        vmem=48, flops=8 * rows * width * ff, moved=4 * width * ff, prefetch=1, name="feed",
    )(own, counts, ff_low, dy, hidden, attended, lse, w_out, gains, *([w_up] * len(ups)), *([w_down] * len(downs)))

    das = [a.reshape(slots, per_slot, inner) for a in gather(datt_low, "patch")]
    sts = gather(stat, "patch")
    got = call(
        functools.partial(attend_back_kernel, peers, scale),
        (slots // pair,),
        [row_block] * (2 * peers) + [whole((2 * HEADS, rows))] * peers + [kv_block],
        [(kv_block, out(keyval.shape, BF16))] + [row_out] * peers,
        scratch=[pltpu.VMEM((peers, padded, LANES), F32)],
        flops=2.5 * attention, moved=8 * slots * keys * inner + 8 * peers * rows * inner, name="attend_back",
    )(*qs, *das, *sts, keyval)
    dkv, dqs = got[0], [a.reshape(rows, inner) for a in got[1:]]
    dqs = [dqs[0]] + [swap(dqs[j], "patch", j) for j in range(1, peers)]

    media_grad, dlat, sums_media = call(
        keyval_back_kernel,
        (slots // group,),
        [
            leading((group, patch_rows, width)), leading((group, keys, 2 * inner)),
            whole(w_keyval.shape), gain_spec,
        ],
        [
            (leading((group, patch_rows, width)), out(media.shape, BF16)),
            (leading((group * per_slot, width)), out((rows, width), F32)),
            (whole((2, width)), out((2, width), F32)),
        ],
        flops=4 * slots * keys * width * inner, moved=8 * slots * keys * width, name="keyval_back",
    )(media, dkv, w_keyval, gains)

    dq_low, latent_grad, sums = call(
        functools.partial(latent_back_kernel, peers),
        (1,),
        [whole((rows, inner))] * peers
        + [whole((rows, width))] * 3 + [whole(w_query.shape), gain_spec, whole((2, width)), whole((2, width))],
        [
            (whole((rows, inner)), out((rows, inner), BF16)),
            (whole((rows, width)), out((rows, width), BF16)),
            (whole((6, width)), out((6, width), F32)),
        ],
        flops=2 * rows * width * inner, moved=2 * width * inner + 12 * rows * width, name="latent_back",
    )(*dqs, dlat, lat, dhidden, w_query, gains, sums_media, sums_ff)

    near = [swap_rows for swap_rows in gather(ff_low, "patch")]
    ff_rows = near + [swap(r, "img", 1) for r in near]
    near = [swap_rows for swap_rows in gather(dy, "patch")]
    dy_rows = near + [swap(r, "img", 1) for r in near]

    def exchanged(values):
        got = [values[0]] + [swap(values[j], "patch", j) for j in range(1, peers)]
        return [g[0] for g in got] + [swap(g[1], "img", 1) for g in got]

    rest = [("img", 1 << k) for k in range(1, log2(n_img))]
    rest_digits = [(name, 2) for name in reversed(rest)]
    down_part = outer(dy_rows, exchanged(act), width // 4, "down_grad")
    down_sum = scatter_sum([Piece(down_part, rest_digits)], rest)[0]
    up_part = outer(exchanged(dpre), ff_rows, part // 2, "up_grad")
    up_sum = scatter_sum([Piece(up_part, rest_digits)], rest)[0]
    if not strided:
        have = lambda i, p: (p * halves + i % 2) * (n_img // 2) + i // 2
        up_sum = lax.ppermute(
            up_sum, ("img", "patch"), [(i * peers + p, have(i, p)) for i in range(n_img) for p in range(peers)]
        )
    up_grad = up_sum.astype(F32).T

    piece = down_sum.reshape(2, peers, -1, part)
    odd = lax.axis_index("img") % 2 == 1
    sent = jnp.where(odd, piece[0], piece[1])
    kept = jnp.where(odd, piece[1], piece[0])
    other = swap(sent, "img", 1)
    both = jnp.stack([jnp.where(odd, other, kept), jnp.where(odd, kept, other)], axis=1)
    both = lax.all_to_all(both, "patch", 0, 0, tiled=True)
    if strided:
        both = both.reshape(peers, 2, -1, n_img // 2, chunk).transpose(3, 1, 0, 4, 2)
    else:
        both = both.transpose(0, 1, 3, 2)
    down_grad = both.reshape(ff, width // shards).astype(F32)

    every = digits_of("img") + digits_of("patch")
    kv_t = outer([dkv.reshape(-1, 2 * inner)], [key_input.reshape(-1, width)], 2 * inner // 4, "keyval_grad")
    q_t = outer([dq_low], [lat_low], inner // 2, "query_grad")
    out_t = outer([dhid_low], [att_low], width // 4, "out_grad")
    small = sums.reshape(6, shards, width // shards).transpose(1, 0, 2)
    order = [(("patch", 1 << k) if which else ("img", 1 << k)) for k in range(log2(max(n_img, peers)))
             for which in (1, 0) if (1 << k) < (peers if which else n_img)]
    kv_sum, q_sum, out_sum, small = scatter_sum([Piece(a, every) for a in (kv_t, q_t, out_t, small)], order)
    return (
        result.reshape(slots, per_slot, width),
        media_grad,
        latent_grad.reshape(slots, per_slot, width),
        q_sum.astype(F32).T,
        kv_sum.astype(F32).T,
        out_sum.astype(F32).T,
        up_grad,
        down_grad,
        small[:3],
        small[3:],
    )


def solution(mesh):
    rows = P("img", "patch", None)
    shard = P(None, ("img", "patch"))
    return jax.shard_map(
        on_device,
        mesh=mesh,
        in_specs=(rows, rows, P("img"), P(), P(), P(), P(), P(), P(), P(), rows),
        out_specs=(rows, rows, rows) + (shard,) * 7,
        check_vma=False,
    )
```

```python
import functools
import math

import jax
import jax.numpy as jnp
from jax import lax
from jax.experimental import pallas as pl
from jax.experimental.pallas import tpu as pltpu
from jax.sharding import PartitionSpec as P

HEADS = 8
SLOTS_PER = 5
EPS = 1e-05
LANES = 128
F32 = jnp.float32
BF16 = jnp.bfloat16
MIB = 1024 * 1024


def swap(values, axis, bit):
    n = lax.axis_size(axis)
    return lax.ppermute(values, axis, [(k, k ^ bit) for k in range(n)])


def log2(n):
    return n.bit_length() - 1


def after(values, *others):
    return lax.optimization_barrier((values,) + others)[0]


def spread(blocks):
    n = lax.axis_size("patch")
    blocks = dict(blocks)
    bit = n // 4
    while bit:
        for j in list(blocks):
            blocks[j ^ bit] = swap(blocks[j], "patch", bit)
        bit //= 2
    return [blocks[j] for j in range(n)]


def digits_of(axis):
    n = lax.axis_size(axis)
    return [(axis, 1 << k) for k in reversed(range(log2(n)))]


def chosen(own, bit):
    axis, weight = bit
    return (own[("patch", "img").index(axis)] // weight) % 2


def plan_of(rows, digits, order):
    digits, plan = list(digits), []
    for bit in order:
        at = digits.index(bit)
        plan.append(rows // 2 ** (at + 1))
        del digits[at]
        rows //= 2
    return plan


def parted(values, inner, which):
    width = values.shape[-1]
    split = values.reshape(-1, 2, inner, width)
    low, high = split[:, 0].reshape(-1, width), split[:, 1].reshape(-1, width)
    return jnp.where(which == 1, high, low), jnp.where(which == 1, low, high)


class Scatter:
    def __init__(self, own, both, order, plan, end, extra=None, name=None):
        self.own, self.both, self.order, self.plan, self.end = own, both, order, plan, end
        self.extra, self.name, self.at, self.open = extra, name, 0, False

    def begin(self, *others):
        kept, sent = self.both
        bit = self.order[self.at]
        sent = after(sent, *others)
        self.got = [swap(sent, *bit)]
        if self.extra is not None:
            self.got.append(swap(self.extra, *bit))
        self.at, self.open = self.at + 1, True

    def finish(self, *others):
        kept, self.open = self.both[0], False
        if others:
            kept = after(kept, *others)
        nxt = None
        if self.at < len(self.order):
            nxt = (self.order[self.at], self.plan[self.at])
        values = fold(self.own, kept, self.got, self.extra, nxt, self.end, self.name)
        if self.extra is not None:
            self.extra = values[-1]
            values = values[:-1]
        if nxt is not None:
            self.both = values
        else:
            self.values = values
        return values[0]

    def run(self):
        while self.open or self.at < len(self.order):
            if not self.open:
                self.begin()
            self.finish()
        return self.values


def stats(values):
    average = jnp.mean(values, axis=-1, keepdims=True)
    centred = values - average
    spread = jnp.mean(centred * centred, axis=-1, keepdims=True)
    inverse = lax.rsqrt(spread + EPS)
    return centred * inverse, inverse


def pull(hat, inverse, grad, gain):
    scaled = grad * gain
    first = jnp.mean(scaled, axis=-1, keepdims=True)
    second = jnp.mean(scaled * hat, axis=-1, keepdims=True)
    return inverse * (scaled - first - hat * second)


def gelu_parts(values):
    cdf = 0.5 + 0.5 * lax.erf(values * (1.0 / math.sqrt(2.0)))
    density = jnp.exp(-0.5 * values * values) * (1.0 / math.sqrt(2.0 * math.pi))
    return values * cdf, cdf + values * density


def dot(a, b, dims=((1,), (0,))):
    return lax.dot_general(a, b, (dims, ((), ())), preferred_element_type=F32)


NT = ((1,), (1,))
TN = ((0,), (0,))


def low_lanes(shape):
    return lax.broadcasted_iota(jnp.int32, shape, len(shape) - 1) < LANES // 2


def live_rows(counts_ref, rows, per_slot):
    row = lax.broadcasted_iota(jnp.int32, (rows, 1), 0)
    live = jnp.zeros((rows, 1), F32)
    for sample in range(rows // (per_slot * SLOTS_PER)):
        start = sample * SLOTS_PER * per_slot
        inside = jnp.logical_and(row >= start, row < start + counts_ref[sample] * per_slot)
        live = jnp.where(inside, 1.0, live)
    return live


def paired(block):
    low = low_lanes(block.shape)
    zero = jnp.zeros_like(block)
    return jnp.concatenate([jnp.where(low, block, zero), jnp.where(low, zero, block)], axis=0)


def unpaired(block):
    half = block.shape[0] // 2
    return jnp.where(low_lanes((half, block.shape[1])), block[:half], block[half:])


def flipped(values):
    a, b = values.shape
    tall, wide = -a % LANES, -b % LANES
    if wide:
        values = jnp.concatenate([values, jnp.zeros((a, wide), F32)], axis=1)
    if tall:
        values = jnp.concatenate([values, jnp.zeros((tall, b + wide), F32)], axis=0)
    return values.T[:b, :a]


def call(kernel, grid, ins, outs, scratch=(), vmem=40, us=2, prefetch=0, name=None):
    return pl.pallas_call(
        kernel,
        grid_spec=pltpu.PrefetchScalarGridSpec(
            num_scalar_prefetch=prefetch,
            grid=grid,
            in_specs=ins,
            out_specs=[spec for spec, _ in outs],
            scratch_shapes=list(scratch),
        ),
        out_shape=[shape for _, shape in outs],
        compiler_params=pltpu.CompilerParams(
            vmem_limit_bytes=vmem * MIB, dimension_semantics=("arbitrary",) * len(grid)
        ),
        cost_estimate=pl.CostEstimate(flops=0, bytes_accessed=int(us * 1e5), transcendentals=0),
        name=name,
    )


def whole(shape):
    zeros = (0,) * len(shape)
    return pl.BlockSpec(tuple(shape), lambda *_: zeros)


def leading(shape):
    zeros = (0,) * (len(shape) - 1)
    return pl.BlockSpec(tuple(shape), lambda g, *_: (g,) + zeros)


def out(shape, dtype):
    return jax.ShapeDtypeStruct(tuple(shape), dtype)


SMEM = pl.BlockSpec(memory_space=pltpu.SMEM)


def packed(values):
    high = values.astype(BF16)
    left = values - high.astype(F32)
    middle = left.astype(BF16)
    small = left - middle.astype(F32)
    top = jnp.concatenate([high.astype(F32), middle.astype(F32)], axis=1)
    bottom = jnp.concatenate([small, jnp.zeros_like(small)], axis=1)
    return jnp.concatenate([top, bottom], axis=0).astype(BF16)


def unpacked(values):
    values = values.astype(F32)
    n, m = values.shape[0] // 2, values.shape[1] // 2
    return values[:n, :m] + values[:n, m:] + values[n:, :m]


def latent_kernel(per_slot, counts, lat, grad, gain, bias, w_query, lat_low, q_low, dy):
    hat, _ = stats(lat[...].astype(F32))
    low = (hat * gain[1:2] + bias[1:2]).astype(BF16)
    lat_low[...] = low
    q_low[...] = dot(low, w_query[...]).astype(BF16)
    live = live_rows(counts, lat.shape[0], per_slot)
    dy[...] = (live * grad[...].astype(F32)).astype(BF16)


def media_kernel(media, lat_low, gain, bias, w_keyval, key_input, keyval):
    n, rows, width = media.shape
    hat, _ = stats(media[...].reshape(n * rows, width).astype(F32))
    low = (hat * gain[0:1] + bias[0:1]).astype(BF16)
    key_input[:, :rows, :] = low.reshape(n, rows, width)
    key_input[:, rows:, :] = lat_low[...].reshape(n, -1, width)
    every = key_input[...].reshape(-1, width)
    keyval[...] = dot(every, w_keyval[...]).astype(BF16).reshape(keyval.shape)


def attend_kernel(peers, per_slot, scale, *refs):
    qs, kv, parts, held = refs[:peers], refs[peers], refs[peers + 1 : 2 * peers + 1], refs[2 * peers + 1]
    n, keys, inner = kv.shape[0], kv.shape[1], kv.shape[2] // 2
    step = pl.program_id(0)
    items = [(s, t) for s in range(n) for t in range(inner // LANES)]
    cuts = [slice(t * LANES, (t + 1) * LANES) for t in range(2 * inner // LANES)]
    rows = [pl.multiple_of((step * n + s) * per_slot, per_slot) for s in range(n)]
    ones = jnp.ones((keys, LANES), BF16)

    @pl.when(step == 0)
    def _():
        held[...] = jnp.zeros_like(held)

    scores = []
    for s, t in items:
        q = paired(jnp.concatenate([ref[pl.ds(rows[s], per_slot), cuts[t]] for ref in qs], axis=0))
        scores.append(dot(q, kv[s, :, cuts[t]], NT) * scale)
    tops = [jnp.max(score, axis=-1, keepdims=True) for score in scores]
    probs = [jnp.exp(score - top).astype(BF16) for score, top in zip(scores, tops)]
    sums = [
        dot(prob, jnp.concatenate([kv[s, :, cuts[inner // LANES + t]], ones], axis=1))
        for prob, (s, t) in zip(probs, items)
    ]
    lane = lax.broadcasted_iota(jnp.int32, (peers * per_slot, LANES), 1)
    logs = [jnp.zeros((peers * per_slot, LANES), F32) for _ in range(n)]
    for (s, t), both, top in zip(items, sums, tops):
        total = unpaired(both[:, LANES:])
        o = (unpaired(both[:, :LANES]) / total).astype(BF16)
        lse = unpaired(jnp.broadcast_to(top, (top.shape[0], LANES))) + jnp.log(total)
        here = jnp.logical_or(lane == t, lane == LANES // 2 + HEADS // 2 + t)
        logs[s] = jnp.where(here, lse, logs[s])
        for i in range(peers):
            parts[i][pl.ds(rows[s], per_slot), cuts[t]] = o[i * per_slot : (i + 1) * per_slot]
    for s in range(n):
        for i in range(peers):
            held[i, pl.ds(rows[s], per_slot), :] = logs[s][i * per_slot : (i + 1) * per_slot]

    @pl.when(step == pl.num_programs(0) - 1)
    def _():
        for i in range(peers):
            turned = held[i].T
            turned = turned[:HEADS] + turned[LANES // 2 : LANES // 2 + HEADS]
            parts[i][-2 * HEADS :, :] = packed(turned)


def mix_kernel(peers, *refs):
    parts = refs[:peers]
    lat, w_out, gain, bias, attended, att_low, hidden, ff_low, lse_out = refs[peers:]
    rows, inner = attended.shape
    logs = [unpacked(ref[rows:, :]) for ref in parts]
    top = functools.reduce(jnp.maximum, logs)
    lse = top + jnp.log(sum(jnp.exp(v - top) for v in logs))
    lse_out[...] = lse
    weights = flipped(jnp.concatenate([jnp.exp(v - lse) for v in logs], axis=0))[:rows]
    low = low_lanes((rows, LANES))
    for t in range(inner // LANES):
        cut = slice(t * LANES, (t + 1) * LANES)
        total = jnp.zeros((rows, LANES), F32)
        for j in range(peers):
            at = j * HEADS + t
            other = at + HEADS // 2
            weight = jnp.where(low, weights[:, at : at + 1], weights[:, other : other + 1])
            total = total + weight * parts[j][:rows, cut].astype(F32)
        attended[:, cut] = total
        att_low[:, cut] = total.astype(BF16)
    state = lat[...].astype(F32) + dot(att_low[...], w_out[...])
    hidden[...] = state
    hat, _ = stats(state)
    ff_low[...] = (hat * gain[2:3] + bias[2:3]).astype(BF16)


def feed_columns(ff_low, dy, ups, downs, acts, dpres, res, dff):
    half = len(ups) // 2
    a = pl.program_id(1)
    parts = []
    for at in (slice(0, half), slice(half, 2 * half)):
        up = jnp.concatenate([ref[...] for ref in ups[at]], axis=1)
        down = jnp.concatenate([ref[...] for ref in downs[at]], axis=0)
        parts.append((up, down, dot(ff_low[...], up), dot(dy[...], down, NT)))
    done = []
    for up, down, pre, dact in parts:
        value, slope = gelu_parts(pre)
        value = value.astype(BF16)
        back = (slope * dact).astype(BF16)
        res[...] += dot(value, down)
        dff[...] += dot(back, up, NT)
        done.append((value, back))
    for at, (act, dpre) in enumerate(zip(acts, dpres)):

        @pl.when(pl.program_id(0) == at)
        def _():
            width = done[0][0].shape[1]
            for k, (value, back) in enumerate(done):
                act[a, :, k * width : (k + 1) * width] = value
                dpre[a, :, k * width : (k + 1) * width] = back


def first_step():
    return jnp.logical_and(pl.program_id(0) == 0, pl.program_id(1) == 0)


def last_step():
    ends = [pl.program_id(k) == pl.num_programs(k) - 1 for k in range(2)]
    return jnp.logical_and(*ends)


def feed_kernel(count, here, own, ff_low, dy, *refs):
    ups, downs, refs = refs[:count], refs[count : 2 * count], refs[2 * count :]
    acts, dpres, (res, dff) = refs[:here], refs[here : 2 * here], refs[2 * here :]

    @pl.when(first_step())
    def _():
        res[...] = jnp.zeros_like(res)
        dff[...] = jnp.zeros_like(dff)

    feed_columns(ff_low, dy, ups, downs, acts, dpres, res, dff)


def feed_end_kernel(per_slot, count, here, own, counts, ff_low, dy, *refs):
    ups, downs, refs = refs[:count], refs[count : 2 * count], refs[2 * count :]
    res_in, dff_in, hidden, attended, lse, w_out, gain = refs[:7]
    acts, dpres, refs = refs[7 : 7 + here], refs[7 + here : 7 + 2 * here], refs[7 + 2 * here :]
    result, dhidden, dhid_low, datt_low, sums, res, dff = refs

    @pl.when(first_step())
    def _():
        res[...] = res_in[...]
        dff[...] = dff_in[...]

    feed_columns(ff_low, dy, ups, downs, acts, dpres, res, dff)

    @pl.when(last_step())
    def _():
        rows, inner = attended.shape
        live = live_rows(counts, rows, per_slot)
        state = hidden[...]
        result[...] = (live * (state + res[...])).astype(BF16)
        hat, inverse = stats(state)
        grad = dff[...]
        sums[0:1] = jnp.sum(grad * hat, axis=0, keepdims=True)
        sums[1:2] = jnp.sum(grad, axis=0, keepdims=True)
        back = dy[...].astype(F32) + pull(hat, inverse, grad, gain[2:3])
        dhidden[...] = back
        dhid_low[...] = back.astype(BF16)
        datt = dot(dhid_low[...], w_out[...], NT).astype(BF16)
        datt_low[:rows, :] = datt
        product = datt.astype(F32) * attended[...]
        low = low_lanes((rows, LANES))
        lane = lax.broadcasted_iota(jnp.int32, (rows, LANES), 1)
        delta = jnp.zeros((rows, LANES), F32)
        for t in range(inner // LANES):
            both = product[:, t * LANES : (t + 1) * LANES]
            first = jnp.sum(jnp.where(low, both, 0.0), axis=-1, keepdims=True)
            second = jnp.sum(jnp.where(low, 0.0, both), axis=-1, keepdims=True)
            delta = jnp.where(lane == t, first, delta)
            delta = jnp.where(lane == HEADS // 2 + t, second, delta)
        turned = flipped(jnp.concatenate([delta, jnp.zeros((-rows % LANES, LANES), F32)], axis=0))
        datt_low[rows:, :] = packed(jnp.concatenate([lse[...], turned[:HEADS]], axis=0))


def attend_back_kernel(peers, per_slot, scale, *refs):
    qs, das, kv, dkv = refs[:peers], refs[peers : 2 * peers], refs[2 * peers], refs[2 * peers + 1]
    dqs, held = refs[2 * peers + 2 : 3 * peers + 2], refs[3 * peers + 2]
    n, inner = kv.shape[0], kv.shape[2] // 2
    step = pl.program_id(0)
    items = [(s, t) for s in range(n) for t in range(inner // LANES)]
    cuts = [slice(t * LANES, (t + 1) * LANES) for t in range(2 * inner // LANES)]
    rows = [pl.multiple_of((step * n + s) * per_slot, per_slot) for s in range(n)]
    later = inner // LANES

    @pl.when(step == 0)
    def _():
        for i in range(peers):
            turned = unpacked(das[i][-4 * HEADS :, :])
            held[i, :, : 2 * HEADS] = flipped(turned)

    def column(block, h):
        other = h + HEADS // 2
        return jnp.concatenate([block[:, h : h + 1], block[:, other : other + 1]], axis=0)

    sts = [
        jnp.concatenate([held[i, pl.ds(row, per_slot), :] for i in range(peers)], axis=0) for row in rows
    ]
    qp = [paired(jnp.concatenate([ref[pl.ds(rows[s], per_slot), cuts[t]] for ref in qs], axis=0)) for s, t in items]
    dp = [paired(jnp.concatenate([ref[pl.ds(rows[s], per_slot), cuts[t]] for ref in das], axis=0)) for s, t in items]
    scores = [dot(q, kv[s, :, cuts[t]], NT) for q, (s, t) in zip(qp, items)]
    dprobs = [dot(d, kv[s, :, cuts[later + t]], NT) for d, (s, t) in zip(dp, items)]
    probs = [jnp.exp(score * scale - column(sts[s], t)) for score, (s, t) in zip(scores, items)]
    dscores = [
        (prob * (dprob - column(sts[s], HEADS + t))).astype(BF16)
        for prob, dprob, (s, t) in zip(probs, dprobs, items)
    ]
    for (s, t), prob, d in zip(items, probs, dp):
        dkv[s, :, cuts[later + t]] = dot(prob.astype(BF16), d, TN).astype(BF16)
    for (s, t), ds, q in zip(items, dscores, qp):
        dkv[s, :, cuts[t]] = (dot(ds, q, TN) * scale).astype(BF16)
    for (s, t), ds in zip(items, dscores):
        dq = (unpaired(dot(ds, kv[s, :, cuts[t]])) * scale).astype(BF16)
        for i in range(peers):
            dqs[i][pl.ds(rows[s], per_slot), cuts[t]] = dq[i * per_slot : (i + 1) * per_slot]


def keyval_back_kernel(media, dkv, w_keyval, gain, media_grad, dlat, sums):
    n, rows, width = media.shape
    grad = dot(dkv[...].reshape(-1, dkv.shape[2]), w_keyval[...], NT).reshape(n, -1, width)
    dlat[...] = grad[:, rows:].reshape(dlat.shape)
    grad = grad[:, :rows].reshape(n * rows, width)
    hat, inverse = stats(media[...].reshape(n * rows, width).astype(F32))
    media_grad[...] = pull(hat, inverse, grad, gain[0:1]).astype(BF16).reshape(media_grad.shape)

    @pl.when(pl.program_id(0) == 0)
    def _():
        sums[...] = jnp.zeros_like(sums)

    sums[0:1] += jnp.sum(grad * hat, axis=0, keepdims=True)
    sums[1:2] += jnp.sum(grad, axis=0, keepdims=True)


def latent_back_kernel(peers, *refs):
    dqs = refs[:peers]
    dlat, lat, dhidden, w_query, gain, sums_media, sums_ff, dq_low, latent_grad, sums = refs[peers:]
    dq = sum(ref[...].astype(F32) for ref in dqs).astype(BF16)
    dq_low[...] = dq
    grad = dlat[...] + dot(dq, w_query[...], NT)
    hat, inverse = stats(lat[...].astype(F32))
    latent_grad[...] = (dhidden[...] + pull(hat, inverse, grad, gain[1:2])).astype(BF16)
    sums[0:1] = sums_media[0:1]
    sums[1:2] = jnp.sum(grad * hat, axis=0, keepdims=True)
    sums[2:3] = sums_ff[0:1]
    sums[3:4] = sums_media[1:2]
    sums[4:5] = jnp.sum(grad, axis=0, keepdims=True)
    sums[5:6] = sums_ff[1:2]


def stack_kernel(*refs):
    for k, ref in enumerate(refs[:-1]):
        refs[-1][k] = ref[...].reshape(refs[-1].shape[1:])


def stacked(blocks, second=False):
    inner = blocks[0].shape[-2:]
    specs = [
        pl.BlockSpec((1,) + inner, lambda *_: (1, 0, 0)) if second and b.ndim == 3 else whole(b.shape) for b in blocks
    ]
    shape = (len(blocks),) + inner
    return call(stack_kernel, (1,), specs, [(whole(shape), out(shape, BF16))], vmem=62, name="stack")(*blocks)[0]


def outer_kernel(count, bit, inner, extra, own, *refs):
    lefts, rights, refs = refs[:count], refs[count : 2 * count], refs[2 * count :]
    more, results, held = refs[:extra], refs[extra:-1], refs[-1]
    width = held.shape[1]

    @pl.when(pl.program_id(0) == 0)
    def _():
        at = 0
        for ref in rights:
            block = ref[...].reshape(-1, width)
            held[at : at + block.shape[0], :] = block
            at += block.shape[0]

    left = jnp.concatenate([ref[...].reshape(-1, ref.shape[-1]) for ref in lefts], axis=0)
    product = dot(left, held[...], TN)
    if bit is None:
        results[0][...] = product.astype(BF16)
        return
    kept, sent = parted(product, inner, chosen(own, bit))
    if extra:
        rows = more[0].shape[1]
        other = more[0][...].astype(F32).reshape(-1, more[0].shape[2])
        kept_more, sent_more = parted(other, rows, chosen(own, bit))
        join = lambda a, b: jnp.concatenate(
            [a.reshape(-1, inner, width), b.reshape(-1, rows, width)], axis=1
        ).reshape(-1, width)
        kept, sent = join(kept, kept_more), join(sent, sent_more)
    results[0][...] = kept.astype(BF16)
    results[1][...] = sent.astype(BF16)


def outer(own, lefts, rights, tile, name, bit=None, inner=0, more=None):
    count = len(lefts)
    a, b = lefts[0].shape[-1], rights[0].shape[-1]

    def block(values, width, moving):
        lead = values.shape[:-1]
        if len(lead) == 2 and lead[0] == 2:
            lead = (1,) + lead[1:]
        zeros = (0,) * len(lead)
        return pl.BlockSpec(lead + (width,), lambda g, *_: zeros + (g if moving else 0,))

    total = sum(math.prod(block(v, b, False).block_shape[:-1]) for v in rights)
    steps = a // tile
    rows, outs = a, 1
    if bit is not None:
        rows, outs = a // 2, 2
    extra = []
    if more is not None:
        extra = [pl.BlockSpec((more.shape[0] // steps,) + more.shape[1:], lambda g, *_: (g, 0, 0))]
        rows += more.shape[0] * more.shape[1] // 2
    got = call(
        functools.partial(outer_kernel, count, bit, inner, len(extra)),
        (steps,),
        [block(v, tile, True) for v in lefts] + [block(v, b, False) for v in rights] + extra,
        [(pl.BlockSpec((rows // steps, b), lambda g, *_: (g, 0)), out((rows, b), BF16))] * outs,
        scratch=[pltpu.VMEM((total, b), BF16)],
        prefetch=1,
        name=name,
    )(own, *lefts, *rights, *([more] if more is not None else []))
    return got if bit is not None else got[0]


def side_by_side_kernel(rows, left, right, result):
    product = dot(left[...], right[...], TN).astype(BF16)
    split = product.reshape(-1, 2, rows, product.shape[1])
    result[...] = jnp.concatenate([split[:, 0], split[:, 1]], axis=-1)


def fold_kernel(nxt, end, extra, own, kept, got, *refs):
    total = kept[...].astype(F32) + got[...].astype(F32)
    if extra:
        refs[-1][...] = refs[0][...] + refs[1][...]
        refs = refs[2:-1]
    if nxt is not None:
        bit, inner = nxt
        keep, send = parted(total, inner, chosen(own, bit))
        refs[0][...] = keep.astype(BF16)
        refs[1][...] = send.astype(BF16)
        return
    for ref, values in zip(refs, end(total)):
        ref[...] = values.astype(ref.dtype)


def fold(own, kept, got, extra, nxt, end, name):
    rows, width = kept.shape
    ins = [kept, got[0]]
    if nxt is not None:
        shapes = [out((rows // 2, width), BF16)] * 2
    else:
        shapes = jax.eval_shape(end, out(kept.shape, F32))
        shapes = [out(s.shape, F32 if s.dtype == F32 else BF16) for s in shapes]
    if extra is not None:
        ins += [extra, got[1]]
        shapes = shapes + [out(extra.shape, F32)]
    return call(
        functools.partial(fold_kernel, nxt, end, extra is not None),
        (1,),
        [whole(v.shape) for v in ins],
        [(whole(s.shape), s) for s in shapes],
        prefetch=1,
        name=name,
    )(own, *ins)


def on_device(
    media, latents, counts, gains, biases, w_query, w_keyval, w_out, w_up, w_down, out_grad
):
    slots, patch_rows, width = media.shape
    per_slot = latents.shape[1]
    inner = w_query.shape[1]
    ff = w_up.shape[1]
    n_img, peers = lax.axis_size("img"), lax.axis_size("patch")
    shards = n_img * peers
    scale = 1.0 / math.sqrt(inner // HEADS)
    rows = slots * per_slot
    keys = patch_rows + per_slot
    padded = -(-rows // LANES) * LANES
    gain_spec = whole(gains.shape)
    lat = latents.reshape(rows, width)

    own = jnp.stack([lax.axis_index("patch"), lax.axis_index("img")]).astype(jnp.int32)
    fine = width // shards % 16 == 0 and inner // shards % 16 == 0
    lat_low, q_low, dy = call(
        functools.partial(latent_kernel, per_slot),
        (1,),
        [SMEM, whole((rows, width)), whole((rows, width)), gain_spec, gain_spec, whole(w_query.shape)],
        [
            (whole((rows, width)), out((rows, width), BF16)),
            (whole((rows, inner)), out((rows, inner), BF16)),
            (whole((rows, width)), out((rows, width), BF16)),
        ],
        vmem=62, name="latent",
    )(counts, lat, out_grad.reshape(rows, width), gains, biases, w_query)
    q_near = q_low
    qs = {0: q_low}
    bit = peers // 2
    qs[bit] = swap(q_low, "patch", bit)
    dys = {0: dy}

    group = slots // 2
    key_input, keyval = call(
        media_kernel,
        (slots // group,),
        [
            leading((group, patch_rows, width)), leading((group * per_slot, width)),
            gain_spec, gain_spec, whole(w_keyval.shape),
        ],
        [
            (leading((group, keys, width)), out((slots, keys, width), BF16)),
            (leading((group, keys, 2 * inner)), out((slots, keys, 2 * inner), BF16)),
        ],
        name="media",
    )(media, lat_low, gains, biases, w_keyval)
    first = after(qs[bit], keyval)
    qs[bit] = first
    while bit > 1:
        bit //= 2
        for j in list(qs):
            qs[j ^ bit] = swap(qs[j], "patch", bit)
    qs = [qs[j] for j in range(peers)]

    pair = 2
    kv_block = leading((pair, keys, 2 * inner))
    part_rows = rows + 2 * HEADS
    stat_out = (whole((HEADS, padded)), out((HEADS, padded), F32))
    parts = call(
        functools.partial(attend_kernel, peers, per_slot, scale),
        (slots // pair,),
        [whole((rows, inner))] * peers + [kv_block],
        [(whole((part_rows, inner)), out((part_rows, inner), BF16))] * peers,
        scratch=[pltpu.VMEM((peers, padded, LANES), F32)],
        name="attend",
    )(*qs, keyval)
    parts = [parts[0]] + [swap(parts[j], "patch", j) for j in range(1, peers)]

    attended, att_low, hidden, ff_low, lse = call(
        functools.partial(mix_kernel, peers),
        (1,),
        [whole((part_rows, inner))] * peers
        + [whole((rows, width)), whole(w_out.shape), gain_spec, gain_spec],
        [
            (whole((rows, inner)), out((rows, inner), F32)),
            (whole((rows, inner)), out((rows, inner), BF16)),
            (whole((rows, width)), out((rows, width), F32)),
            (whole((rows, width)), out((rows, width), BF16)),
            stat_out,
        ],
        vmem=62, name="mix",
    )(*parts, lat, w_out, gains, biases)
    bit = peers // 2
    ffs = {0: ff_low, bit: swap(ff_low, "patch", bit)}
    dys[bit] = swap(after(dy, ff_low), "patch", bit)

    halves = 2
    blocks = ff // (peers * halves * LANES)
    chunk = ff // shards
    strided = chunk % LANES == 0

    def column(own, j, a, k):
        p, y = own[0] ^ j, (own[1] % halves) ^ a
        if strided:
            return (((k // (chunk // LANES)) * halves + y) * peers + p) * (chunk // LANES) + k % (chunk // LANES)
        return (p * halves + y) * blocks + k

    def weights(first, stride):
        ups = [
            pl.BlockSpec((width, LANES), lambda g, a, own, k=k: (0, column(own, first + stride * g, a, k)))
            for k in range(blocks)
        ]
        downs = [
            pl.BlockSpec((LANES, width), lambda g, a, own, k=k: (column(own, first + stride * g, a, k), 0))
            for k in range(blocks)
        ]
        return ups + downs

    part = ff // (peers * halves)
    here = peers // 2
    columns = (whole((halves, rows, part)), out((halves, rows, part), BF16))
    wide_low = (whole((rows, width)), out((rows, width), BF16))
    wide = (whole((rows, width)), out((rows, width), F32))
    count = blocks
    far = call(
        functools.partial(feed_kernel, count, here),
        (here, halves),
        [whole((rows, width))] * 2 + weights(here, 1),
        [columns] * (2 * here) + [wide, wide],
        vmem=62, prefetch=1, name="feed",
    )(own, ff_low, dy, *([w_up] * count), *([w_down] * count))
    ffs[peers // 2] = after(ffs[peers // 2], far[-1])
    ffs = spread(ffs)
    ff_all = stacked(ffs)
    ff_far = swap(ff_all, "img", 1)
    dys[peers // 2] = after(dys[peers // 2], far[-1])
    dys = spread(dys)
    dy_all = stacked(dys)
    dy_far = swap(dy_all, "img", 1)

    def cross(values, *others):
        values = after(tuple(values), *others)
        return [swap(v, "patch", here + k) for k, v in enumerate(values)]

    act_cross = cross(far[:1])
    near = call(
        functools.partial(feed_end_kernel, per_slot, count, here),
        (here, halves),
        [SMEM] + [whole((rows, width))] * 2 + weights(here - 1, -1)
        + [whole((rows, width))] * 3 + [whole((rows, inner)), whole((HEADS, padded)), whole(w_out.shape), gain_spec],
        [columns] * (2 * here)
        + [wide_low, wide, wide_low]
        + [(whole((rows + 4 * HEADS, inner)), out((rows + 4 * HEADS, inner), BF16)), (whole((2, width)), out((2, width), F32))],
        scratch=[pltpu.VMEM((rows, width), F32), pltpu.VMEM((rows, width), F32)],
        vmem=62, prefetch=1, name="feed_end",
    )(own, counts, after(ff_low, ff_all, dy_all), dy, *([w_up] * count), *([w_down] * count),
      far[2 * here], far[2 * here + 1], hidden, attended, lse, w_out, gains)
    result, dhidden, dhid_low, datt_low, sums_ff = near[2 * here :]
    act_near, dpre_near = list(reversed(near[:here])), list(reversed(near[here : 2 * here]))

    datt_low = after(datt_low, act_cross[0])
    das = {0: datt_low, peers // 2: swap(datt_low, "patch", peers // 2)}
    out_rows = width // shards // 2
    out_t = call(
        functools.partial(side_by_side_kernel, out_rows),
        (2,),
        [pl.BlockSpec((rows, width // 2), lambda g: (0, g)), whole((rows, inner))],
        [(leading((shards // 2, out_rows, 2 * inner)), out((shards, out_rows, 2 * inner), BF16))],
        name="out_grad",
    )(after(dhid_low, datt_low), att_low)[0]
    das[peers // 2] = after(das[peers // 2], out_t)
    acts = act_near + act_cross
    acts = [acts[0]] + [swap(acts[j], "patch", j) for j in range(1, here)] + list(acts[here:])
    acts += [swap(after(far[k], das[peers // 2]), "patch", here + k) for k in range(1, here)]
    das = spread(das)

    got = call(
        functools.partial(attend_back_kernel, peers, per_slot, scale),
        (slots // pair,),
        [whole((rows, inner))] * peers + [whole((rows + 4 * HEADS, inner))] * peers + [kv_block],
        [(kv_block, out(keyval.shape, BF16))] + [(whole((rows, inner)), out((rows, inner), BF16))] * peers,
        scratch=[pltpu.VMEM((peers, padded, LANES), F32)],
        name="attend_back",
    )(*qs, *das[:-1], after(das[-1], ff_far), keyval)
    dkv, dqs = got[0], got[1:]
    dkv = after(dkv, dy_far, *acts)
    act_all = stacked(acts, True)
    act_far = swap(act_all, "img", 1)
    dpres = dpre_near + [swap(after(far[here + k], dkv), "patch", here + k) for k in range(here)]
    dpres = [dpres[0]] + [swap(dpres[j], "patch", j) for j in range(1, here)] + dpres[here:]

    every = digits_of("img") + digits_of("patch")
    low_bit, both = [("patch", 1)], [("patch", 2), ("img", 1)]
    last = [bit for bit in reversed(every) if bit not in low_bit + both]
    kv_order, qo_order = low_bit + both + last, low_bit + both[::-1] + last
    kv_plan = plan_of(2 * inner, every, kv_order)
    q_plan, qo_plan = plan_of(inner, every, qo_order), plan_of(2 * inner, every, qo_order)
    kv_sum = Scatter(
        own,
        outer(
            own, [after(dkv, act_all).reshape(-1, 2 * inner)], [key_input.reshape(-1, width)], 2 * inner // 4,
            "keyval_grad", kv_order[0], kv_plan[0],
        ),
        kv_order, kv_plan, lambda t: [flipped(t)], name="keyval_fold",
    )
    kv_sum.begin()

    media_grad, dlat, sums_media = call(
        keyval_back_kernel,
        (slots // group,),
        [
            leading((group, patch_rows, width)), leading((group, keys, 2 * inner)),
            whole(w_keyval.shape), gain_spec,
        ],
        [
            (leading((group, patch_rows, width)), out(media.shape, BF16)),
            (leading((group * per_slot, width)), out((rows, width), F32)),
            (whole((2, width)), out((2, width), F32)),
        ],
        name="keyval_back",
    )(media, after(dkv, *kv_sum.both), w_keyval, gains)
    dpres = list(after(tuple(dpres), kv_sum.finish(media_grad)))
    dqs = [dqs[0]] + [swap(v, "patch", j + 1) for j, v in enumerate(after(tuple(dqs[1:]), *dpres))]
    dpre_all = stacked(after(tuple(dpres), act_far), True)
    dpre_far = swap(dpre_all, "img", 1)

    rest = [("img", 1 << k) for k in range(1, log2(n_img))]
    rest_digits = rest[::-1]
    down_order, down_plan = rest + [("img", 1)], plan_of(width, rest_digits + [("img", 1)], rest + [("img", 1)])
    down_sum = Scatter(
        own,
        outer(own, dys + [dy_far], acts + [after(act_far, dpre_all)], width // 2, "down_grad", down_order[0], down_plan[0]),
        down_order, down_plan, None, name="down_fold",
    )
    down_sum.begin()
    dqs = [dqs[0]] + list(after(tuple(dqs[1:]), *down_sum.both))
    kv_sum.begin(*dqs)

    dq_low, latent_grad, sums = call(
        functools.partial(latent_back_kernel, peers),
        (1,),
        [whole((rows, inner))] * peers
        + [whole((rows, width))] * 3 + [whole(w_query.shape), gain_spec, whole((2, width)), whole((2, width))],
        [
            (whole((rows, inner)), out((rows, inner), BF16)),
            (whole((rows, width)), out((rows, width), BF16)),
            (whole((HEADS, width)), out((HEADS, width), F32)),
        ],
        name="latent_back",
    )(*dqs, dlat, lat, dhidden, w_query, gains, sums_media, sums_ff)

    q_rows = inner // shards

    def open_rows(total):
        other = total[q_rows:]
        other = jnp.concatenate([other[:, :inner], other[:, inner:]], axis=0)
        return [flipped(total[:q_rows]), flipped(other)]

    qo_sum = Scatter(
        own,
        outer(own, [dq_low], [lat_low], inner // 2, "query_grad", qo_order[0], q_plan[0], more=out_t),
        qo_order, qo_plan, open_rows, extra=sums, name="query_fold",
    )
    qo_sum.begin()
    mark = qo_sum.finish()
    qo_sum.begin(dpre_far)
    up_plan = plan_of(part, rest_digits, rest)
    up_sum = Scatter(
        own,
        outer(own, dpres + [after(dpre_far, mark)], ffs + [ff_far], part // 2, "up_grad", rest[0], up_plan[0]),
        rest, up_plan, lambda t: [flipped(t)] if strided else [t.astype(BF16)], name="up_fold",
    )
    up_sum.begin()
    mark = up_sum.both[0]
    for one in (down_sum, kv_sum, kv_sum, qo_sum, down_sum, up_sum, kv_sum, qo_sum):
        mark = one.finish(mark)
        one.begin()
    (kv_sum,) = kv_sum.run()
    (up_sum,) = up_sum.run()
    q_sum, out_sum = qo_sum.run()
    small = lax.dynamic_slice_in_dim(
        qo_sum.extra, (own[1] * peers + own[0]) * (width // shards), width // shards, axis=1
    )
    if not strided:
        have = lambda i, p: (p * halves + i % 2) * (n_img // 2) + i // 2
        up_sum = lax.ppermute(
            up_sum, ("img", "patch"), [(i * peers + p, have(i, p)) for i in range(n_img) for p in range(peers)]
        )
        up_sum = up_sum.astype(F32).T
    up_grad = up_sum

    while down_sum.at < len(down_sum.order):
        down_sum.finish()
        down_sum.begin()

    kept, other = down_sum.both[0], down_sum.got[0]
    kept, other = (v.reshape(peers, -1, part) for v in (kept, other))
    odd = own[1] % 2 == 1
    both = jnp.stack([jnp.where(odd, other, kept), jnp.where(odd, kept, other)], axis=1)
    both = lax.all_to_all(both, "patch", 0, 0, tiled=True)
    if strided:
        both = both.reshape(peers, 2, -1, n_img // 2, chunk).transpose(3, 1, 0, 4, 2)
    else:
        both = both.transpose(0, 1, 3, 2)
    down_grad = both.reshape(ff, width // shards).astype(F32)

    return (
        result.reshape(slots, per_slot, width),
        media_grad,
        latent_grad.reshape(slots, per_slot, width),
        q_sum,
        kv_sum,
        out_sum,
        up_grad,
        down_grad,
        small[:3],
        small[3:6],
    )


def solution(mesh):
    rows = P("img", "patch", None)
    shard = P(None, ("img", "patch"))
    return jax.shard_map(
        on_device,
        mesh=mesh,
        in_specs=(rows, rows, P("img"), P(), P(), P(), P(), P(), P(), P(), rows),
        out_specs=(rows, rows, rows) + (shard,) * 7,
        check_vma=False,
    )
```

```python
import functools
import math

import jax
import jax.numpy as jnp
from jax import lax
from jax.experimental import pallas as pl
from jax.experimental.pallas import tpu as pltpu
from jax.sharding import PartitionSpec as P

HEADS = 8
SLOTS_PER = 5
EPS = 1e-05
LANES = 128
F32 = jnp.float32
BF16 = jnp.bfloat16
MIB = 1024 * 1024


def swap(values, axis, bit):
    n = lax.axis_size(axis)
    return lax.ppermute(values, axis, [(k, k ^ bit) for k in range(n)])


def log2(n):
    return n.bit_length() - 1


def after(values, *others):
    return lax.optimization_barrier((values,) + others)[0]


def spread(blocks):
    n = lax.axis_size("patch")
    blocks = dict(blocks)
    bit = n // 4
    while bit:
        for j in list(blocks):
            blocks[j ^ bit] = swap(blocks[j], "patch", bit)
        bit //= 2
    return [blocks[j] for j in range(n)]


def digits_of(axis):
    n = lax.axis_size(axis)
    return [(axis, 1 << k) for k in reversed(range(log2(n)))]


def chosen(own, bit):
    axis, weight = bit
    return (own[("patch", "img").index(axis)] // weight) % 2


def plan_of(rows, digits, order):
    digits, plan = list(digits), []
    for bit in order:
        at = digits.index(bit)
        plan.append(rows // 2 ** (at + 1))
        del digits[at]
        rows //= 2
    return plan


def parted(values, inner, which):
    width = values.shape[-1]
    split = values.reshape(-1, 2, inner, width)
    low, high = split[:, 0].reshape(-1, width), split[:, 1].reshape(-1, width)
    return jnp.where(which == 1, high, low), jnp.where(which == 1, low, high)


class Scatter:
    def __init__(self, own, both, lanes, end, extra=None, name=None):
        self.own, self.both, self.lanes, self.end = own, both, lanes, end
        self.extra, self.name, self.at, self.open = extra, name, 0, False
        self.steps = len(lanes[0][0])

    def begin(self, *others):
        sent = after(tuple(self.both[1::2]), *others)
        self.got = [swap(v, *order[self.at]) for v, (order, _) in zip(sent, self.lanes)]
        self.at, self.open = self.at + 1, True

    def finish(self, *others):
        kept, self.open = tuple(self.both[::2]), False
        if others:
            kept = after(kept, *others)
        nxt = None
        if self.at < self.steps:
            nxt = [(order[self.at], plan[self.at]) for order, plan in self.lanes]
        values = fold(self.own, kept, self.got, self.extra, nxt, self.end, self.name)
        if self.extra is not None:
            self.extra = values[-1]
            values = values[:-1]
        if nxt is not None:
            self.both = values
        else:
            self.values = values
        return values[0]

    def run(self):
        while self.open or self.at < self.steps:
            if not self.open:
                self.begin()
            self.finish()
        return self.values


def stats(values):
    average = jnp.mean(values, axis=-1, keepdims=True)
    centred = values - average
    spread = jnp.mean(centred * centred, axis=-1, keepdims=True)
    inverse = lax.rsqrt(spread + EPS)
    return centred * inverse, inverse


def pull(hat, inverse, grad, gain):
    scaled = grad * gain
    first = jnp.mean(scaled, axis=-1, keepdims=True)
    second = jnp.mean(scaled * hat, axis=-1, keepdims=True)
    return inverse * (scaled - first - hat * second)


def gelu_parts(values):
    cdf = 0.5 + 0.5 * lax.erf(values * (1.0 / math.sqrt(2.0)))
    density = jnp.exp(-0.5 * values * values) * (1.0 / math.sqrt(2.0 * math.pi))
    return values * cdf, cdf + values * density


def dot(a, b, dims=((1,), (0,))):
    return lax.dot_general(a, b, (dims, ((), ())), preferred_element_type=F32)


NT = ((1,), (1,))
TN = ((0,), (0,))


def low_lanes(shape):
    return lax.broadcasted_iota(jnp.int32, shape, len(shape) - 1) < LANES // 2


def live_rows(counts_ref, rows, per_slot):
    row = lax.broadcasted_iota(jnp.int32, (rows, 1), 0)
    live = jnp.zeros((rows, 1), F32)
    for sample in range(rows // (per_slot * SLOTS_PER)):
        start = sample * SLOTS_PER * per_slot
        inside = jnp.logical_and(row >= start, row < start + counts_ref[sample] * per_slot)
        live = jnp.where(inside, 1.0, live)
    return live


def paired(block):
    low = low_lanes(block.shape)
    zero = jnp.zeros_like(block)
    return jnp.concatenate([jnp.where(low, block, zero), jnp.where(low, zero, block)], axis=0)


def unpaired(block):
    half = block.shape[0] // 2
    return jnp.where(low_lanes((half, block.shape[1])), block[:half], block[half:])


def flipped(values):
    a, b = values.shape
    tall, wide = -a % LANES, -b % LANES
    if wide:
        values = jnp.concatenate([values, jnp.zeros((a, wide), F32)], axis=1)
    if tall:
        values = jnp.concatenate([values, jnp.zeros((tall, b + wide), F32)], axis=0)
    return values.T[:b, :a]


def call(kernel, grid, ins, outs, scratch=(), vmem=40, us=2, prefetch=0, name=None):
    return pl.pallas_call(
        kernel,
        grid_spec=pltpu.PrefetchScalarGridSpec(
            num_scalar_prefetch=prefetch,
            grid=grid,
            in_specs=ins,
            out_specs=[spec for spec, _ in outs],
            scratch_shapes=list(scratch),
        ),
        out_shape=[shape for _, shape in outs],
        compiler_params=pltpu.CompilerParams(
            vmem_limit_bytes=vmem * MIB, dimension_semantics=("arbitrary",) * len(grid)
        ),
        cost_estimate=pl.CostEstimate(flops=0, bytes_accessed=int(us * 1e5), transcendentals=0),
        name=name,
    )


def whole(shape):
    zeros = (0,) * len(shape)
    return pl.BlockSpec(tuple(shape), lambda *_: zeros)


def leading(shape):
    zeros = (0,) * (len(shape) - 1)
    return pl.BlockSpec(tuple(shape), lambda g, *_: (g,) + zeros)


def out(shape, dtype):
    return jax.ShapeDtypeStruct(tuple(shape), dtype)


SMEM = pl.BlockSpec(memory_space=pltpu.SMEM)


def packed(values):
    high = values.astype(BF16)
    left = values - high.astype(F32)
    middle = left.astype(BF16)
    small = left - middle.astype(F32)
    top = jnp.concatenate([high.astype(F32), middle.astype(F32)], axis=1)
    bottom = jnp.concatenate([small, jnp.zeros_like(small)], axis=1)
    return jnp.concatenate([top, bottom], axis=0).astype(BF16)


def unpacked(values):
    values = values.astype(F32)
    n, m = values.shape[0] // 2, values.shape[1] // 2
    return values[:n, :m] + values[:n, m:] + values[n:, :m]


def latent_kernel(per_slot, counts, lat, grad, gain, bias, w_query, lat_low, q_low, dy):
    hat, _ = stats(lat[...].astype(F32))
    low = (hat * gain[1:2] + bias[1:2]).astype(BF16)
    lat_low[...] = low
    q_low[...] = dot(low, w_query[...]).astype(BF16)
    live = live_rows(counts, lat.shape[0], per_slot)
    dy[...] = (live * grad[...].astype(F32)).astype(BF16)


def media_kernel(media, lat_low, gain, bias, w_keyval, key_input, keyval):
    n, rows, width = media.shape
    hat, _ = stats(media[...].reshape(n * rows, width).astype(F32))
    low = (hat * gain[0:1] + bias[0:1]).astype(BF16)
    key_input[:, :rows, :] = low.reshape(n, rows, width)
    key_input[:, rows:, :] = lat_low[...].reshape(n, -1, width)
    every = key_input[...].reshape(-1, width)
    keyval[...] = dot(every, w_keyval[...]).astype(BF16).reshape(keyval.shape)


def attend_kernel(peers, per_slot, scale, *refs):
    qs, kv, parts, held = refs[:peers], refs[peers], refs[peers + 1 : 2 * peers + 1], refs[2 * peers + 1]
    n, keys, inner = kv.shape[0], kv.shape[1], kv.shape[2] // 2
    step = pl.program_id(0)
    items = [(s, t) for s in range(n) for t in range(inner // LANES)]
    cuts = [slice(t * LANES, (t + 1) * LANES) for t in range(2 * inner // LANES)]
    rows = [pl.multiple_of((step * n + s) * per_slot, per_slot) for s in range(n)]
    ones = jnp.ones((keys, LANES), BF16)

    @pl.when(step == 0)
    def _():
        held[...] = jnp.zeros_like(held)

    scores = []
    for s, t in items:
        q = paired(jnp.concatenate([ref[pl.ds(rows[s], per_slot), cuts[t]] for ref in qs], axis=0))
        scores.append(dot(q, kv[s, :, cuts[t]], NT) * scale)
    tops = [jnp.max(score, axis=-1, keepdims=True) for score in scores]
    probs = [jnp.exp(score - top).astype(BF16) for score, top in zip(scores, tops)]
    sums = [
        dot(prob, jnp.concatenate([kv[s, :, cuts[inner // LANES + t]], ones], axis=1))
        for prob, (s, t) in zip(probs, items)
    ]
    lane = lax.broadcasted_iota(jnp.int32, (peers * per_slot, LANES), 1)
    logs = [jnp.zeros((peers * per_slot, LANES), F32) for _ in range(n)]
    for (s, t), both, top in zip(items, sums, tops):
        total = unpaired(both[:, LANES:])
        o = (unpaired(both[:, :LANES]) / total).astype(BF16)
        lse = unpaired(jnp.broadcast_to(top, (top.shape[0], LANES))) + jnp.log(total)
        here = jnp.logical_or(lane == t, lane == LANES // 2 + HEADS // 2 + t)
        logs[s] = jnp.where(here, lse, logs[s])
        for i in range(peers):
            parts[i][pl.ds(rows[s], per_slot), cuts[t]] = o[i * per_slot : (i + 1) * per_slot]
    for s in range(n):
        for i in range(peers):
            held[i, pl.ds(rows[s], per_slot), :] = logs[s][i * per_slot : (i + 1) * per_slot]

    @pl.when(step == pl.num_programs(0) - 1)
    def _():
        for i in range(peers):
            turned = held[i].T
            turned = turned[:HEADS] + turned[LANES // 2 : LANES // 2 + HEADS]
            parts[i][-2 * HEADS :, :] = packed(turned)


def mix_kernel(peers, *refs):
    parts = refs[:peers]
    lat, w_out, gain, bias, attended, att_low, hidden, ff_low, lse_out = refs[peers:]
    rows, inner = attended.shape
    logs = [unpacked(ref[rows:, :]) for ref in parts]
    top = functools.reduce(jnp.maximum, logs)
    lse = top + jnp.log(sum(jnp.exp(v - top) for v in logs))
    lse_out[...] = lse
    weights = flipped(jnp.concatenate([jnp.exp(v - lse) for v in logs], axis=0))[:rows]
    low = low_lanes((rows, LANES))
    for t in range(inner // LANES):
        cut = slice(t * LANES, (t + 1) * LANES)
        total = jnp.zeros((rows, LANES), F32)
        for j in range(peers):
            at = j * HEADS + t
            other = at + HEADS // 2
            weight = jnp.where(low, weights[:, at : at + 1], weights[:, other : other + 1])
            total = total + weight * parts[j][:rows, cut].astype(F32)
        attended[:, cut] = total
        att_low[:, cut] = total.astype(BF16)
    state = lat[...].astype(F32) + dot(att_low[...], w_out[...])
    hidden[...] = state
    hat, _ = stats(state)
    ff_low[...] = (hat * gain[2:3] + bias[2:3]).astype(BF16)


def feed_columns(ff_low, dy, ups, downs, acts, dpres, res, dff):
    half = len(ups) // 2
    a = pl.program_id(1)
    parts = []
    for at in (slice(0, half), slice(half, 2 * half)):
        up = jnp.concatenate([ref[...] for ref in ups[at]], axis=1)
        down = jnp.concatenate([ref[...] for ref in downs[at]], axis=0)
        parts.append((up, down, dot(ff_low[...], up), dot(dy[...], down, NT)))
    done = []
    for up, down, pre, dact in parts:
        value, slope = gelu_parts(pre)
        value = value.astype(BF16)
        back = (slope * dact).astype(BF16)
        res[...] += dot(value, down)
        dff[...] += dot(back, up, NT)
        done.append((value, back))
    for at, (act, dpre) in enumerate(zip(acts, dpres)):

        @pl.when(pl.program_id(0) == at)
        def _():
            width = done[0][0].shape[1]
            for k, (value, back) in enumerate(done):
                act[a, :, k * width : (k + 1) * width] = value
                dpre[a, :, k * width : (k + 1) * width] = back


def first_step():
    return jnp.logical_and(pl.program_id(0) == 0, pl.program_id(1) == 0)


def last_step():
    ends = [pl.program_id(k) == pl.num_programs(k) - 1 for k in range(2)]
    return jnp.logical_and(*ends)


def feed_kernel(count, here, own, ff_low, dy, *refs):
    ups, downs, refs = refs[:count], refs[count : 2 * count], refs[2 * count :]
    acts, dpres, (res, dff) = refs[:here], refs[here : 2 * here], refs[2 * here :]

    @pl.when(first_step())
    def _():
        res[...] = jnp.zeros_like(res)
        dff[...] = jnp.zeros_like(dff)

    feed_columns(ff_low, dy, ups, downs, acts, dpres, res, dff)


def feed_end_kernel(per_slot, count, here, own, counts, ff_low, dy, *refs):
    ups, downs, refs = refs[:count], refs[count : 2 * count], refs[2 * count :]
    res_in, dff_in, hidden, attended, lse, w_out, gain = refs[:7]
    acts, dpres, refs = refs[7 : 7 + here], refs[7 + here : 7 + 2 * here], refs[7 + 2 * here :]
    result, dhidden, dhid_low, datt_low, sums, res, dff = refs

    @pl.when(first_step())
    def _():
        res[...] = res_in[...]
        dff[...] = dff_in[...]

    feed_columns(ff_low, dy, ups, downs, acts, dpres, res, dff)

    @pl.when(last_step())
    def _():
        rows, inner = attended.shape
        live = live_rows(counts, rows, per_slot)
        state = hidden[...]
        result[...] = (live * (state + res[...])).astype(BF16)
        hat, inverse = stats(state)
        grad = dff[...]
        sums[0:1] = jnp.sum(grad * hat, axis=0, keepdims=True)
        sums[1:2] = jnp.sum(grad, axis=0, keepdims=True)
        back = dy[...].astype(F32) + pull(hat, inverse, grad, gain[2:3])
        dhidden[...] = back
        dhid_low[...] = back.astype(BF16)
        datt = dot(dhid_low[...], w_out[...], NT).astype(BF16)
        datt_low[:rows, :] = datt
        product = datt.astype(F32) * attended[...]
        low = low_lanes((rows, LANES))
        lane = lax.broadcasted_iota(jnp.int32, (rows, LANES), 1)
        delta = jnp.zeros((rows, LANES), F32)
        for t in range(inner // LANES):
            both = product[:, t * LANES : (t + 1) * LANES]
            first = jnp.sum(jnp.where(low, both, 0.0), axis=-1, keepdims=True)
            second = jnp.sum(jnp.where(low, 0.0, both), axis=-1, keepdims=True)
            delta = jnp.where(lane == t, first, delta)
            delta = jnp.where(lane == HEADS // 2 + t, second, delta)
        turned = flipped(jnp.concatenate([delta, jnp.zeros((-rows % LANES, LANES), F32)], axis=0))
        datt_low[rows:, :] = packed(jnp.concatenate([lse[...], turned[:HEADS]], axis=0))


def attend_back_kernel(peers, per_slot, scale, *refs):
    qs, das, kv, dkv = refs[:peers], refs[peers : 2 * peers], refs[2 * peers], refs[2 * peers + 1]
    dqs, held = refs[2 * peers + 2 : 3 * peers + 2], refs[3 * peers + 2]
    n, inner = kv.shape[0], kv.shape[2] // 2
    step = pl.program_id(0)
    items = [(s, t) for s in range(n) for t in range(inner // LANES)]
    cuts = [slice(t * LANES, (t + 1) * LANES) for t in range(2 * inner // LANES)]
    rows = [pl.multiple_of((step * n + s) * per_slot, per_slot) for s in range(n)]
    later = inner // LANES

    @pl.when(step == 0)
    def _():
        for i in range(peers):
            turned = unpacked(das[i][-4 * HEADS :, :])
            held[i, :, : 2 * HEADS] = flipped(turned)

    def column(block, h):
        other = h + HEADS // 2
        return jnp.concatenate([block[:, h : h + 1], block[:, other : other + 1]], axis=0)

    sts = [
        jnp.concatenate([held[i, pl.ds(row, per_slot), :] for i in range(peers)], axis=0) for row in rows
    ]
    qp = [paired(jnp.concatenate([ref[pl.ds(rows[s], per_slot), cuts[t]] for ref in qs], axis=0)) for s, t in items]
    dp = [paired(jnp.concatenate([ref[pl.ds(rows[s], per_slot), cuts[t]] for ref in das], axis=0)) for s, t in items]
    scores = [dot(q, kv[s, :, cuts[t]], NT) for q, (s, t) in zip(qp, items)]
    dprobs = [dot(d, kv[s, :, cuts[later + t]], NT) for d, (s, t) in zip(dp, items)]
    probs = [jnp.exp(score * scale - column(sts[s], t)) for score, (s, t) in zip(scores, items)]
    dscores = [
        (prob * (dprob - column(sts[s], HEADS + t))).astype(BF16)
        for prob, dprob, (s, t) in zip(probs, dprobs, items)
    ]
    for (s, t), prob, d in zip(items, probs, dp):
        dkv[s, :, cuts[later + t]] = dot(prob.astype(BF16), d, TN).astype(BF16)
    for (s, t), ds, q in zip(items, dscores, qp):
        dkv[s, :, cuts[t]] = (dot(ds, q, TN) * scale).astype(BF16)
    for (s, t), ds in zip(items, dscores):
        dq = (unpaired(dot(ds, kv[s, :, cuts[t]])) * scale).astype(BF16)
        for i in range(peers):
            dqs[i][pl.ds(rows[s], per_slot), cuts[t]] = dq[i * per_slot : (i + 1) * per_slot]


def keyval_back_kernel(media, dkv, w_keyval, gain, media_grad, dlat, sums):
    n, rows, width = media.shape
    grad = dot(dkv[...].reshape(-1, dkv.shape[2]), w_keyval[...], NT).reshape(n, -1, width)
    dlat[...] = grad[:, rows:].reshape(dlat.shape)
    grad = grad[:, :rows].reshape(n * rows, width)
    hat, inverse = stats(media[...].reshape(n * rows, width).astype(F32))
    media_grad[...] = pull(hat, inverse, grad, gain[0:1]).astype(BF16).reshape(media_grad.shape)

    @pl.when(pl.program_id(0) == 0)
    def _():
        sums[...] = jnp.zeros_like(sums)

    sums[0:1] += jnp.sum(grad * hat, axis=0, keepdims=True)
    sums[1:2] += jnp.sum(grad, axis=0, keepdims=True)


def latent_back_kernel(peers, *refs):
    dqs = refs[:peers]
    dlat, lat, dhidden, w_query, gain, sums_media, sums_ff, dq_low, latent_grad, sums = refs[peers:]
    dq = sum(ref[...].astype(F32) for ref in dqs).astype(BF16)
    dq_low[...] = dq
    grad = dlat[...] + dot(dq, w_query[...], NT)
    hat, inverse = stats(lat[...].astype(F32))
    latent_grad[...] = (dhidden[...] + pull(hat, inverse, grad, gain[1:2])).astype(BF16)
    sums[0:1] = sums_media[0:1]
    sums[1:2] = jnp.sum(grad * hat, axis=0, keepdims=True)
    sums[2:3] = sums_ff[0:1]
    sums[3:4] = sums_media[1:2]
    sums[4:5] = jnp.sum(grad, axis=0, keepdims=True)
    sums[5:6] = sums_ff[1:2]


def halved(values):
    high = values.astype(BF16).astype(F32)
    return jnp.concatenate([high, values - high], axis=0).astype(BF16)


def joined(values):
    values = values.astype(F32)
    half = values.shape[0] // 2
    return values[:half] + values[half:]


def outer_kernel(count, lanes, own, *refs):
    lefts, rights, refs = refs[:count], refs[count : 2 * count], refs[2 * count :]
    results, held = refs[:-1], refs[-1]

    @pl.when(pl.program_id(0) == 0)
    def _():
        at = 0
        for ref in rights:
            rows, width = ref.shape[-2:]
            for k in range(held.shape[1] // width):
                held[at : at + rows, k * width : (k + 1) * width] = ref[k] if len(ref.shape) == 3 else ref[...]
            at += rows

    left = jnp.concatenate([ref[...].reshape(-1, ref.shape[-1]) for ref in lefts], axis=0)
    product = dot(left, held[...], TN)
    width = product.shape[1] // len(lanes)
    for k, (bit, inner) in enumerate(lanes):
        kept, sent = parted(product[:, k * width : (k + 1) * width], inner, chosen(own, bit))
        results[2 * k][...] = kept.astype(BF16)
        results[2 * k + 1][...] = sent.astype(BF16)


def outer(own, lefts, rights, tile, lanes, name):
    count = len(lefts)
    wide = lambda v: v.shape[-1] * (v.shape[0] if v.ndim == 3 else 1)
    a, b = wide(lefts[0]), wide(rights[0])

    def left_spec(v):
        if v.ndim == 3:
            return pl.BlockSpec((1, v.shape[1], tile), lambda g, *_: (g, 0, 0))
        return pl.BlockSpec((v.shape[0], tile), lambda g, *_: (0, g))

    total = sum(v.shape[-2] for v in rights)
    steps, part = a // tile, b // len(lanes)
    spec = pl.BlockSpec((tile // 2, part), lambda g, *_: (g, 0))
    return call(
        functools.partial(outer_kernel, count, [(order[0], plan[0]) for order, plan in lanes]),
        (steps,),
        [left_spec(v) for v in lefts] + [whole(v.shape) for v in rights],
        [(spec, out((a // 2, part), BF16))] * (2 * len(lanes)),
        scratch=[pltpu.VMEM((total, b), BF16)],
        us=4, prefetch=1, name=name,
    )(own, *lefts, *rights)


def query_kernel(bit, rows, own, dq, lat_low, out_t, sums, kept, sent):
    width = lat_low.shape[1]
    which = chosen(own, bit)
    other_rows = out_t.shape[1]
    product = dot(dq[...], lat_low[...], TN)
    first = parted(product, rows, which)
    second = parted(out_t[...].astype(F32).reshape(-1, width), other_rows, which)
    both = [
        jnp.concatenate([a.reshape(-1, rows, width), b.reshape(-1, other_rows, width)], axis=1).reshape(-1, width)
        for a, b in zip(first, second)
    ]
    head = 2 * sums.shape[0]
    kept[...] = both[0].astype(BF16)
    sent[:head, :] = halved(sums[...])
    sent[head:, :] = both[1].astype(BF16)


def side_by_side_kernel(rows, left, right, result):
    product = dot(left[...], right[...], TN).astype(BF16)
    split = product.reshape(-1, 2, rows, product.shape[1])
    result[...] = jnp.concatenate([split[:, 0], split[:, 1]], axis=-1)


def fold_kernel(nxt, end, lanes, extra, own, *refs):
    kept, got, refs = refs[:lanes], refs[lanes : 2 * lanes], refs[2 * lanes :]
    head = 0
    if extra:
        more, refs = refs[0], refs[1:]
        head = 2 * more.shape[0]
        small = more[...] + joined(got[0][:head, :])
        refs[-1][...] = small
    totals = [a[...].astype(F32) + b[head:, :].astype(F32) for a, b in zip(kept, got)]
    if nxt is None:
        for ref, values in zip(refs, end(*totals)):
            ref[...] = values.astype(ref.dtype)
        return
    for k, (total, (bit, inner)) in enumerate(zip(totals, nxt)):
        keep, send = parted(total, inner, chosen(own, bit))
        refs[2 * k][...] = keep.astype(BF16)
        refs[2 * k + 1][head:, :] = send.astype(BF16)
    if extra:
        refs[1][:head, :] = halved(small)


def fold(own, kept, got, extra, nxt, end, name):
    ins = list(kept) + list(got)
    if nxt is not None:
        head = 0 if extra is None else 2 * extra.shape[0]
        shapes = []
        for v in kept:
            rows, width = v.shape
            shapes += [out((rows // 2, width), BF16), out((head + rows // 2, width), BF16)]
    else:
        shapes = list(jax.eval_shape(end, *(out(v.shape, F32) for v in kept)))
    if extra is not None:
        ins.append(extra)
        shapes.append(out(extra.shape, F32))
    return call(
        functools.partial(fold_kernel, nxt, end, len(kept), extra is not None),
        (1,),
        [whole(v.shape) for v in ins],
        [(whole(s.shape), s) for s in shapes],
        us=1, prefetch=1, name=name,
    )(own, *ins)


def place_kernel(block, parts, result):
    peers, _, width = parts.shape
    for p in range(peers):
        for k in range(width // block):
            at = (k * peers + p) * block
            result[:, at : at + block] = parts[p, :, k * block : (k + 1) * block].astype(F32)


def on_device(
    media, latents, counts, gains, biases, w_query, w_keyval, w_out, w_up, w_down, out_grad
):
    slots, patch_rows, width = media.shape
    per_slot = latents.shape[1]
    inner = w_query.shape[1]
    ff = w_up.shape[1]
    n_img, peers = lax.axis_size("img"), lax.axis_size("patch")
    shards = n_img * peers
    scale = 1.0 / math.sqrt(inner // HEADS)
    rows = slots * per_slot
    keys = patch_rows + per_slot
    padded = -(-rows // LANES) * LANES
    gain_spec = whole(gains.shape)
    lat = latents.reshape(rows, width)

    own = jnp.stack([lax.axis_index("patch"), lax.axis_index("img")]).astype(jnp.int32)
    fine = width // shards % 16 == 0 and inner // shards % 16 == 0
    lat_low, q_low, dy = call(
        functools.partial(latent_kernel, per_slot),
        (1,),
        [SMEM, whole((rows, width)), whole((rows, width)), gain_spec, gain_spec, whole(w_query.shape)],
        [
            (whole((rows, width)), out((rows, width), BF16)),
            (whole((rows, inner)), out((rows, inner), BF16)),
            (whole((rows, width)), out((rows, width), BF16)),
        ],
        vmem=62, name="latent",
    )(counts, lat, out_grad.reshape(rows, width), gains, biases, w_query)
    qs = {0: q_low}
    bit = peers // 2
    qs[bit] = swap(q_low, "patch", bit)
    dys = {0: dy, bit: swap(dy, "patch", bit)}

    group = slots // 2
    key_input, keyval = call(
        media_kernel,
        (slots // group,),
        [
            leading((group, patch_rows, width)), leading((group * per_slot, width)),
            gain_spec, gain_spec, whole(w_keyval.shape),
        ],
        [
            (leading((group, keys, width)), out((slots, keys, width), BF16)),
            (leading((group, keys, 2 * inner)), out((slots, keys, 2 * inner), BF16)),
        ],
        name="media",
    )(media, lat_low, gains, biases, w_keyval)
    first = after(qs[bit], keyval)
    qs[bit] = first
    while bit > 1:
        bit //= 2
        for j in list(qs):
            qs[j ^ bit] = swap(qs[j], "patch", bit)
    qs = [after(qs[0], dys[peers // 2])] + [qs[j] for j in range(1, peers)]

    pair = 2
    kv_block = leading((pair, keys, 2 * inner))
    part_rows = rows + 2 * HEADS
    stat_out = (whole((HEADS, padded)), out((HEADS, padded), F32))
    parts = call(
        functools.partial(attend_kernel, peers, per_slot, scale),
        (slots // pair,),
        [whole((rows, inner))] * peers + [kv_block],
        [(whole((part_rows, inner)), out((part_rows, inner), BF16))] * peers,
        scratch=[pltpu.VMEM((peers, padded, LANES), F32)],
        name="attend",
    )(*qs, keyval)
    parts = [parts[0]] + [swap(parts[j], "patch", j) for j in range(1, peers)]

    attended, att_low, hidden, ff_low, lse = call(
        functools.partial(mix_kernel, peers),
        (1,),
        [whole((part_rows, inner))] * peers
        + [whole((rows, width)), whole(w_out.shape), gain_spec, gain_spec],
        [
            (whole((rows, inner)), out((rows, inner), F32)),
            (whole((rows, inner)), out((rows, inner), BF16)),
            (whole((rows, width)), out((rows, width), F32)),
            (whole((rows, width)), out((rows, width), BF16)),
            stat_out,
        ],
        vmem=62, name="mix",
    )(*parts, lat, w_out, gains, biases)
    bit = peers // 2
    ffs = {0: ff_low, bit: swap(ff_low, "patch", bit)}
    dys = spread({0: after(dy, ff_low), bit: after(dys[bit], ff_low)})

    halves = 2
    blocks = ff // (peers * halves * LANES)
    chunk = ff // shards
    strided = chunk % LANES == 0

    def column(own, j, a, k):
        p, k = own[0] ^ j, a * blocks + k
        if strided:
            return ((k // (chunk // LANES)) * peers + p) * (chunk // LANES) + k % (chunk // LANES)
        return p * halves * blocks + k

    def weights(first, stride):
        ups = [
            pl.BlockSpec((width, LANES), lambda g, a, own, k=k: (0, column(own, first + stride * g, a, k)))
            for k in range(blocks)
        ]
        downs = [
            pl.BlockSpec((LANES, width), lambda g, a, own, k=k: (column(own, first + stride * g, a, k), 0))
            for k in range(blocks)
        ]
        return ups + downs

    part = ff // (peers * halves)
    here = peers // 2
    columns = (whole((halves, rows, part)), out((halves, rows, part), BF16))
    wide_low = (whole((rows, width)), out((rows, width), BF16))
    wide = (whole((rows, width)), out((rows, width), F32))
    count = blocks
    far = call(
        functools.partial(feed_kernel, count, here),
        (here, halves),
        [whole((rows, width))] * 2 + weights(here, 1),
        [columns] * (2 * here) + [wide, wide],
        vmem=62, prefetch=1, name="feed",
    )(own, ff_low, dy, *([w_up] * count), *([w_down] * count))
    ffs[peers // 2] = after(ffs[peers // 2], far[-1])
    ffs = spread(ffs)

    def cross(values):
        return [swap(v, "patch", here + k) for k, v in enumerate(values)]

    act_cross = cross(after(tuple(far[:here]), ffs[peers // 2]))
    near = call(
        functools.partial(feed_end_kernel, per_slot, count, here),
        (here, halves),
        [SMEM] + [whole((rows, width))] * 2 + weights(here - 1, -1)
        + [whole((rows, width))] * 3 + [whole((rows, inner)), whole((HEADS, padded)), whole(w_out.shape), gain_spec],
        [columns] * (2 * here)
        + [wide_low, wide, wide_low]
        + [(whole((rows + 4 * HEADS, inner)), out((rows + 4 * HEADS, inner), BF16)), (whole((2, width)), out((2, width), F32))],
        scratch=[pltpu.VMEM((rows, width), F32), pltpu.VMEM((rows, width), F32)],
        vmem=62, prefetch=1, name="feed_end",
    )(own, counts, after(ff_low, *ffs[1:], *dys[1:]), dy, *([w_up] * count), *([w_down] * count),
      far[2 * here], far[2 * here + 1], hidden, attended, lse, w_out, gains)
    result, dhidden, dhid_low, datt_low, sums_ff = near[2 * here :]
    act_near, dpre_near = list(reversed(near[:here])), list(reversed(near[here : 2 * here]))

    das = {0: datt_low, peers // 2: swap(datt_low, "patch", peers // 2)}
    out_rows = width // shards // 2
    out_t = call(
        functools.partial(side_by_side_kernel, out_rows),
        (2,),
        [pl.BlockSpec((rows, width // 2), lambda g: (0, g)), whole((rows, inner))],
        [(leading((shards // 2, out_rows, 2 * inner)), out((shards, out_rows, 2 * inner), BF16))],
        name="out_grad",
    )(after(dhid_low, datt_low), att_low)[0]
    near_swaps = lambda values: [values[0]] + [swap(values[j], "patch", j) for j in range(1, here)]

    every = digits_of("img") + digits_of("patch")
    ff_bits = digits_of("img")
    ff_orders = [ff_bits[::-1], ff_bits[-2:] + ff_bits[:-2][::-1]]

    def ff_lanes(rows):
        return [(order, plan_of(rows, ff_bits, order)) for order in ff_orders]

    acts = near_swaps(act_near) + act_cross
    down_lanes = ff_lanes(width)
    down_sum = Scatter(
        own, outer(own, dys[:-1] + [after(dys[-1], out_t)], acts, width // 2, down_lanes, "down_grad"), down_lanes,
        lambda *t: [jnp.concatenate(t, axis=1).astype(BF16)], name="down_fold",
    )
    down_sum.begin()
    das[peers // 2] = after(das[peers // 2], *down_sum.both)
    das = spread(das)
    dpres = near_swaps(dpre_near) + cross(after(tuple(far[here : 2 * here]), *down_sum.both))

    got = call(
        functools.partial(attend_back_kernel, peers, per_slot, scale),
        (slots // pair,),
        [whole((rows, inner))] * peers + [whole((rows + 4 * HEADS, inner))] * peers + [kv_block],
        [(kv_block, out(keyval.shape, BF16))] + [(whole((rows, inner)), out((rows, inner), BF16))] * peers,
        scratch=[pltpu.VMEM((peers, padded, LANES), F32)],
        name="attend_back",
    )(*qs, *das, keyval)
    dkv, dqs = got[0], got[1:]
    dqs = [dqs[0]] + [swap(dqs[j], "patch", j) for j in range(1, peers)]

    low_bit, both = [("patch", 1)], [("patch", 2), ("img", 1)]
    last = [bit for bit in reversed(every) if bit not in low_bit + both]
    kv_order, qo_order = low_bit + both + last, low_bit + both[::-1] + last
    kv_lanes = [(kv_order, plan_of(2 * inner, every, kv_order))]
    kv_sum = Scatter(
        own,
        outer(own, [dkv.reshape(-1, 2 * inner)], [key_input.reshape(-1, width)], 2 * inner // 4, kv_lanes, "keyval_grad"),
        kv_lanes, lambda t: [t], name="keyval_fold",
    )
    kv_sum.begin()
    mark = down_sum.finish(*kv_sum.both)
    down_sum.begin()
    up_lanes = ff_lanes(halves * part)

    def up_end(*totals):
        total = jnp.concatenate(totals, axis=1)
        return [flipped(total)] if strided else [total.astype(BF16)]

    up_sum = Scatter(
        own, outer(own, dpres[:-1] + [after(dpres[-1], mark)], ffs, part, up_lanes, "up_grad"), up_lanes, up_end,
        name="up_fold",
    )
    up_sum.begin()

    media_grad, dlat, sums_media = call(
        keyval_back_kernel,
        (slots // group,),
        [
            leading((group, patch_rows, width)), leading((group, keys, 2 * inner)),
            whole(w_keyval.shape), gain_spec,
        ],
        [
            (leading((group, patch_rows, width)), out(media.shape, BF16)),
            (leading((group * per_slot, width)), out((rows, width), F32)),
            (whole((2, width)), out((2, width), F32)),
        ],
        name="keyval_back",
    )(media, after(dkv, *up_sum.both), w_keyval, gains)
    mark = down_sum.finish(media_grad)
    down_sum.begin()
    mark = kv_sum.finish(mark)
    kv_sum.begin()

    dq_low, latent_grad, sums = call(
        functools.partial(latent_back_kernel, peers),
        (1,),
        [whole((rows, inner))] * peers
        + [whole((rows, width))] * 3 + [whole(w_query.shape), gain_spec, whole((2, width)), whole((2, width))],
        [
            (whole((rows, inner)), out((rows, inner), BF16)),
            (whole((rows, width)), out((rows, width), BF16)),
            (whole((HEADS, width)), out((HEADS, width), F32)),
        ],
        name="latent_back",
    )(*dqs, after(dlat, mark), lat, dhidden, w_query, gains, sums_media, sums_ff)

    q_rows = inner // shards

    def open_rows(total):
        other = total[q_rows:]
        return [total[:q_rows], jnp.concatenate([other[:, :inner], other[:, inner:]], axis=0)]

    q_plan, qo_plan = plan_of(inner, every, qo_order), plan_of(2 * inner, every, qo_order)
    head = 2 * sums.shape[0]
    qo_both = call(
        functools.partial(query_kernel, qo_order[0], q_plan[0]),
        (1,),
        [whole(v.shape) for v in (dq_low, lat_low, out_t, sums)],
        [(whole((inner, width)), out((inner, width), BF16)), (whole((head + inner, width)), out((head + inner, width), BF16))],
        prefetch=1, name="query_grad",
    )(own, dq_low, lat_low, out_t, sums)
    qo_sum = Scatter(own, qo_both, [(qo_order, qo_plan)], open_rows, extra=sums, name="query_fold")
    qo_sum.begin()

    mark = qo_sum.both[0]
    if down_sum.steps == down_sum.at:
        mark = down_sum.finish(mark)
    for one in (qo_sum, up_sum, kv_sum, up_sum, qo_sum, kv_sum, qo_sum, kv_sum, qo_sum):
        mark = one.finish(mark)
        if one.at < one.steps:
            one.begin()
    (up_sum,) = up_sum.run()
    (kv_sum,) = kv_sum.run()
    q_sum, out_sum = qo_sum.run()
    (down,) = down_sum.run()
    small = lax.dynamic_slice_in_dim(
        qo_sum.extra, (own[1] * peers + own[0]) * (width // shards), width // shards, axis=1
    )
    if not strided:
        pairs = [((b % n_img) * peers + b // n_img, b) for b in range(shards)]
        up_sum = lax.ppermute(up_sum, ("img", "patch"), pairs).astype(F32).T

    down = lax.all_to_all(down.reshape(peers, -1, halves * part), "patch", 0, 0, tiled=True)
    down_t = call(
        functools.partial(place_kernel, chunk if strided else halves * part),
        (1,),
        [whole(down.shape)],
        [(whole((width // shards, ff)), out((width // shards, ff), F32))],
        name="down_place",
    )(down)[0]

    return (
        result.reshape(slots, per_slot, width),
        media_grad,
        latent_grad.reshape(slots, per_slot, width),
        q_sum.T,
        kv_sum.T,
        out_sum.T,
        up_sum,
        down_t.T,
        small[:3],
        small[3:6],
    )


def solution(mesh):
    rows = P("img", "patch", None)
    shard = P(None, ("img", "patch"))
    return jax.shard_map(
        on_device,
        mesh=mesh,
        in_specs=(rows, rows, P("img"), P(), P(), P(), P(), P(), P(), P(), rows),
        out_specs=(rows, rows, rows) + (shard,) * 7,
        check_vma=False,
    )
```

```python
import functools
import math

import jax
import jax.numpy as jnp
from jax import lax
from jax.experimental import pallas as pl
from jax.experimental.pallas import tpu as pltpu
from jax.sharding import PartitionSpec as P

HEADS = 8
SLOTS_PER = 5
EPS = 1e-05
LANES = 128
F32 = jnp.float32
BF16 = jnp.bfloat16
MIB = 1024 * 1024
TIMES = dict(latent=2.9, media=2.7, attend=3.1, mix=3.8, feed=9.6, feed_end=12.0, down_grad=4.0, attend_back=1.7, keyval_grad=3.8, up_grad=4.0, keyval_back=4.0, latent_back=1.6, query_grad=1.5)
RATE = 2e+09
ORDER = "OGXBVDWPKDLRUUQDKQKQUKQKQ"
KV_ORDER, QO_ORDER = "cxyz", "czxy"


def swap(values, axis, bit):
    n = lax.axis_size(axis)
    return lax.ppermute(values, axis, [(k, k ^ bit) for k in range(n)])


def log2(n):
    return n.bit_length() - 1


def after(values, *others):
    return lax.optimization_barrier((values,) + others)[0]


def spread(blocks):
    n = lax.axis_size("patch")
    blocks = dict(blocks)
    bit = n // 4
    while bit:
        for j in list(blocks):
            blocks[j ^ bit] = swap(blocks[j], "patch", bit)
        bit //= 2
    return [blocks[j] for j in range(n)]


def digits_of(axis):
    n = lax.axis_size(axis)
    return [(axis, 1 << k) for k in reversed(range(log2(n)))]


def chosen(own, bit):
    axis, weight = bit
    return (own[("patch", "img").index(axis)] // weight) % 2


def plan_of(rows, digits, order):
    digits, plan = list(digits), []
    for bit in order:
        at = digits.index(bit)
        plan.append(rows // 2 ** (at + 1))
        del digits[at]
        rows //= 2
    return plan


def parted(values, inner, which):
    width = values.shape[-1]
    split = values.reshape(-1, 2, inner, width)
    low, high = split[:, 0].reshape(-1, width), split[:, 1].reshape(-1, width)
    return jnp.where(which == 1, high, low), jnp.where(which == 1, low, high)


class Scatter:
    def __init__(self, own, both, lanes, end, extra=None, name=None):
        self.own, self.both, self.lanes, self.end = own, both, lanes, end
        self.extra, self.name, self.at, self.open = extra, name, 0, False
        self.steps = len(lanes[0][0])

    def begin(self, *others):
        sent = after(tuple(self.both[1::2]), *others)
        self.got = [swap(v, *order[self.at]) for v, (order, _) in zip(sent, self.lanes)]
        self.at, self.open = self.at + 1, True

    def finish(self, *others):
        kept, self.open = tuple(self.both[::2]), False
        if others:
            kept = after(kept, *others)
        nxt = None
        if self.at < self.steps:
            if all(order[self.at :] == self.lanes[0][0][self.at :] for order, _ in self.lanes):
                self.lanes = self.lanes[:1]
            nxt = [(order[self.at], plan[self.at]) for order, plan in self.lanes]
        values = fold(self.own, kept, self.got, self.extra, nxt, self.end, self.name)
        if self.extra is not None:
            self.extra = values[-1]
            values = values[:-1]
        if nxt is not None:
            self.both = values
        else:
            self.values = values
        return values[0]

    def run(self):
        while self.open:
            self.finish()
            if self.at < self.steps:
                self.begin()
        return self.values


def stats(values):
    average = jnp.mean(values, axis=-1, keepdims=True)
    centred = values - average
    spread = jnp.mean(centred * centred, axis=-1, keepdims=True)
    inverse = lax.rsqrt(spread + EPS)
    return centred * inverse, inverse


def pull(hat, inverse, grad, gain):
    scaled = grad * gain
    first = jnp.mean(scaled, axis=-1, keepdims=True)
    second = jnp.mean(scaled * hat, axis=-1, keepdims=True)
    return inverse * (scaled - first - hat * second)


def gelu_parts(values):
    cdf = 0.5 + 0.5 * lax.erf(values * (1.0 / math.sqrt(2.0)))
    density = jnp.exp(-0.5 * values * values) * (1.0 / math.sqrt(2.0 * math.pi))
    return values * cdf, cdf + values * density


def dot(a, b, dims=((1,), (0,))):
    return lax.dot_general(a, b, (dims, ((), ())), preferred_element_type=F32)


NT = ((1,), (1,))
TN = ((0,), (0,))


def low_lanes(shape):
    return lax.broadcasted_iota(jnp.int32, shape, len(shape) - 1) < LANES // 2


def live_rows(counts_ref, rows, per_slot):
    row = lax.broadcasted_iota(jnp.int32, (rows, 1), 0)
    live = jnp.zeros((rows, 1), F32)
    for sample in range(rows // (per_slot * SLOTS_PER)):
        start = sample * SLOTS_PER * per_slot
        inside = jnp.logical_and(row >= start, row < start + counts_ref[sample] * per_slot)
        live = jnp.where(inside, 1.0, live)
    return live


def paired(block):
    low = low_lanes(block.shape)
    zero = jnp.zeros_like(block)
    return jnp.concatenate([jnp.where(low, block, zero), jnp.where(low, zero, block)], axis=0)


def unpaired(block):
    half = block.shape[0] // 2
    return jnp.where(low_lanes((half, block.shape[1])), block[:half], block[half:])


def flipped(values):
    a, b = values.shape
    tall, wide = -a % LANES, -b % LANES
    if wide:
        values = jnp.concatenate([values, jnp.zeros((a, wide), F32)], axis=1)
    if tall:
        values = jnp.concatenate([values, jnp.zeros((tall, b + wide), F32)], axis=0)
    return values.T[:b, :a]


def call(kernel, grid, ins, outs, scratch=(), vmem=40, prefetch=0, name=None):
    return pl.pallas_call(
        kernel,
        grid_spec=pltpu.PrefetchScalarGridSpec(
            num_scalar_prefetch=prefetch,
            grid=grid,
            in_specs=ins,
            out_specs=[spec for spec, _ in outs],
            scratch_shapes=list(scratch),
        ),
        out_shape=[shape for _, shape in outs],
        compiler_params=pltpu.CompilerParams(
            vmem_limit_bytes=vmem * MIB, dimension_semantics=("arbitrary",) * len(grid)
        ),
        cost_estimate=pl.CostEstimate(flops=int(TIMES.get(name, 0.8) * RATE), bytes_accessed=100000, transcendentals=0),
        name=name,
    )


def whole(shape):
    zeros = (0,) * len(shape)
    return pl.BlockSpec(tuple(shape), lambda *_: zeros)


def leading(shape):
    zeros = (0,) * (len(shape) - 1)
    return pl.BlockSpec(tuple(shape), lambda g, *_: (g,) + zeros)


def out(shape, dtype):
    return jax.ShapeDtypeStruct(tuple(shape), dtype)


SMEM = pl.BlockSpec(memory_space=pltpu.SMEM)


def packed(values):
    high = values.astype(BF16)
    left = values - high.astype(F32)
    middle = left.astype(BF16)
    small = left - middle.astype(F32)
    top = jnp.concatenate([high.astype(F32), middle.astype(F32)], axis=1)
    bottom = jnp.concatenate([small, jnp.zeros_like(small)], axis=1)
    return jnp.concatenate([top, bottom], axis=0).astype(BF16)


def unpacked(values):
    values = values.astype(F32)
    n, m = values.shape[0] // 2, values.shape[1] // 2
    return values[:n, :m] + values[:n, m:] + values[n:, :m]


def latent_kernel(per_slot, counts, lat, grad, gain, bias, w_query, lat_low, q_low, dy):
    hat, _ = stats(lat[...].astype(F32))
    low = (hat * gain[1:2] + bias[1:2]).astype(BF16)
    lat_low[...] = low
    q_low[...] = dot(low, w_query[...]).astype(BF16)
    live = live_rows(counts, lat.shape[0], per_slot)
    dy[...] = (live * grad[...].astype(F32)).astype(BF16)


def media_kernel(media, lat_low, gain, bias, w_keyval, key_input, keyval):
    n, rows, width = media.shape
    hat, _ = stats(media[...].reshape(n * rows, width).astype(F32))
    low = (hat * gain[0:1] + bias[0:1]).astype(BF16)
    key_input[:, :rows, :] = low.reshape(n, rows, width)
    key_input[:, rows:, :] = lat_low[...].reshape(n, -1, width)
    every = key_input[...].reshape(-1, width)
    keyval[...] = dot(every, w_keyval[...]).astype(BF16).reshape(keyval.shape)


def attend_kernel(peers, per_slot, scale, *refs):
    qs, kv, parts, held = refs[:peers], refs[peers], refs[peers + 1 : 2 * peers + 1], refs[2 * peers + 1]
    n, keys, inner = kv.shape[0], kv.shape[1], kv.shape[2] // 2
    step = pl.program_id(0)
    items = [(s, t) for s in range(n) for t in range(inner // LANES)]
    cuts = [slice(t * LANES, (t + 1) * LANES) for t in range(2 * inner // LANES)]
    rows = [pl.multiple_of((step * n + s) * per_slot, per_slot) for s in range(n)]
    ones = jnp.ones((keys, LANES), BF16)

    @pl.when(step == 0)
    def _():
        held[...] = jnp.zeros_like(held)

    scores = []
    for s, t in items:
        q = paired(jnp.concatenate([ref[pl.ds(rows[s], per_slot), cuts[t]] for ref in qs], axis=0))
        scores.append(dot(q, kv[s, :, cuts[t]], NT) * scale)
    tops = [jnp.max(score, axis=-1, keepdims=True) for score in scores]
    probs = [jnp.exp(score - top).astype(BF16) for score, top in zip(scores, tops)]
    sums = [
        dot(prob, jnp.concatenate([kv[s, :, cuts[inner // LANES + t]], ones], axis=1))
        for prob, (s, t) in zip(probs, items)
    ]
    lane = lax.broadcasted_iota(jnp.int32, (peers * per_slot, LANES), 1)
    logs = [jnp.zeros((peers * per_slot, LANES), F32) for _ in range(n)]
    for (s, t), both, top in zip(items, sums, tops):
        total = unpaired(both[:, LANES:])
        o = (unpaired(both[:, :LANES]) / total).astype(BF16)
        lse = unpaired(jnp.broadcast_to(top, (top.shape[0], LANES))) + jnp.log(total)
        here = jnp.logical_or(lane == t, lane == LANES // 2 + HEADS // 2 + t)
        logs[s] = jnp.where(here, lse, logs[s])
        for i in range(peers):
            parts[i][pl.ds(rows[s], per_slot), cuts[t]] = o[i * per_slot : (i + 1) * per_slot]
    for s in range(n):
        for i in range(peers):
            held[i, pl.ds(rows[s], per_slot), :] = logs[s][i * per_slot : (i + 1) * per_slot]

    @pl.when(step == pl.num_programs(0) - 1)
    def _():
        for i in range(peers):
            turned = held[i].T
            turned = turned[:HEADS] + turned[LANES // 2 : LANES // 2 + HEADS]
            parts[i][-2 * HEADS :, :] = packed(turned)


def mix_kernel(peers, *refs):
    parts = refs[:peers]
    lat, w_out, gain, bias, attended, att_low, hidden, ff_low, lse_out = refs[peers:]
    rows, inner = attended.shape
    logs = [unpacked(ref[rows:, :]) for ref in parts]
    top = functools.reduce(jnp.maximum, logs)
    lse = top + jnp.log(sum(jnp.exp(v - top) for v in logs))
    lse_out[...] = lse
    weights = flipped(jnp.concatenate([jnp.exp(v - lse) for v in logs], axis=0))[:rows]
    low = low_lanes((rows, LANES))
    for t in range(inner // LANES):
        cut = slice(t * LANES, (t + 1) * LANES)
        total = jnp.zeros((rows, LANES), F32)
        for j in range(peers):
            at = j * HEADS + t
            other = at + HEADS // 2
            weight = jnp.where(low, weights[:, at : at + 1], weights[:, other : other + 1])
            total = total + weight * parts[j][:rows, cut].astype(F32)
        attended[:, cut] = total
        att_low[:, cut] = total.astype(BF16)
    state = lat[...].astype(F32) + dot(att_low[...], w_out[...])
    hidden[...] = state
    hat, _ = stats(state)
    ff_low[...] = (hat * gain[2:3] + bias[2:3]).astype(BF16)


def feed_columns(ff_low, dy, ups, downs, acts, dpres, res, dff):
    half = len(ups) // 2
    a = pl.program_id(1)
    parts = []
    for at in (slice(0, half), slice(half, 2 * half)):
        up = jnp.concatenate([ref[...] for ref in ups[at]], axis=1)
        down = jnp.concatenate([ref[...] for ref in downs[at]], axis=0)
        parts.append((up, down, dot(ff_low[...], up), dot(dy[...], down, NT)))
    done = []
    for up, down, pre, dact in parts:
        value, slope = gelu_parts(pre)
        value = value.astype(BF16)
        back = (slope * dact).astype(BF16)
        res[...] += dot(value, down)
        dff[...] += dot(back, up, NT)
        done.append((value, back))
    for at, (act, dpre) in enumerate(zip(acts, dpres)):

        @pl.when(pl.program_id(0) == at)
        def _():
            width = done[0][0].shape[1]
            for k, (value, back) in enumerate(done):
                act[a, :, k * width : (k + 1) * width] = value
                dpre[a, :, k * width : (k + 1) * width] = back


def first_step():
    return jnp.logical_and(pl.program_id(0) == 0, pl.program_id(1) == 0)


def last_step():
    ends = [pl.program_id(k) == pl.num_programs(k) - 1 for k in range(2)]
    return jnp.logical_and(*ends)


def feed_kernel(count, here, own, ff_low, dy, *refs):
    ups, downs, refs = refs[:count], refs[count : 2 * count], refs[2 * count :]
    acts, dpres, (res, dff) = refs[:here], refs[here : 2 * here], refs[2 * here :]

    @pl.when(first_step())
    def _():
        res[...] = jnp.zeros_like(res)
        dff[...] = jnp.zeros_like(dff)

    feed_columns(ff_low, dy, ups, downs, acts, dpres, res, dff)


def feed_end_kernel(per_slot, count, here, own, counts, ff_low, dy, *refs):
    ups, downs, refs = refs[:count], refs[count : 2 * count], refs[2 * count :]
    res_in, dff_in, hidden, attended, lse, w_out, gain = refs[:7]
    acts, dpres, refs = refs[7 : 7 + here], refs[7 + here : 7 + 2 * here], refs[7 + 2 * here :]
    result, dhidden, dhid_low, datt_low, sums, res, dff = refs

    @pl.when(first_step())
    def _():
        res[...] = res_in[...]
        dff[...] = dff_in[...]

    feed_columns(ff_low, dy, ups, downs, acts, dpres, res, dff)

    @pl.when(last_step())
    def _():
        rows, inner = attended.shape
        live = live_rows(counts, rows, per_slot)
        state = hidden[...]
        result[...] = (live * (state + res[...])).astype(BF16)
        hat, inverse = stats(state)
        grad = dff[...]
        sums[0:1] = jnp.sum(grad * hat, axis=0, keepdims=True)
        sums[1:2] = jnp.sum(grad, axis=0, keepdims=True)
        back = dy[...].astype(F32) + pull(hat, inverse, grad, gain[2:3])
        dhidden[...] = back
        dhid_low[...] = back.astype(BF16)
        datt = dot(dhid_low[...], w_out[...], NT).astype(BF16)
        datt_low[:rows, :] = datt
        product = datt.astype(F32) * attended[...]
        low = low_lanes((rows, LANES))
        lane = lax.broadcasted_iota(jnp.int32, (rows, LANES), 1)
        delta = jnp.zeros((rows, LANES), F32)
        for t in range(inner // LANES):
            both = product[:, t * LANES : (t + 1) * LANES]
            first = jnp.sum(jnp.where(low, both, 0.0), axis=-1, keepdims=True)
            second = jnp.sum(jnp.where(low, 0.0, both), axis=-1, keepdims=True)
            delta = jnp.where(lane == t, first, delta)
            delta = jnp.where(lane == HEADS // 2 + t, second, delta)
        turned = flipped(jnp.concatenate([delta, jnp.zeros((-rows % LANES, LANES), F32)], axis=0))
        datt_low[rows:, :] = packed(jnp.concatenate([lse[...], turned[:HEADS]], axis=0))


def attend_back_kernel(peers, per_slot, scale, *refs):
    qs, das, kv, dkv = refs[:peers], refs[peers : 2 * peers], refs[2 * peers], refs[2 * peers + 1]
    dqs, held = refs[2 * peers + 2 : 3 * peers + 2], refs[3 * peers + 2]
    n, inner = kv.shape[0], kv.shape[2] // 2
    step = pl.program_id(0)
    items = [(s, t) for s in range(n) for t in range(inner // LANES)]
    cuts = [slice(t * LANES, (t + 1) * LANES) for t in range(2 * inner // LANES)]
    rows = [pl.multiple_of((step * n + s) * per_slot, per_slot) for s in range(n)]
    later = inner // LANES

    @pl.when(step == 0)
    def _():
        for i in range(peers):
            turned = unpacked(das[i][-4 * HEADS :, :])
            held[i, :, : 2 * HEADS] = flipped(turned)

    def column(block, h):
        other = h + HEADS // 2
        return jnp.concatenate([block[:, h : h + 1], block[:, other : other + 1]], axis=0)

    sts = [
        jnp.concatenate([held[i, pl.ds(row, per_slot), :] for i in range(peers)], axis=0) for row in rows
    ]
    qp = [paired(jnp.concatenate([ref[pl.ds(rows[s], per_slot), cuts[t]] for ref in qs], axis=0)) for s, t in items]
    dp = [paired(jnp.concatenate([ref[pl.ds(rows[s], per_slot), cuts[t]] for ref in das], axis=0)) for s, t in items]
    scores = [dot(q, kv[s, :, cuts[t]], NT) for q, (s, t) in zip(qp, items)]
    dprobs = [dot(d, kv[s, :, cuts[later + t]], NT) for d, (s, t) in zip(dp, items)]
    probs = [jnp.exp(score * scale - column(sts[s], t)) for score, (s, t) in zip(scores, items)]
    dscores = [
        (prob * (dprob - column(sts[s], HEADS + t))).astype(BF16)
        for prob, dprob, (s, t) in zip(probs, dprobs, items)
    ]
    for (s, t), prob, d in zip(items, probs, dp):
        dkv[s, :, cuts[later + t]] = dot(prob.astype(BF16), d, TN).astype(BF16)
    for (s, t), ds, q in zip(items, dscores, qp):
        dkv[s, :, cuts[t]] = (dot(ds, q, TN) * scale).astype(BF16)
    for (s, t), ds in zip(items, dscores):
        dq = (unpaired(dot(ds, kv[s, :, cuts[t]])) * scale).astype(BF16)
        for i in range(peers):
            dqs[i][pl.ds(rows[s], per_slot), cuts[t]] = dq[i * per_slot : (i + 1) * per_slot]


def keyval_back_kernel(media, dkv, w_keyval, gain, media_grad, dlat, sums):
    n, rows, width = media.shape
    grad = dot(dkv[...].reshape(-1, dkv.shape[2]), w_keyval[...], NT).reshape(n, -1, width)
    dlat[...] = grad[:, rows:].reshape(dlat.shape)
    grad = grad[:, :rows].reshape(n * rows, width)
    hat, inverse = stats(media[...].reshape(n * rows, width).astype(F32))
    media_grad[...] = pull(hat, inverse, grad, gain[0:1]).astype(BF16).reshape(media_grad.shape)

    @pl.when(pl.program_id(0) == 0)
    def _():
        sums[...] = jnp.zeros_like(sums)

    sums[0:1] += jnp.sum(grad * hat, axis=0, keepdims=True)
    sums[1:2] += jnp.sum(grad, axis=0, keepdims=True)


def latent_back_kernel(peers, *refs):
    dqs = refs[:peers]
    dlat, lat, dhidden, w_query, gain, sums_media, sums_ff, dq_low, latent_grad, sums = refs[peers:]
    dq = sum(ref[...].astype(F32) for ref in dqs).astype(BF16)
    dq_low[...] = dq
    grad = dlat[...] + dot(dq, w_query[...], NT)
    hat, inverse = stats(lat[...].astype(F32))
    latent_grad[...] = (dhidden[...] + pull(hat, inverse, grad, gain[1:2])).astype(BF16)
    sums[0:1] = sums_media[0:1]
    sums[1:2] = jnp.sum(grad * hat, axis=0, keepdims=True)
    sums[2:3] = sums_ff[0:1]
    sums[3:4] = sums_media[1:2]
    sums[4:5] = jnp.sum(grad, axis=0, keepdims=True)
    sums[5:6] = sums_ff[1:2]


def halved(values):
    high = values.astype(BF16).astype(F32)
    return jnp.concatenate([high, values - high], axis=0).astype(BF16)


def joined(values):
    values = values.astype(F32)
    half = values.shape[0] // 2
    return values[:half] + values[half:]


def outer_kernel(count, lanes, own, *refs):
    lefts, rights, refs = refs[:count], refs[count : 2 * count], refs[2 * count :]
    results, held = refs[:-1], refs[-1]

    @pl.when(pl.program_id(0) == 0)
    def _():
        at = 0
        for ref in rights:
            rows, width = ref.shape[-2:]
            for k in range(held.shape[1] // width):
                held[at : at + rows, k * width : (k + 1) * width] = ref[k] if len(ref.shape) == 3 else ref[...]
            at += rows

    left = jnp.concatenate([ref[...].reshape(-1, ref.shape[-1]) for ref in lefts], axis=0)
    product = dot(left, held[...], TN)
    width = product.shape[1] // len(lanes)
    for k, (bit, inner) in enumerate(lanes):
        kept, sent = parted(product[:, k * width : (k + 1) * width], inner, chosen(own, bit))
        results[2 * k][...] = kept.astype(BF16)
        results[2 * k + 1][...] = sent.astype(BF16)


def outer(own, lefts, rights, tile, lanes, name):
    count = len(lefts)
    wide = lambda v: v.shape[-1] * (v.shape[0] if v.ndim == 3 else 1)
    a, b = wide(lefts[0]), wide(rights[0])

    def left_spec(v):
        if v.ndim == 3:
            return pl.BlockSpec((1, v.shape[1], tile), lambda g, *_: (g, 0, 0))
        return pl.BlockSpec((v.shape[0], tile), lambda g, *_: (0, g))

    total = sum(v.shape[-2] for v in rights)
    steps, part = a // tile, b // len(lanes)
    spec = pl.BlockSpec((tile // 2, part), lambda g, *_: (g, 0))
    return call(
        functools.partial(outer_kernel, count, [(order[0], plan[0]) for order, plan in lanes]),
        (steps,),
        [left_spec(v) for v in lefts] + [whole(v.shape) for v in rights],
        [(spec, out((a // 2, part), BF16))] * (2 * len(lanes)),
        scratch=[pltpu.VMEM((total, b), BF16)],
        prefetch=1, name=name,
    )(own, *lefts, *rights)


def query_kernel(bit, rows, own, dq, lat_low, out_t, sums, kept, sent):
    width = lat_low.shape[1]
    which = chosen(own, bit)
    other_rows = out_t.shape[1]
    product = dot(dq[...], lat_low[...], TN)
    first = parted(product, rows, which)
    second = parted(out_t[...].astype(F32).reshape(-1, width), other_rows, which)
    both = [
        jnp.concatenate([a.reshape(-1, rows, width), b.reshape(-1, other_rows, width)], axis=1).reshape(-1, width)
        for a, b in zip(first, second)
    ]
    head = 2 * sums.shape[0]
    kept[...] = both[0].astype(BF16)
    sent[:head, :] = halved(sums[...])
    sent[head:, :] = both[1].astype(BF16)


def side_by_side_kernel(rows, left, right, result):
    product = dot(left[...], right[...], TN).astype(BF16)
    split = product.reshape(-1, 2, rows, product.shape[1])
    result[...] = jnp.concatenate([split[:, 0], split[:, 1]], axis=-1)


def fold_kernel(nxt, end, lanes, extra, own, *refs):
    kept, got, refs = refs[:lanes], refs[lanes : 2 * lanes], refs[2 * lanes :]
    head = 0
    if extra:
        more, refs = refs[0], refs[1:]
        head = 2 * more.shape[0]
        small = more[...] + joined(got[0][:head, :])
        refs[-1][...] = small
    totals = [a[...].astype(F32) + b[head:, :].astype(F32) for a, b in zip(kept, got)]
    if nxt is None:
        for ref, values in zip(refs, end(*totals)):
            ref[...] = values.astype(ref.dtype)
        return
    if len(nxt) < len(totals):
        totals = [jnp.concatenate(totals, axis=1)]
    for k, (total, (bit, inner)) in enumerate(zip(totals, nxt)):
        keep, send = parted(total, inner, chosen(own, bit))
        refs[2 * k][...] = keep.astype(BF16)
        refs[2 * k + 1][head:, :] = send.astype(BF16)
    if extra:
        refs[1][:head, :] = halved(small)


def fold(own, kept, got, extra, nxt, end, name):
    ins = list(kept) + list(got)
    if nxt is not None:
        head = 0 if extra is None else 2 * extra.shape[0]
        shapes = []
        for _ in nxt:
            rows, width = kept[0].shape[0], kept[0].shape[1] * len(kept) // len(nxt)
            shapes += [out((rows // 2, width), BF16), out((head + rows // 2, width), BF16)]
    else:
        shapes = list(jax.eval_shape(end, *(out(v.shape, F32) for v in kept)))
    if extra is not None:
        ins.append(extra)
        shapes.append(out(extra.shape, F32))
    return call(
        functools.partial(fold_kernel, nxt, end, len(kept), extra is not None),
        (1,),
        [whole(v.shape) for v in ins],
        [(whole(s.shape), s) for s in shapes],
        prefetch=1, name=name,
    )(own, *ins)


def place_kernel(block, parts, result):
    peers, _, width = parts.shape
    for p in range(peers):
        for k in range(width // block):
            at = (k * peers + p) * block
            result[:, at : at + block] = parts[p, :, k * block : (k + 1) * block].astype(F32)


def on_device(
    media, latents, counts, gains, biases, w_query, w_keyval, w_out, w_up, w_down, out_grad
):
    slots, patch_rows, width = media.shape
    per_slot = latents.shape[1]
    inner = w_query.shape[1]
    ff = w_up.shape[1]
    n_img, peers = lax.axis_size("img"), lax.axis_size("patch")
    shards = n_img * peers
    scale = 1.0 / math.sqrt(inner // HEADS)
    rows = slots * per_slot
    keys = patch_rows + per_slot
    padded = -(-rows // LANES) * LANES
    gain_spec = whole(gains.shape)
    lat = latents.reshape(rows, width)

    own = jnp.stack([lax.axis_index("patch"), lax.axis_index("img")]).astype(jnp.int32)
    fine = width // shards % 16 == 0 and inner // shards % 16 == 0
    lat_low, q_low, dy = call(
        functools.partial(latent_kernel, per_slot),
        (1,),
        [SMEM, whole((rows, width)), whole((rows, width)), gain_spec, gain_spec, whole(w_query.shape)],
        [
            (whole((rows, width)), out((rows, width), BF16)),
            (whole((rows, inner)), out((rows, inner), BF16)),
            (whole((rows, width)), out((rows, width), BF16)),
        ],
        vmem=62, name="latent",
    )(counts, lat, out_grad.reshape(rows, width), gains, biases, w_query)
    qs = {0: q_low}
    bit = peers // 2
    qs[bit] = swap(q_low, "patch", bit)

    group = slots // 2
    key_input, keyval = call(
        media_kernel,
        (slots // group,),
        [
            leading((group, patch_rows, width)), leading((group * per_slot, width)),
            gain_spec, gain_spec, whole(w_keyval.shape),
        ],
        [
            (leading((group, keys, width)), out((slots, keys, width), BF16)),
            (leading((group, keys, 2 * inner)), out((slots, keys, 2 * inner), BF16)),
        ],
        name="media",
    )(media, lat_low, gains, biases, w_keyval)
    first = after(qs[bit], keyval)
    qs[bit] = first
    while bit > 1:
        bit //= 2
        for j in list(qs):
            qs[j ^ bit] = swap(qs[j], "patch", bit)
    qs = [qs[j] for j in range(peers)]

    pair = 2
    kv_block = leading((pair, keys, 2 * inner))
    part_rows = rows + 2 * HEADS
    stat_out = (whole((HEADS, padded)), out((HEADS, padded), F32))
    parts = call(
        functools.partial(attend_kernel, peers, per_slot, scale),
        (slots // pair,),
        [whole((rows, inner))] * peers + [kv_block],
        [(whole((part_rows, inner)), out((part_rows, inner), BF16))] * peers,
        scratch=[pltpu.VMEM((peers, padded, LANES), F32)],
        name="attend",
    )(*qs, keyval)
    dys = {0: dy, peers // 2: swap(dy, "patch", peers // 2)}
    parts = [parts[0]] + [swap(after(parts[j], dys[peers // 2]), "patch", j) for j in range(1, peers)]

    attended, att_low, hidden, ff_low, lse = call(
        functools.partial(mix_kernel, peers),
        (1,),
        [whole((part_rows, inner))] * peers
        + [whole((rows, width)), whole(w_out.shape), gain_spec, gain_spec],
        [
            (whole((rows, inner)), out((rows, inner), F32)),
            (whole((rows, inner)), out((rows, inner), BF16)),
            (whole((rows, width)), out((rows, width), F32)),
            (whole((rows, width)), out((rows, width), BF16)),
            stat_out,
        ],
        vmem=62, name="mix",
    )(*parts, lat, w_out, gains, biases)
    bit = peers // 2
    ffs = {0: ff_low, bit: swap(ff_low, "patch", bit)}
    dys = spread({0: after(dy, ff_low), bit: after(dys[bit], ff_low)})

    halves = 2
    blocks = ff // (peers * halves * LANES)
    chunk = ff // shards
    strided = chunk % LANES == 0

    def column(own, j, a, k):
        p, k = own[0] ^ j, a * blocks + k
        if strided:
            return ((k // (chunk // LANES)) * peers + p) * (chunk // LANES) + k % (chunk // LANES)
        return p * halves * blocks + k

    def weights(first, stride):
        ups = [
            pl.BlockSpec((width, LANES), lambda g, a, own, k=k: (0, column(own, first + stride * g, a, k)))
            for k in range(blocks)
        ]
        downs = [
            pl.BlockSpec((LANES, width), lambda g, a, own, k=k: (column(own, first + stride * g, a, k), 0))
            for k in range(blocks)
        ]
        return ups + downs

    part = ff // (peers * halves)
    here = peers // 2
    columns = (whole((halves, rows, part)), out((halves, rows, part), BF16))
    wide_low = (whole((rows, width)), out((rows, width), BF16))
    wide = (whole((rows, width)), out((rows, width), F32))
    count = blocks
    far = call(
        functools.partial(feed_kernel, count, here),
        (here, halves),
        [whole((rows, width))] * 2 + weights(here, 1),
        [columns] * (2 * here) + [wide, wide],
        vmem=62, prefetch=1, name="feed",
    )(own, ff_low, dy, *([w_up] * count), *([w_down] * count))
    ffs[peers // 2] = after(ffs[peers // 2], far[-1])
    ffs = spread(ffs)

    def cross(values):
        return [swap(v, "patch", here + k) for k, v in enumerate(values)]

    act_cross = cross(after(tuple(far[:here]), ffs[peers // 2]))
    near = call(
        functools.partial(feed_end_kernel, per_slot, count, here),
        (here, halves),
        [SMEM] + [whole((rows, width))] * 2 + weights(here - 1, -1)
        + [whole((rows, width))] * 3 + [whole((rows, inner)), whole((HEADS, padded)), whole(w_out.shape), gain_spec],
        [columns] * (2 * here)
        + [wide_low, wide, wide_low]
        + [(whole((rows + 4 * HEADS, inner)), out((rows + 4 * HEADS, inner), BF16)), (whole((2, width)), out((2, width), F32))],
        scratch=[pltpu.VMEM((rows, width), F32), pltpu.VMEM((rows, width), F32)],
        vmem=62, prefetch=1, name="feed_end",
    )(own, counts, after(ff_low, *ffs[1:], *dys[1:]), dy, *([w_up] * count), *([w_down] * count),
      far[2 * here], far[2 * here + 1], hidden, attended, lse, w_out, gains)
    result, dhidden, dhid_low, datt_low, sums_ff = near[2 * here :]
    act_near, dpre_near = list(reversed(near[:here])), list(reversed(near[here : 2 * here]))

    das = {0: datt_low, peers // 2: swap(datt_low, "patch", peers // 2)}
    out_rows = width // shards // 2
    q_rows = inner // shards
    every, ff_bits = digits_of("img") + digits_of("patch"), digits_of("img")
    ff_orders = [ff_bits[::-1], ff_bits[-2:] + ff_bits[:-2][::-1]]
    named = {"c": ("patch", 1), "x": ("patch", 2), "y": ("img", 1), "z": ("img", 2)}

    def order_of(letters):
        head = [named[k] for k in letters]
        return head + [bit for bit in reversed(every) if bit not in head]

    def ff_lanes(rows):
        return [(order, plan_of(rows, ff_bits, order)) for order in ff_orders]

    def near_swaps(values):
        return [values[0]] + [swap(values[j], "patch", j) for j in range(1, here)]

    kv_order, qo_order = order_of(KV_ORDER), order_of(QO_ORDER)
    acts = near_swaps(act_near) + act_cross
    dpre_first = near_swaps(dpre_near)
    got, sums_of = {}, {}

    def out_grad(mark):
        got["out_t"] = call(
            functools.partial(side_by_side_kernel, out_rows),
            (2,),
            [pl.BlockSpec((rows, width // 2), lambda g: (0, g)), whole((rows, inner))],
            [(leading((shards // 2, out_rows, 2 * inner)), out((shards, out_rows, 2 * inner), BF16))],
            name="out_grad",
        )(after(dhid_low, mark), att_low)[0]
        return got["out_t"]

    def begun(letter, scatter):
        sums_of[letter] = scatter
        mark = scatter.both[0]
        scatter.begin()
        return mark

    def down_grad(mark):
        lanes = ff_lanes(width)
        both = outer(own, dys[:-1] + [after(dys[-1], mark)], acts, width // 2, lanes, "down_grad")
        return begun("D", Scatter(own, both, lanes, lambda t: [t.astype(BF16)], name="down_fold"))

    def send_dpre(mark):
        got["dpres"] = dpre_first + cross(after(tuple(far[here : 2 * here]), mark))
        return mark

    def attend_back(mark):
        near_das = spread({0: das[0], peers // 2: after(das[peers // 2], mark)})
        values = call(
            functools.partial(attend_back_kernel, peers, per_slot, scale),
            (slots // pair,),
            [whole((rows, inner))] * peers + [whole((rows + 4 * HEADS, inner))] * peers + [kv_block],
            [(kv_block, out(keyval.shape, BF16))] + [(whole((rows, inner)), out((rows, inner), BF16))] * peers,
            scratch=[pltpu.VMEM((peers, padded, LANES), F32)],
            name="attend_back",
        )(*qs, *near_das, keyval)
        got["dkv"], dqs = values[0], values[1:]
        got["dqs"] = [dqs[0]] + [swap(dqs[j], "patch", j) for j in range(1, peers)]
        return got["dkv"]

    def keyval_back(mark):
        got["media_grad"], got["dlat"], got["sums_media"] = call(
            keyval_back_kernel,
            (slots // group,),
            [
                leading((group, patch_rows, width)), leading((group, keys, 2 * inner)),
                whole(w_keyval.shape), gain_spec,
            ],
            [
                (leading((group, patch_rows, width)), out(media.shape, BF16)),
                (leading((group * per_slot, width)), out((rows, width), F32)),
                (whole((2, width)), out((2, width), F32)),
            ],
            name="keyval_back",
        )(media, after(got["dkv"], mark), w_keyval, gains)
        return got["sums_media"]

    def keyval_grad(mark):
        lanes = [(kv_order, plan_of(2 * inner, every, kv_order))]
        both = outer(
            own, [after(got["dkv"], mark).reshape(-1, 2 * inner)], [key_input.reshape(-1, width)], 2 * inner // 4,
            lanes, "keyval_grad",
        )
        return begun("K", Scatter(own, both, lanes, lambda t: [t], name="keyval_fold"))

    def up_grad(mark):
        lanes, dpres = ff_lanes(halves * part), got["dpres"]
        both = outer(own, dpres[:-1] + [after(dpres[-1], mark)], ffs, part, lanes, "up_grad")
        end = lambda t: [flipped(t)] if strided else [t.astype(BF16)]
        return begun("U", Scatter(own, both, lanes, end, name="up_fold"))

    def latent_back(mark):
        got["dq_low"], got["latent_grad"], got["sums"] = call(
            functools.partial(latent_back_kernel, peers),
            (1,),
            [whole((rows, inner))] * peers
            + [whole((rows, width))] * 3 + [whole(w_query.shape), gain_spec, whole((2, width)), whole((2, width))],
            [
                (whole((rows, inner)), out((rows, inner), BF16)),
                (whole((rows, width)), out((rows, width), BF16)),
                (whole((HEADS, width)), out((HEADS, width), F32)),
            ],
            name="latent_back",
        )(*got["dqs"], after(got["dlat"], mark), lat, dhidden, w_query, gains, got["sums_media"], sums_ff)
        return got["dq_low"]

    def open_rows(total):
        other = total[q_rows:]
        return [total[:q_rows], jnp.concatenate([other[:, :inner], other[:, inner:]], axis=0)]

    def query_grad(mark):
        q_plan, qo_plan = plan_of(inner, every, qo_order), plan_of(2 * inner, every, qo_order)
        sums = got["sums"]
        tall = 2 * sums.shape[0] + inner
        ins = (after(got["dq_low"], mark), lat_low, got["out_t"], sums)
        both = call(
            functools.partial(query_kernel, qo_order[0], q_plan[0]),
            (1,),
            [whole(v.shape) for v in ins],
            [(whole((inner, width)), out((inner, width), BF16)), (whole((tall, width)), out((tall, width), BF16))],
            prefetch=1, name="query_grad",
        )(own, *ins)
        return begun("Q", Scatter(own, both, [(qo_order, qo_plan)], open_rows, extra=sums, name="query_fold"))

    tasks = dict(
        O=out_grad, G=down_grad, X=send_dpre, B=attend_back, V=keyval_back, W=keyval_grad, P=up_grad, L=latent_back,
        R=query_grad,
    )
    mark = datt_low
    for letter in ORDER:
        if letter in tasks:
            mark = tasks[letter](mark)
        else:
            one = sums_of[letter]
            mark = one.finish(mark)
            if one.at < one.steps:
                one.begin()
    media_grad, latent_grad = got["media_grad"], got["latent_grad"]
    qo_sum = sums_of["Q"]
    (up_sum,), (kv_sum,), (down,), (q_sum, out_sum) = (sums_of[k].run() for k in "UKDQ")
    small = lax.dynamic_slice_in_dim(
        qo_sum.extra, (own[1] * peers + own[0]) * (width // shards), width // shards, axis=1
    )
    if not strided:
        pairs = [((b % n_img) * peers + b // n_img, b) for b in range(shards)]
        up_sum = lax.ppermute(up_sum, ("img", "patch"), pairs).astype(F32).T

    down = lax.all_to_all(down.reshape(peers, -1, halves * part), "patch", 0, 0, tiled=True)
    down_t = call(
        functools.partial(place_kernel, chunk if strided else halves * part),
        (1,),
        [whole(down.shape)],
        [(whole((width // shards, ff)), out((width // shards, ff), F32))],
        name="down_place",
    )(down)[0]

    return (
        result.reshape(slots, per_slot, width),
        media_grad,
        latent_grad.reshape(slots, per_slot, width),
        q_sum.T,
        kv_sum.T,
        out_sum.T,
        up_sum,
        down_t.T,
        small[:3],
        small[3:6],
    )


def solution(mesh):
    rows = P("img", "patch", None)
    shard = P(None, ("img", "patch"))
    return jax.shard_map(
        on_device,
        mesh=mesh,
        in_specs=(rows, rows, P("img"), P(), P(), P(), P(), P(), P(), P(), rows),
        out_specs=(rows, rows, rows) + (shard,) * 7,
        check_vma=False,
    )
```

```python
import functools
import math

import jax
import jax.numpy as jnp
from jax import lax
from jax.experimental import pallas as pl
from jax.experimental.pallas import tpu as pltpu
from jax.sharding import PartitionSpec as P

HEADS = 8
SLOTS_PER = 5
EPS = 1e-05
LANES = 128
F32 = jnp.float32
BF16 = jnp.bfloat16
MIB = 1024 * 1024
TIMES = dict(latent=2.9, media=2.7, attend=3.1, mix=3.8, feed=0.1, feed_end=36.0, down_grad=4.0, attend_back=1.7, keyval_grad=11.4, up_grad=4.0, keyval_back=4.0, latent_back=1.6, query_grad=1.5, pair=0.8, down_fold=0.8, up_fold=0.8, keyval_fold=0.8, query_fold=1.6, out_grad=0.8)
RATE = 2e+09
ORDER = "OGXBVDWYPKDLRUUQDKQKUQKQKQ"
KV_ORDER, QO_ORDER = "cxyz", "cyzx"


def swap(values, axis, bit):
    n = lax.axis_size(axis)
    return lax.ppermute(values, axis, [(k, k ^ bit) for k in range(n)])


def log2(n):
    return n.bit_length() - 1


def after(values, *others):
    return lax.optimization_barrier((values,) + others)[0]


def spread(blocks):
    n = lax.axis_size("patch")
    blocks = dict(blocks)
    bit = n // 4
    while bit:
        for j in list(blocks):
            blocks[j ^ bit] = swap(blocks[j], "patch", bit)
        bit //= 2
    return [blocks[j] for j in range(n)]


def digits_of(axis):
    n = lax.axis_size(axis)
    return [(axis, 1 << k) for k in reversed(range(log2(n)))]


def chosen(own, bit):
    axis, weight = bit
    return (own[("patch", "img").index(axis)] // weight) % 2


def plan_of(rows, digits, order):
    digits, plan = list(digits), []
    for bit in order:
        at = digits.index(bit)
        plan.append(rows // 2 ** (at + 1))
        del digits[at]
        rows //= 2
    return plan


def parted(values, inner, which):
    width = values.shape[-1]
    split = values.reshape(-1, 2, inner, width)
    low, high = split[:, 0].reshape(-1, width), split[:, 1].reshape(-1, width)
    return jnp.where(which == 1, high, low), jnp.where(which == 1, low, high)


class Scatter:
    def __init__(self, own, both, lanes, end, extra=None, name=None):
        self.own, self.both, self.lanes, self.end = own, both, lanes, end
        self.extra, self.name, self.at, self.open = extra, name, 0, False
        self.steps = len(lanes[0][0])

    def begin(self, *others):
        sent = after(tuple(self.both[1::2]), *others)
        self.got = [swap(v, *order[self.at]) for v, (order, _) in zip(sent, self.lanes)]
        self.at, self.open = self.at + 1, True

    def finish(self, *others):
        kept, self.open = tuple(self.both[::2]), False
        if others:
            kept = after(kept, *others)
        nxt = None
        if self.at < self.steps:
            if all(order[self.at :] == self.lanes[0][0][self.at :] for order, _ in self.lanes):
                self.lanes = self.lanes[:1]
            nxt = [(order[self.at], plan[self.at]) for order, plan in self.lanes]
        values = fold(self.own, kept, self.got, self.extra, nxt, self.end, self.name)
        if self.extra is not None:
            self.extra = values[-1]
            values = values[:-1]
        if nxt is not None:
            self.both = values
        else:
            self.values = values
        return values[0]

    def run(self):
        while self.open:
            self.finish()
            if self.at < self.steps:
                self.begin()
        return self.values


def stats(values):
    average = jnp.mean(values, axis=-1, keepdims=True)
    centred = values - average
    spread = jnp.mean(centred * centred, axis=-1, keepdims=True)
    inverse = lax.rsqrt(spread + EPS)
    return centred * inverse, inverse


def pull(hat, inverse, grad, gain):
    scaled = grad * gain
    first = jnp.mean(scaled, axis=-1, keepdims=True)
    second = jnp.mean(scaled * hat, axis=-1, keepdims=True)
    return inverse * (scaled - first - hat * second)


def gelu_parts(values):
    cdf = 0.5 + 0.5 * lax.erf(values * (1.0 / math.sqrt(2.0)))
    density = jnp.exp(-0.5 * values * values) * (1.0 / math.sqrt(2.0 * math.pi))
    return values * cdf, cdf + values * density


def dot(a, b, dims=((1,), (0,))):
    return lax.dot_general(a, b, (dims, ((), ())), preferred_element_type=F32)


NT = ((1,), (1,))
TN = ((0,), (0,))


def low_lanes(shape):
    return lax.broadcasted_iota(jnp.int32, shape, len(shape) - 1) < LANES // 2


def live_rows(counts_ref, rows, per_slot):
    row = lax.broadcasted_iota(jnp.int32, (rows, 1), 0)
    live = jnp.zeros((rows, 1), F32)
    for sample in range(rows // (per_slot * SLOTS_PER)):
        start = sample * SLOTS_PER * per_slot
        inside = jnp.logical_and(row >= start, row < start + counts_ref[sample] * per_slot)
        live = jnp.where(inside, 1.0, live)
    return live


def paired(block):
    low = low_lanes(block.shape)
    zero = jnp.zeros_like(block)
    return jnp.concatenate([jnp.where(low, block, zero), jnp.where(low, zero, block)], axis=0)


def unpaired(block):
    half = block.shape[0] // 2
    return jnp.where(low_lanes((half, block.shape[1])), block[:half], block[half:])


def flipped(values):
    a, b = values.shape
    tall, wide = -a % LANES, -b % LANES
    if wide:
        values = jnp.concatenate([values, jnp.zeros((a, wide), F32)], axis=1)
    if tall:
        values = jnp.concatenate([values, jnp.zeros((tall, b + wide), F32)], axis=0)
    return values.T[:b, :a]


def call(kernel, grid, ins, outs, scratch=(), vmem=40, prefetch=0, name=None):
    return pl.pallas_call(
        kernel,
        grid_spec=pltpu.PrefetchScalarGridSpec(
            num_scalar_prefetch=prefetch,
            grid=grid,
            in_specs=ins,
            out_specs=[spec for spec, _ in outs],
            scratch_shapes=list(scratch),
        ),
        out_shape=[shape for _, shape in outs],
        compiler_params=pltpu.CompilerParams(
            vmem_limit_bytes=vmem * MIB, dimension_semantics=("arbitrary",) * len(grid)
        ),
        cost_estimate=pl.CostEstimate(flops=int(TIMES.get(name, 0.8) * RATE), bytes_accessed=100000, transcendentals=0),
        name=name,
    )


def whole(shape):
    zeros = (0,) * len(shape)
    return pl.BlockSpec(tuple(shape), lambda *_: zeros)


def leading(shape):
    zeros = (0,) * (len(shape) - 1)
    return pl.BlockSpec(tuple(shape), lambda g, *_: (g,) + zeros)


def out(shape, dtype):
    return jax.ShapeDtypeStruct(tuple(shape), dtype)


SMEM = pl.BlockSpec(memory_space=pltpu.SMEM)


def packed(values):
    high = values.astype(BF16)
    left = values - high.astype(F32)
    middle = left.astype(BF16)
    small = left - middle.astype(F32)
    top = jnp.concatenate([high.astype(F32), middle.astype(F32)], axis=1)
    bottom = jnp.concatenate([small, jnp.zeros_like(small)], axis=1)
    return jnp.concatenate([top, bottom], axis=0).astype(BF16)


def unpacked(values):
    values = values.astype(F32)
    n, m = values.shape[0] // 2, values.shape[1] // 2
    return values[:n, :m] + values[:n, m:] + values[n:, :m]


def latent_kernel(per_slot, counts, lat, grad, gain, bias, w_query, lat_low, q_low, dy):
    hat, _ = stats(lat[...].astype(F32))
    low = (hat * gain[1:2] + bias[1:2]).astype(BF16)
    lat_low[...] = low
    q_low[...] = dot(low, w_query[...]).astype(BF16)
    live = live_rows(counts, lat.shape[0], per_slot)
    dy[...] = (live * grad[...].astype(F32)).astype(BF16)


def media_kernel(media, lat_low, gain, bias, w_keyval, key_input, keyval):
    n, rows, width = media.shape
    hat, _ = stats(media[...].reshape(n * rows, width).astype(F32))
    low = (hat * gain[0:1] + bias[0:1]).astype(BF16)
    key_input[:, :rows, :] = low.reshape(n, rows, width)
    key_input[:, rows:, :] = lat_low[...].reshape(n, -1, width)
    every = key_input[...].reshape(-1, width)
    keyval[...] = dot(every, w_keyval[...]).astype(BF16).reshape(keyval.shape)


def attend_kernel(peers, per_slot, scale, *refs):
    qs, kv, parts, held = refs[:peers], refs[peers], refs[peers + 1 : 2 * peers + 1], refs[2 * peers + 1]
    n, keys, inner = kv.shape[0], kv.shape[1], kv.shape[2] // 2
    step = pl.program_id(0)
    items = [(s, t) for s in range(n) for t in range(inner // LANES)]
    cuts = [slice(t * LANES, (t + 1) * LANES) for t in range(2 * inner // LANES)]
    rows = [pl.multiple_of((step * n + s) * per_slot, per_slot) for s in range(n)]
    ones = jnp.ones((keys, LANES), BF16)

    @pl.when(step == 0)
    def _():
        held[...] = jnp.zeros_like(held)

    scores = []
    for s, t in items:
        q = paired(jnp.concatenate([ref[pl.ds(rows[s], per_slot), cuts[t]] for ref in qs], axis=0))
        scores.append(dot(q, kv[s, :, cuts[t]], NT) * scale)
    tops = [jnp.max(score, axis=-1, keepdims=True) for score in scores]
    probs = [jnp.exp(score - top).astype(BF16) for score, top in zip(scores, tops)]
    sums = [
        dot(prob, jnp.concatenate([kv[s, :, cuts[inner // LANES + t]], ones], axis=1))
        for prob, (s, t) in zip(probs, items)
    ]
    lane = lax.broadcasted_iota(jnp.int32, (peers * per_slot, LANES), 1)
    logs = [jnp.zeros((peers * per_slot, LANES), F32) for _ in range(n)]
    for (s, t), both, top in zip(items, sums, tops):
        total = unpaired(both[:, LANES:])
        o = (unpaired(both[:, :LANES]) / total).astype(BF16)
        lse = unpaired(jnp.broadcast_to(top, (top.shape[0], LANES))) + jnp.log(total)
        here = jnp.logical_or(lane == t, lane == LANES // 2 + HEADS // 2 + t)
        logs[s] = jnp.where(here, lse, logs[s])
        for i in range(peers):
            parts[i][pl.ds(rows[s], per_slot), cuts[t]] = o[i * per_slot : (i + 1) * per_slot]
    for s in range(n):
        for i in range(peers):
            held[i, pl.ds(rows[s], per_slot), :] = logs[s][i * per_slot : (i + 1) * per_slot]

    @pl.when(step == pl.num_programs(0) - 1)
    def _():
        for i in range(peers):
            turned = held[i].T
            turned = turned[:HEADS] + turned[LANES // 2 : LANES // 2 + HEADS]
            parts[i][-2 * HEADS :, :] = packed(turned)


def mix_kernel(peers, *refs):
    parts = refs[:peers]
    lat, w_out, gain, bias, attended, att_low, hidden, ff_low, lse_out = refs[peers:]
    rows, inner = attended.shape
    logs = [unpacked(ref[rows:, :]) for ref in parts]
    top = functools.reduce(jnp.maximum, logs)
    lse = top + jnp.log(sum(jnp.exp(v - top) for v in logs))
    lse_out[...] = lse
    weights = flipped(jnp.concatenate([jnp.exp(v - lse) for v in logs], axis=0))[:rows]
    low = low_lanes((rows, LANES))
    for t in range(inner // LANES):
        cut = slice(t * LANES, (t + 1) * LANES)
        total = jnp.zeros((rows, LANES), F32)
        for j in range(peers):
            at = j * HEADS + t
            other = at + HEADS // 2
            weight = jnp.where(low, weights[:, at : at + 1], weights[:, other : other + 1])
            total = total + weight * parts[j][:rows, cut].astype(F32)
        attended[:, cut] = total
        att_low[:, cut] = total.astype(BF16)
    state = lat[...].astype(F32) + dot(att_low[...], w_out[...])
    hidden[...] = state
    hat, _ = stats(state)
    ff_low[...] = (hat * gain[2:3] + bias[2:3]).astype(BF16)


def feed_columns(ff_low, dy, ups, downs, acts, dpres, res, dff):
    half = len(ups) // 2
    a = pl.program_id(1)
    parts = []
    for at in (slice(0, half), slice(half, 2 * half)):
        up = jnp.concatenate([ref[...] for ref in ups[at]], axis=1)
        down = jnp.concatenate([ref[...] for ref in downs[at]], axis=0)
        parts.append((up, down, dot(ff_low[...], up), dot(dy[...], down, NT)))
    done = []
    for up, down, pre, dact in parts:
        value, slope = gelu_parts(pre)
        value = value.astype(BF16)
        back = (slope * dact).astype(BF16)
        res[...] += dot(value, down)
        dff[...] += dot(back, up, NT)
        done.append((value, back))
    for at, (act, dpre) in enumerate(zip(acts, dpres)):

        @pl.when(pl.program_id(0) == at)
        def _():
            width = done[0][0].shape[1]
            for k, (value, back) in enumerate(done):
                act[a, :, k * width : (k + 1) * width] = value
                dpre[a, :, k * width : (k + 1) * width] = back


def first_step():
    return jnp.logical_and(pl.program_id(0) == 0, pl.program_id(1) == 0)


def last_step():
    ends = [pl.program_id(k) == pl.num_programs(k) - 1 for k in range(2)]
    return jnp.logical_and(*ends)


def feed_kernel(count, here, own, ff_low, dy, *refs):
    ups, downs, refs = refs[:count], refs[count : 2 * count], refs[2 * count :]
    acts, dpres, (res, dff) = refs[:here], refs[here : 2 * here], refs[2 * here :]

    @pl.when(first_step())
    def _():
        res[...] = jnp.zeros_like(res)
        dff[...] = jnp.zeros_like(dff)

    feed_columns(ff_low, dy, ups, downs, acts, dpres, res, dff)


def feed_end_kernel(per_slot, count, here, own, counts, ff_low, dy, *refs):
    ups, downs, refs = refs[:count], refs[count : 2 * count], refs[2 * count :]
    res_in, dff_in, hidden, attended, lse, w_out, gain = refs[:7]
    acts, dpres, refs = refs[7 : 7 + here], refs[7 + here : 7 + 2 * here], refs[7 + 2 * here :]
    result, dhidden, dhid_low, datt_low, sums, res, dff = refs

    @pl.when(first_step())
    def _():
        res[...] = res_in[...]
        dff[...] = dff_in[...]

    feed_columns(ff_low, dy, ups, downs, acts, dpres, res, dff)

    @pl.when(last_step())
    def _():
        rows, inner = attended.shape
        live = live_rows(counts, rows, per_slot)
        state = hidden[...]
        result[...] = (live * (state + res[...])).astype(BF16)
        hat, inverse = stats(state)
        grad = dff[...]
        sums[0:1] = jnp.sum(grad * hat, axis=0, keepdims=True)
        sums[1:2] = jnp.sum(grad, axis=0, keepdims=True)
        back = dy[...].astype(F32) + pull(hat, inverse, grad, gain[2:3])
        dhidden[...] = back
        dhid_low[...] = back.astype(BF16)
        datt = dot(dhid_low[...], w_out[...], NT).astype(BF16)
        datt_low[:rows, :] = datt
        product = datt.astype(F32) * attended[...]
        low = low_lanes((rows, LANES))
        lane = lax.broadcasted_iota(jnp.int32, (rows, LANES), 1)
        delta = jnp.zeros((rows, LANES), F32)
        for t in range(inner // LANES):
            both = product[:, t * LANES : (t + 1) * LANES]
            first = jnp.sum(jnp.where(low, both, 0.0), axis=-1, keepdims=True)
            second = jnp.sum(jnp.where(low, 0.0, both), axis=-1, keepdims=True)
            delta = jnp.where(lane == t, first, delta)
            delta = jnp.where(lane == HEADS // 2 + t, second, delta)
        turned = flipped(jnp.concatenate([delta, jnp.zeros((-rows % LANES, LANES), F32)], axis=0))
        datt_low[rows:, :] = packed(jnp.concatenate([lse[...], turned[:HEADS]], axis=0))


def attend_back_kernel(peers, per_slot, scale, *refs):
    qs, das, kv, dkv = refs[:peers], refs[peers : 2 * peers], refs[2 * peers], refs[2 * peers + 1]
    (near, cross), held = refs[2 * peers + 2 : 2 * peers + 4], refs[2 * peers + 4]
    dqs = [(cross if i % 2 else near, i // 2) for i in range(peers)]
    n, inner = kv.shape[0], kv.shape[2] // 2
    step = pl.program_id(0)
    items = [(s, t) for s in range(n) for t in range(inner // LANES)]
    cuts = [slice(t * LANES, (t + 1) * LANES) for t in range(2 * inner // LANES)]
    rows = [pl.multiple_of((step * n + s) * per_slot, per_slot) for s in range(n)]
    later = inner // LANES

    @pl.when(step == 0)
    def _():
        for i in range(peers):
            turned = unpacked(das[i][-4 * HEADS :, :])
            held[i, :, : 2 * HEADS] = flipped(turned)

    def column(block, h):
        other = h + HEADS // 2
        return jnp.concatenate([block[:, h : h + 1], block[:, other : other + 1]], axis=0)

    sts = [
        jnp.concatenate([held[i, pl.ds(row, per_slot), :] for i in range(peers)], axis=0) for row in rows
    ]
    qp = [paired(jnp.concatenate([ref[pl.ds(rows[s], per_slot), cuts[t]] for ref in qs], axis=0)) for s, t in items]
    dp = [paired(jnp.concatenate([ref[pl.ds(rows[s], per_slot), cuts[t]] for ref in das], axis=0)) for s, t in items]
    scores = [dot(q, kv[s, :, cuts[t]], NT) for q, (s, t) in zip(qp, items)]
    dprobs = [dot(d, kv[s, :, cuts[later + t]], NT) for d, (s, t) in zip(dp, items)]
    probs = [jnp.exp(score * scale - column(sts[s], t)) for score, (s, t) in zip(scores, items)]
    dscores = [
        (prob * (dprob - column(sts[s], HEADS + t))).astype(BF16)
        for prob, dprob, (s, t) in zip(probs, dprobs, items)
    ]
    for (s, t), prob, d in zip(items, probs, dp):
        dkv[s, :, cuts[later + t]] = dot(prob.astype(BF16), d, TN).astype(BF16)
    for (s, t), ds, q in zip(items, dscores, qp):
        dkv[s, :, cuts[t]] = (dot(ds, q, TN) * scale).astype(BF16)
    for (s, t), ds in zip(items, dscores):
        dq = (unpaired(dot(ds, kv[s, :, cuts[t]])) * scale).astype(BF16)
        for i in range(peers):
            ref, at = dqs[i]
            ref[at, pl.ds(rows[s], per_slot), cuts[t]] = dq[i * per_slot : (i + 1) * per_slot]


def pair_kernel(near, other, mine, sent):
    total = near[...].astype(F32) + other[...].astype(F32)
    mine[...] = total[0].astype(BF16)
    sent[...] = total[1].astype(BF16)


def keyval_back_kernel(media, dkv, w_keyval, gain, media_grad, dlat, sums):
    n, rows, width = media.shape
    grad = dot(dkv[...].reshape(-1, dkv.shape[2]), w_keyval[...], NT).reshape(n, -1, width)
    dlat[...] = grad[:, rows:].reshape(dlat.shape)
    grad = grad[:, :rows].reshape(n * rows, width)
    hat, inverse = stats(media[...].reshape(n * rows, width).astype(F32))
    media_grad[...] = pull(hat, inverse, grad, gain[0:1]).astype(BF16).reshape(media_grad.shape)

    @pl.when(pl.program_id(0) == 0)
    def _():
        sums[...] = jnp.zeros_like(sums)

    sums[0:1] += jnp.sum(grad * hat, axis=0, keepdims=True)
    sums[1:2] += jnp.sum(grad, axis=0, keepdims=True)


def latent_back_kernel(peers, *refs):
    dqs = refs[:peers]
    dlat, lat, dhidden, w_query, gain, sums_media, sums_ff, dq_low, latent_grad, sums = refs[peers:]
    dq = sum(ref[...].astype(F32) for ref in dqs).astype(BF16)
    dq_low[...] = dq
    grad = dlat[...] + dot(dq, w_query[...], NT)
    hat, inverse = stats(lat[...].astype(F32))
    latent_grad[...] = (dhidden[...] + pull(hat, inverse, grad, gain[1:2])).astype(BF16)
    sums[0:1] = sums_media[0:1]
    sums[1:2] = jnp.sum(grad * hat, axis=0, keepdims=True)
    sums[2:3] = sums_ff[0:1]
    sums[3:4] = sums_media[1:2]
    sums[4:5] = jnp.sum(grad, axis=0, keepdims=True)
    sums[5:6] = sums_ff[1:2]


def halved(values):
    high = values.astype(BF16).astype(F32)
    return jnp.concatenate([high, values - high], axis=0).astype(BF16)


def joined(values):
    values = values.astype(F32)
    half = values.shape[0] // 2
    return values[:half] + values[half:]


def outer_kernel(count, lanes, own, *refs):
    lefts, rights, refs = refs[:count], refs[count : 2 * count], refs[2 * count :]
    results, held = refs[:-1], refs[-1]

    @pl.when(pl.program_id(0) == 0)
    def _():
        at = 0
        for ref in rights:
            rows, width = ref.shape[-2:]
            for k in range(held.shape[1] // width):
                held[at : at + rows, k * width : (k + 1) * width] = ref[k] if len(ref.shape) == 3 else ref[...]
            at += rows

    left = jnp.concatenate([ref[...].reshape(-1, ref.shape[-1]) for ref in lefts], axis=0)
    product = dot(left, held[...], TN)
    width = product.shape[1] // len(lanes)
    for k, (bit, inner) in enumerate(lanes):
        kept, sent = parted(product[:, k * width : (k + 1) * width], inner, chosen(own, bit))
        results[2 * k][...] = kept.astype(BF16)
        results[2 * k + 1][...] = sent.astype(BF16)


def outer(own, lefts, rights, tile, lanes, name):
    count = len(lefts)
    wide = lambda v: v.shape[-1] * (v.shape[0] if v.ndim == 3 else 1)
    a, b = wide(lefts[0]), wide(rights[0])

    def left_spec(v):
        if v.ndim == 3:
            return pl.BlockSpec((1, v.shape[1], tile), lambda g, *_: (g, 0, 0))
        return pl.BlockSpec((v.shape[0], tile), lambda g, *_: (0, g))

    total = sum(v.shape[-2] for v in rights)
    steps, part = a // tile, b // len(lanes)
    spec = pl.BlockSpec((tile // 2, part), lambda g, *_: (g, 0))
    return call(
        functools.partial(outer_kernel, count, [(order[0], plan[0]) for order, plan in lanes]),
        (steps,),
        [left_spec(v) for v in lefts] + [whole(v.shape) for v in rights],
        [(spec, out((a // 2, part), BF16))] * (2 * len(lanes)),
        scratch=[pltpu.VMEM((total, b), BF16)],
        prefetch=1, name=name,
    )(own, *lefts, *rights)


def query_kernel(bit, rows, own, dq, lat_low, out_t, sums, kept, sent):
    width = lat_low.shape[1]
    which = chosen(own, bit)
    other_rows = out_t.shape[1]
    product = dot(dq[...], lat_low[...], TN)
    first = parted(product, rows, which)
    second = parted(out_t[...].astype(F32).reshape(-1, width), other_rows, which)
    both = [
        jnp.concatenate([a.reshape(-1, rows, width), b.reshape(-1, other_rows, width)], axis=1).reshape(-1, width)
        for a, b in zip(first, second)
    ]
    head = 2 * sums.shape[0]
    kept[...] = both[0].astype(BF16)
    sent[:head, :] = halved(sums[...])
    sent[head:, :] = both[1].astype(BF16)


def side_by_side_kernel(rows, left, right, result):
    product = dot(left[...], right[...], TN).astype(BF16)
    split = product.reshape(-1, 2, rows, product.shape[1])
    result[...] = jnp.concatenate([split[:, 0], split[:, 1]], axis=-1)


def fold_kernel(nxt, end, lanes, extra, own, *refs):
    kept, got, refs = refs[:lanes], refs[lanes : 2 * lanes], refs[2 * lanes :]
    head = 0
    if extra:
        more, refs = refs[0], refs[1:]
        head = 2 * more.shape[0]
        small = more[...] + joined(got[0][:head, :])
        refs[-1][...] = small
    totals = [a[...].astype(F32) + b[head:, :].astype(F32) for a, b in zip(kept, got)]
    if nxt is None:
        for ref, values in zip(refs, end(*totals)):
            ref[...] = values.astype(ref.dtype)
        return
    if len(nxt) < len(totals):
        totals = [jnp.concatenate(totals, axis=1)]
    for k, (total, (bit, inner)) in enumerate(zip(totals, nxt)):
        keep, send = parted(total, inner, chosen(own, bit))
        refs[2 * k][...] = keep.astype(BF16)
        refs[2 * k + 1][head:, :] = send.astype(BF16)
    if extra:
        refs[1][:head, :] = halved(small)


def fold(own, kept, got, extra, nxt, end, name):
    ins = list(kept) + list(got)
    if nxt is not None:
        head = 0 if extra is None else 2 * extra.shape[0]
        shapes = []
        for _ in nxt:
            rows, width = kept[0].shape[0], kept[0].shape[1] * len(kept) // len(nxt)
            shapes += [out((rows // 2, width), BF16), out((head + rows // 2, width), BF16)]
    else:
        shapes = list(jax.eval_shape(end, *(out(v.shape, F32) for v in kept)))
    if extra is not None:
        ins.append(extra)
        shapes.append(out(extra.shape, F32))
    return call(
        functools.partial(fold_kernel, nxt, end, len(kept), extra is not None),
        (1,),
        [whole(v.shape) for v in ins],
        [(whole(s.shape), s) for s in shapes],
        prefetch=1, name=name,
    )(own, *ins)


def place_kernel(block, parts, result):
    peers, _, width = parts.shape
    for p in range(peers):
        for k in range(width // block):
            at = (k * peers + p) * block
            result[:, at : at + block] = parts[p, :, k * block : (k + 1) * block].astype(F32)


def on_device(
    media, latents, counts, gains, biases, w_query, w_keyval, w_out, w_up, w_down, out_grad
):
    slots, patch_rows, width = media.shape
    per_slot = latents.shape[1]
    inner = w_query.shape[1]
    ff = w_up.shape[1]
    n_img, peers = lax.axis_size("img"), lax.axis_size("patch")
    shards = n_img * peers
    scale = 1.0 / math.sqrt(inner // HEADS)
    rows = slots * per_slot
    keys = patch_rows + per_slot
    padded = -(-rows // LANES) * LANES
    gain_spec = whole(gains.shape)
    lat = latents.reshape(rows, width)

    own = jnp.stack([lax.axis_index("patch"), lax.axis_index("img")]).astype(jnp.int32)
    fine = width // shards % 16 == 0 and inner // shards % 16 == 0
    lat_low, q_low, dy = call(
        functools.partial(latent_kernel, per_slot),
        (1,),
        [SMEM, whole((rows, width)), whole((rows, width)), gain_spec, gain_spec, whole(w_query.shape)],
        [
            (whole((rows, width)), out((rows, width), BF16)),
            (whole((rows, inner)), out((rows, inner), BF16)),
            (whole((rows, width)), out((rows, width), BF16)),
        ],
        vmem=62, name="latent",
    )(counts, lat, out_grad.reshape(rows, width), gains, biases, w_query)
    qs = {0: q_low}
    bit = peers // 2
    qs[bit] = swap(q_low, "patch", bit)

    group = slots // 2
    key_input, keyval = call(
        media_kernel,
        (slots // group,),
        [
            leading((group, patch_rows, width)), leading((group * per_slot, width)),
            gain_spec, gain_spec, whole(w_keyval.shape),
        ],
        [
            (leading((group, keys, width)), out((slots, keys, width), BF16)),
            (leading((group, keys, 2 * inner)), out((slots, keys, 2 * inner), BF16)),
        ],
        name="media",
    )(media, lat_low, gains, biases, w_keyval)
    first = after(qs[bit], keyval)
    qs[bit] = first
    while bit > 1:
        bit //= 2
        for j in list(qs):
            qs[j ^ bit] = swap(qs[j], "patch", bit)
    qs = [qs[j] for j in range(peers)]

    pair = 2
    kv_block = leading((pair, keys, 2 * inner))
    part_rows = rows + 2 * HEADS
    stat_out = (whole((HEADS, padded)), out((HEADS, padded), F32))
    parts = call(
        functools.partial(attend_kernel, peers, per_slot, scale),
        (slots // pair,),
        [whole((rows, inner))] * peers + [kv_block],
        [(whole((part_rows, inner)), out((part_rows, inner), BF16))] * peers,
        scratch=[pltpu.VMEM((peers, padded, LANES), F32)],
        name="attend",
    )(*qs, keyval)
    parts = [parts[0]] + [swap(parts[j], "patch", j) for j in range(1, peers)]
    dys = {0: dy, peers // 2: swap(after(dy, *parts[1:]), "patch", peers // 2)}

    attended, att_low, hidden, ff_low, lse = call(
        functools.partial(mix_kernel, peers),
        (1,),
        [whole((part_rows, inner))] * peers
        + [whole((rows, width)), whole(w_out.shape), gain_spec, gain_spec],
        [
            (whole((rows, inner)), out((rows, inner), F32)),
            (whole((rows, inner)), out((rows, inner), BF16)),
            (whole((rows, width)), out((rows, width), F32)),
            (whole((rows, width)), out((rows, width), BF16)),
            stat_out,
        ],
        vmem=62, name="mix",
    )(*parts, lat, w_out, gains, biases)
    bit = peers // 2
    ffs = {0: ff_low, bit: swap(ff_low, "patch", bit)}

    halves = 2
    blocks = ff // (peers * halves * LANES)
    chunk = ff // shards
    strided = chunk % LANES == 0

    def column(own, j, a, k):
        p, k = own[0] ^ j, a * blocks + k
        if strided:
            return ((k // (chunk // LANES)) * peers + p) * (chunk // LANES) + k % (chunk // LANES)
        return p * halves * blocks + k

    def weights(first, stride):
        ups = [
            pl.BlockSpec((width, LANES), lambda g, a, own, k=k: (0, column(own, first + stride * g, a, k)))
            for k in range(blocks)
        ]
        downs = [
            pl.BlockSpec((LANES, width), lambda g, a, own, k=k: (column(own, first + stride * g, a, k), 0))
            for k in range(blocks)
        ]
        return ups + downs

    part = ff // (peers * halves)
    here = peers // 2
    columns = (whole((halves, rows, part)), out((halves, rows, part), BF16))
    wide_low = (whole((rows, width)), out((rows, width), BF16))
    wide = (whole((rows, width)), out((rows, width), F32))
    count = blocks
    far = call(
        functools.partial(feed_kernel, count, here),
        (here, halves),
        [whole((rows, width))] * 2 + weights(here, 1),
        [columns] * (2 * here) + [wide, wide],
        vmem=62, prefetch=1, name="feed",
    )(own, ff_low, dy, *([w_up] * count), *([w_down] * count))
    dys = spread({0: after(dy, ff_low), bit: after(dys[bit], far[-1])})
    ffs[peers // 2] = after(ffs[peers // 2], dys[bit])
    ffs = spread(ffs)

    def cross(values):
        return [swap(v, "patch", here + k) for k, v in enumerate(values)]

    act_cross = cross(after(tuple(far[:here]), ffs[peers // 2]))
    near = call(
        functools.partial(feed_end_kernel, per_slot, count, here),
        (here, halves),
        [SMEM] + [whole((rows, width))] * 2 + weights(here - 1, -1)
        + [whole((rows, width))] * 3 + [whole((rows, inner)), whole((HEADS, padded)), whole(w_out.shape), gain_spec],
        [columns] * (2 * here)
        + [wide_low, wide, wide_low]
        + [(whole((rows + 4 * HEADS, inner)), out((rows + 4 * HEADS, inner), BF16)), (whole((2, width)), out((2, width), F32))],
        scratch=[pltpu.VMEM((rows, width), F32), pltpu.VMEM((rows, width), F32)],
        vmem=62, prefetch=1, name="feed_end",
    )(own, counts, after(ff_low, *ffs[1:], *dys[1:]), dy, *([w_up] * count), *([w_down] * count),
      far[2 * here], far[2 * here + 1], hidden, attended, lse, w_out, gains)
    result, dhidden, dhid_low, datt_low, sums_ff = near[2 * here :]
    act_near, dpre_near = list(reversed(near[:here])), list(reversed(near[here : 2 * here]))

    das = {0: datt_low, peers // 2: swap(datt_low, "patch", peers // 2)}
    out_rows = width // shards // 2
    q_rows = inner // shards
    every, ff_bits = digits_of("img") + digits_of("patch"), digits_of("img")
    ff_orders = [ff_bits[::-1], ff_bits[-2:] + ff_bits[:-2][::-1]]
    named = {"c": ("patch", 1), "x": ("patch", 2), "y": ("img", 1), "z": ("img", 2)}

    def order_of(letters):
        head = [named[k] for k in letters]
        return head + [bit for bit in reversed(every) if bit not in head]

    def ff_lanes(rows):
        return [(order, plan_of(rows, ff_bits, order)) for order in ff_orders]

    def near_swaps(values):
        return [values[0]] + [swap(values[j], "patch", j) for j in range(1, here)]

    kv_order, qo_order = order_of(KV_ORDER), order_of(QO_ORDER)
    acts = near_swaps(act_near) + act_cross
    dpre_first = near_swaps(dpre_near)
    got, sums_of = {}, {}

    def out_grad(mark):
        got["out_t"] = call(
            functools.partial(side_by_side_kernel, out_rows),
            (2,),
            [pl.BlockSpec((rows, width // 2), lambda g: (0, g)), whole((rows, inner))],
            [(leading((shards // 2, out_rows, 2 * inner)), out((shards, out_rows, 2 * inner), BF16))],
            name="out_grad",
        )(after(dhid_low, mark), att_low)[0]
        return got["out_t"]

    def begun(letter, scatter):
        sums_of[letter] = scatter
        mark = scatter.both[0]
        scatter.begin()
        return mark

    def down_grad(mark):
        lanes = ff_lanes(width)
        both = outer(own, dys[:-1] + [after(dys[-1], mark)], acts, width // 2, lanes, "down_grad")
        return begun("D", Scatter(own, both, lanes, lambda t: [t.astype(BF16)], name="down_fold"))

    def send_dpre(mark):
        got["dpres"] = dpre_first + cross(after(tuple(far[here : 2 * here]), mark))
        return mark

    def attend_back(mark):
        near_das = spread({0: das[0], peers // 2: after(das[peers // 2], mark)})
        values = call(
            functools.partial(attend_back_kernel, peers, per_slot, scale),
            (slots // pair,),
            [whole((rows, inner))] * peers + [whole((rows + 4 * HEADS, inner))] * peers + [kv_block],
            [(kv_block, out(keyval.shape, BF16))]
            + [(whole((here, rows, inner)), out((here, rows, inner), BF16))] * 2,
            scratch=[pltpu.VMEM((peers, padded, LANES), F32)],
            name="attend_back",
        )(*qs, *near_das, keyval)
        got["dkv"], near_dq, cross_dq = values
        got["pair"] = (near_dq, swap(cross_dq, "patch", 1))
        return got["dkv"]

    def pair_dq(mark):
        near_dq, other = got["pair"]
        mine, sent = call(
            pair_kernel,
            (1,),
            [whole(near_dq.shape)] * 2,
            [(whole((rows, inner)), out((rows, inner), BF16))] * 2,
            name="pair",
        )(after(near_dq, mark), other)
        got["dqs"] = [mine, swap(sent, "patch", here)]
        return mine

    def keyval_back(mark):
        got["media_grad"], got["dlat"], got["sums_media"] = call(
            keyval_back_kernel,
            (slots // group,),
            [
                leading((group, patch_rows, width)), leading((group, keys, 2 * inner)),
                whole(w_keyval.shape), gain_spec,
            ],
            [
                (leading((group, patch_rows, width)), out(media.shape, BF16)),
                (leading((group * per_slot, width)), out((rows, width), F32)),
                (whole((2, width)), out((2, width), F32)),
            ],
            name="keyval_back",
        )(media, after(got["dkv"], mark), w_keyval, gains)
        return got["sums_media"]

    def keyval_grad(mark):
        lanes = [(kv_order, plan_of(2 * inner, every, kv_order))]
        both = outer(
            own, [after(got["dkv"], mark).reshape(-1, 2 * inner)], [key_input.reshape(-1, width)], 2 * inner // 4,
            lanes, "keyval_grad",
        )
        return begun("K", Scatter(own, both, lanes, lambda t: [t], name="keyval_fold"))

    def up_grad(mark):
        lanes, dpres = ff_lanes(halves * part), got["dpres"]
        both = outer(own, dpres[:-1] + [after(dpres[-1], mark)], ffs, part, lanes, "up_grad")
        end = lambda t: [flipped(t)] if strided else [t.astype(BF16)]
        return begun("U", Scatter(own, both, lanes, end, name="up_fold"))

    def latent_back(mark):
        got["dq_low"], got["latent_grad"], got["sums"] = call(
            functools.partial(latent_back_kernel, here),
            (1,),
            [whole((rows, inner))] * here
            + [whole((rows, width))] * 3 + [whole(w_query.shape), gain_spec, whole((2, width)), whole((2, width))],
            [
                (whole((rows, inner)), out((rows, inner), BF16)),
                (whole((rows, width)), out((rows, width), BF16)),
                (whole((HEADS, width)), out((HEADS, width), F32)),
            ],
            name="latent_back",
        )(*got["dqs"], after(got["dlat"], mark), lat, dhidden, w_query, gains, got["sums_media"], sums_ff)
        return got["dq_low"]

    def open_rows(total):
        other = total[q_rows:]
        return [total[:q_rows], jnp.concatenate([other[:, :inner], other[:, inner:]], axis=0)]

    def query_grad(mark):
        q_plan, qo_plan = plan_of(inner, every, qo_order), plan_of(2 * inner, every, qo_order)
        sums = got["sums"]
        tall = 2 * sums.shape[0] + inner
        ins = (after(got["dq_low"], mark), lat_low, got["out_t"], sums)
        both = call(
            functools.partial(query_kernel, qo_order[0], q_plan[0]),
            (1,),
            [whole(v.shape) for v in ins],
            [(whole((inner, width)), out((inner, width), BF16)), (whole((tall, width)), out((tall, width), BF16))],
            prefetch=1, name="query_grad",
        )(own, *ins)
        return begun("Q", Scatter(own, both, [(qo_order, qo_plan)], open_rows, extra=sums, name="query_fold"))

    tasks = dict(
        O=out_grad, G=down_grad, X=send_dpre, B=attend_back, Y=pair_dq, V=keyval_back, W=keyval_grad, P=up_grad, L=latent_back,
        R=query_grad,
    )
    mark = datt_low
    for letter in ORDER:
        if letter in tasks:
            mark = tasks[letter](mark)
        else:
            one = sums_of[letter]
            mark = one.finish(mark)
            if one.at < one.steps:
                one.begin()
    media_grad, latent_grad = got["media_grad"], got["latent_grad"]
    qo_sum = sums_of["Q"]
    (up_sum,), (kv_sum,), (down,), (q_sum, out_sum) = (sums_of[k].run() for k in "UKDQ")
    small = lax.dynamic_slice_in_dim(
        qo_sum.extra, (own[1] * peers + own[0]) * (width // shards), width // shards, axis=1
    )
    if not strided:
        pairs = [((b % n_img) * peers + b // n_img, b) for b in range(shards)]
        up_sum = lax.ppermute(up_sum, ("img", "patch"), pairs).astype(F32).T

    down = lax.all_to_all(down.reshape(peers, -1, halves * part), "patch", 0, 0, tiled=True)
    down_t = call(
        functools.partial(place_kernel, chunk if strided else halves * part),
        (1,),
        [whole(down.shape)],
        [(whole((width // shards, ff)), out((width // shards, ff), F32))],
        name="down_place",
    )(down)[0]

    return (
        result.reshape(slots, per_slot, width),
        media_grad,
        latent_grad.reshape(slots, per_slot, width),
        q_sum.T,
        kv_sum.T,
        out_sum.T,
        up_sum,
        down_t.T,
        small[:3],
        small[3:6],
    )


def solution(mesh):
    rows = P("img", "patch", None)
    shard = P(None, ("img", "patch"))
    return jax.shard_map(
        on_device,
        mesh=mesh,
        in_specs=(rows, rows, P("img"), P(), P(), P(), P(), P(), P(), P(), rows),
        out_specs=(rows, rows, rows) + (shard,) * 7,
        check_vma=False,
    )
```

```python
import functools
import math

import jax
import jax.numpy as jnp
from jax import lax
from jax.experimental import pallas as pl
from jax.experimental.pallas import tpu as pltpu
from jax.sharding import PartitionSpec as P

HEADS = 8
SLOTS_PER = 5
EPS = 1e-05
LANES = 128
F32 = jnp.float32
BF16 = jnp.bfloat16
MIB = 1024 * 1024
TIMES = dict(latent=2.9, media=2.7, attend=3.1, mix=3.8, feed=0.1, feed_end=36.0, down_grad=4.0, attend_back=1.7, keyval_grad=11.4, up_grad=4.0, keyval_back=4.0, latent_back=1.6, query_grad=1.5, pair=0.8, down_fold=0.8, up_fold=0.8, keyval_fold=0.8, query_fold=1.6, out_grad=0.8)
RATE = 2e+09
ORDER = "OGXBVDWYPKDLRUDUKQQKUQKQKQ"
KV_ORDER, QO_ORDER = "cxyz", "cxyz"


def swap(values, axis, bit):
    n = lax.axis_size(axis)
    return lax.ppermute(values, axis, [(k, k ^ bit) for k in range(n)])


def log2(n):
    return n.bit_length() - 1


def after(values, *others):
    return lax.optimization_barrier((values,) + others)[0]


def spread(blocks):
    n = lax.axis_size("patch")
    blocks = dict(blocks)
    bit = n // 4
    while bit:
        for j in list(blocks):
            blocks[j ^ bit] = swap(blocks[j], "patch", bit)
        bit //= 2
    return [blocks[j] for j in range(n)]


def digits_of(axis):
    n = lax.axis_size(axis)
    return [(axis, 1 << k) for k in reversed(range(log2(n)))]


def chosen(own, bit):
    axis, weight = bit
    return (own[("patch", "img").index(axis)] // weight) % 2


def plan_of(rows, digits, order):
    digits, plan = list(digits), []
    for bit in order:
        at = digits.index(bit)
        plan.append(rows // 2 ** (at + 1))
        del digits[at]
        rows //= 2
    return plan


def parted(values, inner, which):
    width = values.shape[-1]
    split = values.reshape(-1, 2, inner, width)
    low, high = split[:, 0].reshape(-1, width), split[:, 1].reshape(-1, width)
    return jnp.where(which == 1, high, low), jnp.where(which == 1, low, high)


class Scatter:
    def __init__(self, own, both, lanes, end, extra=None, name=None):
        self.own, self.both, self.lanes, self.end = own, both, lanes, end
        self.extra, self.name, self.at, self.open = extra, name, 0, False
        self.steps = len(lanes[0][0])

    def begin(self, *others):
        sent = after(tuple(self.both[1::2]), *others)
        self.got = [swap(v, *order[self.at]) for v, (order, _) in zip(sent, self.lanes)]
        self.at, self.open = self.at + 1, True

    def finish(self, *others):
        kept, self.open = tuple(self.both[::2]), False
        if others:
            kept = after(kept, *others)
        nxt = None
        if self.at < self.steps:
            if all(order[self.at :] == self.lanes[0][0][self.at :] for order, _ in self.lanes):
                self.lanes = self.lanes[:1]
            nxt = [(order[self.at], plan[self.at]) for order, plan in self.lanes]
        values = fold(self.own, kept, self.got, self.extra, nxt, self.end, self.name)
        if self.extra is not None:
            self.extra = values[-1]
            values = values[:-1]
        if nxt is not None:
            self.both = values
        else:
            self.values = values
        return values[0]

    def run(self):
        while self.open:
            self.finish()
            if self.at < self.steps:
                self.begin()
        return self.values


def stats(values):
    average = jnp.mean(values, axis=-1, keepdims=True)
    centred = values - average
    spread = jnp.mean(centred * centred, axis=-1, keepdims=True)
    inverse = lax.rsqrt(spread + EPS)
    return centred * inverse, inverse


def pull(hat, inverse, grad, gain):
    scaled = grad * gain
    first = jnp.mean(scaled, axis=-1, keepdims=True)
    second = jnp.mean(scaled * hat, axis=-1, keepdims=True)
    return inverse * (scaled - first - hat * second)


def gelu_parts(values):
    cdf = 0.5 + 0.5 * lax.erf(values * (1.0 / math.sqrt(2.0)))
    density = jnp.exp(-0.5 * values * values) * (1.0 / math.sqrt(2.0 * math.pi))
    return values * cdf, cdf + values * density


def dot(a, b, dims=((1,), (0,))):
    return lax.dot_general(a, b, (dims, ((), ())), preferred_element_type=F32)


NT = ((1,), (1,))
TN = ((0,), (0,))


def low_lanes(shape):
    return lax.broadcasted_iota(jnp.int32, shape, len(shape) - 1) < LANES // 2


def live_rows(counts_ref, rows, per_slot):
    row = lax.broadcasted_iota(jnp.int32, (rows, 1), 0)
    live = jnp.zeros((rows, 1), F32)
    for sample in range(rows // (per_slot * SLOTS_PER)):
        start = sample * SLOTS_PER * per_slot
        inside = jnp.logical_and(row >= start, row < start + counts_ref[sample] * per_slot)
        live = jnp.where(inside, 1.0, live)
    return live


def paired(block):
    low = low_lanes(block.shape)
    zero = jnp.zeros_like(block)
    return jnp.concatenate([jnp.where(low, block, zero), jnp.where(low, zero, block)], axis=0)


def unpaired(block):
    half = block.shape[0] // 2
    return jnp.where(low_lanes((half, block.shape[1])), block[:half], block[half:])


def flipped(values):
    a, b = values.shape
    tall, wide = -a % LANES, -b % LANES
    if wide:
        values = jnp.concatenate([values, jnp.zeros((a, wide), F32)], axis=1)
    if tall:
        values = jnp.concatenate([values, jnp.zeros((tall, b + wide), F32)], axis=0)
    return values.T[:b, :a]


def call(kernel, grid, ins, outs, scratch=(), vmem=40, prefetch=0, name=None):
    return pl.pallas_call(
        kernel,
        grid_spec=pltpu.PrefetchScalarGridSpec(
            num_scalar_prefetch=prefetch,
            grid=grid,
            in_specs=ins,
            out_specs=[spec for spec, _ in outs],
            scratch_shapes=list(scratch),
        ),
        out_shape=[shape for _, shape in outs],
        compiler_params=pltpu.CompilerParams(
            vmem_limit_bytes=vmem * MIB, dimension_semantics=("arbitrary",) * len(grid)
        ),
        cost_estimate=pl.CostEstimate(flops=int(TIMES.get(name, 0.8) * RATE), bytes_accessed=100000, transcendentals=0),
        name=name,
    )


def whole(shape):
    zeros = (0,) * len(shape)
    return pl.BlockSpec(tuple(shape), lambda *_: zeros)


def leading(shape):
    zeros = (0,) * (len(shape) - 1)
    return pl.BlockSpec(tuple(shape), lambda g, *_: (g,) + zeros)


def out(shape, dtype):
    return jax.ShapeDtypeStruct(tuple(shape), dtype)


SMEM = pl.BlockSpec(memory_space=pltpu.SMEM)


def packed(values):
    high = values.astype(BF16)
    left = values - high.astype(F32)
    middle = left.astype(BF16)
    small = left - middle.astype(F32)
    top = jnp.concatenate([high.astype(F32), middle.astype(F32)], axis=1)
    bottom = jnp.concatenate([small, jnp.zeros_like(small)], axis=1)
    return jnp.concatenate([top, bottom], axis=0).astype(BF16)


def unpacked(values):
    values = values.astype(F32)
    n, m = values.shape[0] // 2, values.shape[1] // 2
    return values[:n, :m] + values[:n, m:] + values[n:, :m]


def latent_kernel(per_slot, counts, lat, grad, gain, bias, w_query, lat_low, q_low, dy):
    hat, _ = stats(lat[...].astype(F32))
    low = (hat * gain[1:2] + bias[1:2]).astype(BF16)
    lat_low[...] = low
    q_low[...] = dot(low, w_query[...]).astype(BF16)
    live = live_rows(counts, lat.shape[0], per_slot)
    dy[...] = (live * grad[...].astype(F32)).astype(BF16)


def media_kernel(media, lat_low, gain, bias, w_keyval, key_input, keyval):
    n, rows, width = media.shape
    hat, _ = stats(media[...].reshape(n * rows, width).astype(F32))
    low = (hat * gain[0:1] + bias[0:1]).astype(BF16)
    key_input[:, :rows, :] = low.reshape(n, rows, width)
    key_input[:, rows:, :] = lat_low[...].reshape(n, -1, width)
    every = key_input[...].reshape(-1, width)
    keyval[...] = dot(every, w_keyval[...]).astype(BF16).reshape(keyval.shape)


def attend_kernel(peers, per_slot, scale, *refs):
    qs, kv, parts, held = refs[:peers], refs[peers], refs[peers + 1 : 2 * peers + 1], refs[2 * peers + 1]
    n, keys, inner = kv.shape[0], kv.shape[1], kv.shape[2] // 2
    step = pl.program_id(0)
    items = [(s, t) for s in range(n) for t in range(inner // LANES)]
    cuts = [slice(t * LANES, (t + 1) * LANES) for t in range(2 * inner // LANES)]
    rows = [pl.multiple_of((step * n + s) * per_slot, per_slot) for s in range(n)]
    ones = jnp.ones((keys, LANES), BF16)

    @pl.when(step == 0)
    def _():
        held[...] = jnp.zeros_like(held)

    scores = []
    for s, t in items:
        q = paired(jnp.concatenate([ref[pl.ds(rows[s], per_slot), cuts[t]] for ref in qs], axis=0))
        scores.append(dot(q, kv[s, :, cuts[t]], NT) * scale)
    tops = [jnp.max(score, axis=-1, keepdims=True) for score in scores]
    probs = [jnp.exp(score - top).astype(BF16) for score, top in zip(scores, tops)]
    sums = [
        dot(prob, jnp.concatenate([kv[s, :, cuts[inner // LANES + t]], ones], axis=1))
        for prob, (s, t) in zip(probs, items)
    ]
    lane = lax.broadcasted_iota(jnp.int32, (peers * per_slot, LANES), 1)
    logs = [jnp.zeros((peers * per_slot, LANES), F32) for _ in range(n)]
    for (s, t), both, top in zip(items, sums, tops):
        total = unpaired(both[:, LANES:])
        o = (unpaired(both[:, :LANES]) / total).astype(BF16)
        lse = unpaired(jnp.broadcast_to(top, (top.shape[0], LANES))) + jnp.log(total)
        here = jnp.logical_or(lane == t, lane == LANES // 2 + HEADS // 2 + t)
        logs[s] = jnp.where(here, lse, logs[s])
        for i in range(peers):
            parts[i][pl.ds(rows[s], per_slot), cuts[t]] = o[i * per_slot : (i + 1) * per_slot]
    for s in range(n):
        for i in range(peers):
            held[i, pl.ds(rows[s], per_slot), :] = logs[s][i * per_slot : (i + 1) * per_slot]

    @pl.when(step == pl.num_programs(0) - 1)
    def _():
        for i in range(peers):
            turned = held[i].T
            turned = turned[:HEADS] + turned[LANES // 2 : LANES // 2 + HEADS]
            parts[i][-2 * HEADS :, :] = packed(turned)


def mix_kernel(peers, *refs):
    parts = refs[:peers]
    lat, w_out, gain, bias, attended, att_low, hidden, ff_low, lse_out = refs[peers:]
    rows, inner = attended.shape
    logs = [unpacked(ref[rows:, :]) for ref in parts]
    top = functools.reduce(jnp.maximum, logs)
    lse = top + jnp.log(sum(jnp.exp(v - top) for v in logs))
    lse_out[...] = lse
    weights = flipped(jnp.concatenate([jnp.exp(v - lse) for v in logs], axis=0))[:rows]
    low = low_lanes((rows, LANES))
    for t in range(inner // LANES):
        cut = slice(t * LANES, (t + 1) * LANES)
        total = jnp.zeros((rows, LANES), F32)
        for j in range(peers):
            at = j * HEADS + t
            other = at + HEADS // 2
            weight = jnp.where(low, weights[:, at : at + 1], weights[:, other : other + 1])
            total = total + weight * parts[j][:rows, cut].astype(F32)
        attended[:, cut] = total
        att_low[:, cut] = total.astype(BF16)
    state = lat[...].astype(F32) + dot(att_low[...], w_out[...])
    hidden[...] = state
    hat, _ = stats(state)
    ff_low[...] = (hat * gain[2:3] + bias[2:3]).astype(BF16)


def feed_columns(ff_low, dy, ups, downs, acts, dpres, res, dff):
    half = len(ups) // 2
    a = pl.program_id(1)
    parts = []
    for at in (slice(0, half), slice(half, 2 * half)):
        up = jnp.concatenate([ref[...] for ref in ups[at]], axis=1)
        down = jnp.concatenate([ref[...] for ref in downs[at]], axis=0)
        parts.append((up, down, dot(ff_low[...], up), dot(dy[...], down, NT)))
    done = []
    for up, down, pre, dact in parts:
        value, slope = gelu_parts(pre)
        value = value.astype(BF16)
        back = (slope * dact).astype(BF16)
        res[...] += dot(value, down)
        dff[...] += dot(back, up, NT)
        done.append((value, back))
    for at, (act, dpre) in enumerate(zip(acts, dpres)):

        @pl.when(pl.program_id(0) == at)
        def _():
            width = done[0][0].shape[1]
            for k, (value, back) in enumerate(done):
                act[a, :, k * width : (k + 1) * width] = value
                dpre[a, :, k * width : (k + 1) * width] = back


def first_step():
    return jnp.logical_and(pl.program_id(0) == 0, pl.program_id(1) == 0)


def last_step():
    ends = [pl.program_id(k) == pl.num_programs(k) - 1 for k in range(2)]
    return jnp.logical_and(*ends)


def feed_kernel(count, here, own, ff_low, dy, *refs):
    ups, downs, refs = refs[:count], refs[count : 2 * count], refs[2 * count :]
    acts, dpres, (res, dff) = refs[:here], refs[here : 2 * here], refs[2 * here :]

    @pl.when(first_step())
    def _():
        res[...] = jnp.zeros_like(res)
        dff[...] = jnp.zeros_like(dff)

    feed_columns(ff_low, dy, ups, downs, acts, dpres, res, dff)


def feed_end_kernel(per_slot, count, here, own, counts, ff_low, dy, *refs):
    ups, downs, refs = refs[:count], refs[count : 2 * count], refs[2 * count :]
    res_in, dff_in, hidden, attended, lse, w_out, gain = refs[:7]
    acts, dpres, refs = refs[7 : 7 + here], refs[7 + here : 7 + 2 * here], refs[7 + 2 * here :]
    result, dhidden, dhid_low, datt_low, sums, res, dff = refs

    @pl.when(first_step())
    def _():
        res[...] = res_in[...]
        dff[...] = dff_in[...]

    feed_columns(ff_low, dy, ups, downs, acts, dpres, res, dff)

    @pl.when(last_step())
    def _():
        rows, inner = attended.shape
        live = live_rows(counts, rows, per_slot)
        state = hidden[...]
        result[...] = (live * (state + res[...])).astype(BF16)
        hat, inverse = stats(state)
        grad = dff[...]
        sums[0:1] = jnp.sum(grad * hat, axis=0, keepdims=True)
        sums[1:2] = jnp.sum(grad, axis=0, keepdims=True)
        back = dy[...].astype(F32) + pull(hat, inverse, grad, gain[2:3])
        dhidden[...] = back
        dhid_low[...] = back.astype(BF16)
        datt = dot(dhid_low[...], w_out[...], NT).astype(BF16)
        datt_low[:rows, :] = datt
        product = datt.astype(F32) * attended[...]
        low = low_lanes((rows, LANES))
        lane = lax.broadcasted_iota(jnp.int32, (rows, LANES), 1)
        delta = jnp.zeros((rows, LANES), F32)
        for t in range(inner // LANES):
            both = product[:, t * LANES : (t + 1) * LANES]
            first = jnp.sum(jnp.where(low, both, 0.0), axis=-1, keepdims=True)
            second = jnp.sum(jnp.where(low, 0.0, both), axis=-1, keepdims=True)
            delta = jnp.where(lane == t, first, delta)
            delta = jnp.where(lane == HEADS // 2 + t, second, delta)
        turned = flipped(jnp.concatenate([delta, jnp.zeros((-rows % LANES, LANES), F32)], axis=0))
        datt_low[rows:, :] = packed(jnp.concatenate([lse[...], turned[:HEADS]], axis=0))


def attend_back_kernel(peers, per_slot, scale, *refs):
    qs, das, kv, dkv = refs[:peers], refs[peers : 2 * peers], refs[2 * peers], refs[2 * peers + 1]
    (near, cross), held = refs[2 * peers + 2 : 2 * peers + 4], refs[2 * peers + 4]
    dqs = [(cross if i % 2 else near, i // 2) for i in range(peers)]
    n, inner = kv.shape[0], kv.shape[2] // 2
    step = pl.program_id(0)
    items = [(s, t) for s in range(n) for t in range(inner // LANES)]
    cuts = [slice(t * LANES, (t + 1) * LANES) for t in range(2 * inner // LANES)]
    rows = [pl.multiple_of((step * n + s) * per_slot, per_slot) for s in range(n)]
    later = inner // LANES

    @pl.when(step == 0)
    def _():
        for i in range(peers):
            turned = unpacked(das[i][-4 * HEADS :, :])
            held[i, :, : 2 * HEADS] = flipped(turned)

    def column(block, h):
        other = h + HEADS // 2
        return jnp.concatenate([block[:, h : h + 1], block[:, other : other + 1]], axis=0)

    sts = [
        jnp.concatenate([held[i, pl.ds(row, per_slot), :] for i in range(peers)], axis=0) for row in rows
    ]
    qp = [paired(jnp.concatenate([ref[pl.ds(rows[s], per_slot), cuts[t]] for ref in qs], axis=0)) for s, t in items]
    dp = [paired(jnp.concatenate([ref[pl.ds(rows[s], per_slot), cuts[t]] for ref in das], axis=0)) for s, t in items]
    scores = [dot(q, kv[s, :, cuts[t]], NT) for q, (s, t) in zip(qp, items)]
    dprobs = [dot(d, kv[s, :, cuts[later + t]], NT) for d, (s, t) in zip(dp, items)]
    probs = [jnp.exp(score * scale - column(sts[s], t)) for score, (s, t) in zip(scores, items)]
    dscores = [
        (prob * (dprob - column(sts[s], HEADS + t))).astype(BF16)
        for prob, dprob, (s, t) in zip(probs, dprobs, items)
    ]
    for (s, t), prob, d in zip(items, probs, dp):
        dkv[s, :, cuts[later + t]] = dot(prob.astype(BF16), d, TN).astype(BF16)
    for (s, t), ds, q in zip(items, dscores, qp):
        dkv[s, :, cuts[t]] = (dot(ds, q, TN) * scale).astype(BF16)
    for (s, t), ds in zip(items, dscores):
        dq = (unpaired(dot(ds, kv[s, :, cuts[t]])) * scale).astype(BF16)
        for i in range(peers):
            ref, at = dqs[i]
            ref[at, pl.ds(rows[s], per_slot), cuts[t]] = dq[i * per_slot : (i + 1) * per_slot]


def pair_kernel(near, other, mine, sent):
    total = near[...].astype(F32) + other[...].astype(F32)
    mine[...] = total[0].astype(BF16)
    sent[...] = total[1].astype(BF16)


def keyval_back_kernel(media, dkv, w_keyval, gain, media_grad, dlat, sums):
    n, rows, width = media.shape
    grad = dot(dkv[...].reshape(-1, dkv.shape[2]), w_keyval[...], NT).reshape(n, -1, width)
    dlat[...] = grad[:, rows:].reshape(dlat.shape)
    grad = grad[:, :rows].reshape(n * rows, width)
    hat, inverse = stats(media[...].reshape(n * rows, width).astype(F32))
    media_grad[...] = pull(hat, inverse, grad, gain[0:1]).astype(BF16).reshape(media_grad.shape)

    @pl.when(pl.program_id(0) == 0)
    def _():
        sums[...] = jnp.zeros_like(sums)

    sums[0:1] += jnp.sum(grad * hat, axis=0, keepdims=True)
    sums[1:2] += jnp.sum(grad, axis=0, keepdims=True)


def latent_back_kernel(peers, *refs):
    dqs = refs[:peers]
    dlat, lat, dhidden, w_query, gain, sums_media, sums_ff, dq_low, latent_grad, sums = refs[peers:]
    dq = sum(ref[...].astype(F32) for ref in dqs).astype(BF16)
    dq_low[...] = dq
    grad = dlat[...] + dot(dq, w_query[...], NT)
    hat, inverse = stats(lat[...].astype(F32))
    latent_grad[...] = (dhidden[...] + pull(hat, inverse, grad, gain[1:2])).astype(BF16)
    sums[0:1] = sums_media[0:1]
    sums[1:2] = jnp.sum(grad * hat, axis=0, keepdims=True)
    sums[2:3] = sums_ff[0:1]
    sums[3:4] = sums_media[1:2]
    sums[4:5] = jnp.sum(grad, axis=0, keepdims=True)
    sums[5:6] = sums_ff[1:2]


def halved(values):
    high = values.astype(BF16).astype(F32)
    return jnp.concatenate([high, values - high], axis=0).astype(BF16)


def joined(values):
    values = values.astype(F32)
    half = values.shape[0] // 2
    return values[:half] + values[half:]


def outer_kernel(count, lanes, own, *refs):
    lefts, rights, refs = refs[:count], refs[count : 2 * count], refs[2 * count :]
    results, held = refs[:-1], refs[-1]

    @pl.when(pl.program_id(0) == 0)
    def _():
        at = 0
        for ref in rights:
            rows, width = ref.shape[-2:]
            for k in range(held.shape[1] // width):
                held[at : at + rows, k * width : (k + 1) * width] = ref[k] if len(ref.shape) == 3 else ref[...]
            at += rows

    left = jnp.concatenate([ref[...].reshape(-1, ref.shape[-1]) for ref in lefts], axis=0)
    product = dot(left, held[...], TN)
    width = product.shape[1] // len(lanes)
    for k, (bit, inner) in enumerate(lanes):
        kept, sent = parted(product[:, k * width : (k + 1) * width], inner, chosen(own, bit))
        results[2 * k][...] = kept.astype(BF16)
        results[2 * k + 1][...] = sent.astype(BF16)


def outer(own, lefts, rights, tile, lanes, name):
    count = len(lefts)
    wide = lambda v: v.shape[-1] * (v.shape[0] if v.ndim == 3 else 1)
    a, b = wide(lefts[0]), wide(rights[0])

    def left_spec(v):
        if v.ndim == 3:
            return pl.BlockSpec((1, v.shape[1], tile), lambda g, *_: (g, 0, 0))
        return pl.BlockSpec((v.shape[0], tile), lambda g, *_: (0, g))

    total = sum(v.shape[-2] for v in rights)
    steps, part = a // tile, b // len(lanes)
    spec = pl.BlockSpec((tile // 2, part), lambda g, *_: (g, 0))
    return call(
        functools.partial(outer_kernel, count, [(order[0], plan[0]) for order, plan in lanes]),
        (steps,),
        [left_spec(v) for v in lefts] + [whole(v.shape) for v in rights],
        [(spec, out((a // 2, part), BF16))] * (2 * len(lanes)),
        scratch=[pltpu.VMEM((total, b), BF16)],
        prefetch=1, name=name,
    )(own, *lefts, *rights)


def query_kernel(bit, rows, own, dq, lat_low, out_t, sums, kept, sent):
    width = lat_low.shape[1]
    which = chosen(own, bit)
    other_rows = out_t.shape[1]
    product = dot(dq[...], lat_low[...], TN)
    first = parted(product, rows, which)
    second = parted(out_t[...].astype(F32).reshape(-1, width), other_rows, which)
    both = [
        jnp.concatenate([a.reshape(-1, rows, width), b.reshape(-1, other_rows, width)], axis=1).reshape(-1, width)
        for a, b in zip(first, second)
    ]
    head = 2 * sums.shape[0]
    kept[...] = both[0].astype(BF16)
    sent[:head, :] = halved(sums[...])
    sent[head:, :] = both[1].astype(BF16)


def side_by_side_kernel(rows, left, right, result):
    product = dot(left[...], right[...], TN).astype(BF16)
    split = product.reshape(-1, 2, rows, product.shape[1])
    result[...] = jnp.concatenate([split[:, 0], split[:, 1]], axis=-1)


def fold_kernel(nxt, end, lanes, extra, own, *refs):
    kept, got, refs = refs[:lanes], refs[lanes : 2 * lanes], refs[2 * lanes :]
    head = 0
    if extra:
        more, refs = refs[0], refs[1:]
        head = 2 * more.shape[0]
        small = more[...] + joined(got[0][:head, :])
        refs[-1][...] = small
    totals = [a[...].astype(F32) + b[head:, :].astype(F32) for a, b in zip(kept, got)]
    if nxt is None:
        for ref, values in zip(refs, end(*totals)):
            ref[...] = values.astype(ref.dtype)
        return
    if len(nxt) < len(totals):
        totals = [jnp.concatenate(totals, axis=1)]
    for k, (total, (bit, inner)) in enumerate(zip(totals, nxt)):
        keep, send = parted(total, inner, chosen(own, bit))
        refs[2 * k][...] = keep.astype(BF16)
        refs[2 * k + 1][head:, :] = send.astype(BF16)
    if extra:
        refs[1][:head, :] = halved(small)


def fold(own, kept, got, extra, nxt, end, name):
    ins = list(kept) + list(got)
    if nxt is not None:
        head = 0 if extra is None else 2 * extra.shape[0]
        shapes = []
        for _ in nxt:
            rows, width = kept[0].shape[0], kept[0].shape[1] * len(kept) // len(nxt)
            shapes += [out((rows // 2, width), BF16), out((head + rows // 2, width), BF16)]
    else:
        shapes = list(jax.eval_shape(end, *(out(v.shape, F32) for v in kept)))
    if extra is not None:
        ins.append(extra)
        shapes.append(out(extra.shape, F32))
    return call(
        functools.partial(fold_kernel, nxt, end, len(kept), extra is not None),
        (1,),
        [whole(v.shape) for v in ins],
        [(whole(s.shape), s) for s in shapes],
        prefetch=1, name=name,
    )(own, *ins)


def place_kernel(block, parts, result):
    peers, _, width = parts.shape
    for p in range(peers):
        for k in range(width // block):
            at = (k * peers + p) * block
            result[:, at : at + block] = parts[p, :, k * block : (k + 1) * block].astype(F32)


def on_device(
    media, latents, counts, gains, biases, w_query, w_keyval, w_out, w_up, w_down, out_grad
):
    slots, patch_rows, width = media.shape
    per_slot = latents.shape[1]
    inner = w_query.shape[1]
    ff = w_up.shape[1]
    n_img, peers = lax.axis_size("img"), lax.axis_size("patch")
    shards = n_img * peers
    scale = 1.0 / math.sqrt(inner // HEADS)
    rows = slots * per_slot
    keys = patch_rows + per_slot
    padded = -(-rows // LANES) * LANES
    gain_spec = whole(gains.shape)
    lat = latents.reshape(rows, width)

    own = jnp.stack([lax.axis_index("patch"), lax.axis_index("img")]).astype(jnp.int32)
    fine = width // shards % 16 == 0 and inner // shards % 16 == 0
    lat_low, q_low, dy = call(
        functools.partial(latent_kernel, per_slot),
        (1,),
        [SMEM, whole((rows, width)), whole((rows, width)), gain_spec, gain_spec, whole(w_query.shape)],
        [
            (whole((rows, width)), out((rows, width), BF16)),
            (whole((rows, inner)), out((rows, inner), BF16)),
            (whole((rows, width)), out((rows, width), BF16)),
        ],
        vmem=62, name="latent",
    )(counts, lat, out_grad.reshape(rows, width), gains, biases, w_query)
    qs = {0: q_low}
    bit = peers // 2
    qs[bit] = swap(q_low, "patch", bit)

    group = slots // 2
    key_input, keyval = call(
        media_kernel,
        (slots // group,),
        [
            leading((group, patch_rows, width)), leading((group * per_slot, width)),
            gain_spec, gain_spec, whole(w_keyval.shape),
        ],
        [
            (leading((group, keys, width)), out((slots, keys, width), BF16)),
            (leading((group, keys, 2 * inner)), out((slots, keys, 2 * inner), BF16)),
        ],
        vmem=62, name="media",
    )(media, lat_low, gains, biases, w_keyval)
    first = after(qs[bit], keyval)
    qs[bit] = first
    while bit > 1:
        bit //= 2
        for j in list(qs):
            qs[j ^ bit] = swap(qs[j], "patch", bit)
    qs = [qs[j] for j in range(peers)]

    pair = 2
    kv_block = leading((pair, keys, 2 * inner))
    part_rows = rows + 2 * HEADS
    stat_out = (whole((HEADS, padded)), out((HEADS, padded), F32))
    parts = call(
        functools.partial(attend_kernel, peers, per_slot, scale),
        (slots // pair,),
        [whole((rows, inner))] * peers + [kv_block],
        [(whole((part_rows, inner)), out((part_rows, inner), BF16))] * peers,
        scratch=[pltpu.VMEM((peers, padded, LANES), F32)],
        name="attend",
    )(*qs, keyval)
    parts = [parts[0]] + [swap(parts[j], "patch", j) for j in range(1, peers)]
    dys = {0: dy, peers // 2: swap(after(dy, *parts[1:]), "patch", peers // 2)}

    attended, att_low, hidden, ff_low, lse = call(
        functools.partial(mix_kernel, peers),
        (1,),
        [whole((part_rows, inner))] * peers
        + [whole((rows, width)), whole(w_out.shape), gain_spec, gain_spec],
        [
            (whole((rows, inner)), out((rows, inner), F32)),
            (whole((rows, inner)), out((rows, inner), BF16)),
            (whole((rows, width)), out((rows, width), F32)),
            (whole((rows, width)), out((rows, width), BF16)),
            stat_out,
        ],
        vmem=62, name="mix",
    )(*parts, lat, w_out, gains, biases)
    bit = peers // 2
    ffs = {0: ff_low, bit: swap(ff_low, "patch", bit)}

    halves = 2
    blocks = ff // (peers * halves * LANES)
    chunk = ff // shards
    strided = chunk % LANES == 0

    def column(own, j, a, k):
        p, k = own[0] ^ j, a * blocks + k
        if strided:
            return ((k // (chunk // LANES)) * peers + p) * (chunk // LANES) + k % (chunk // LANES)
        return p * halves * blocks + k

    def weights(first, stride):
        ups = [
            pl.BlockSpec((width, LANES), lambda g, a, own, k=k: (0, column(own, first + stride * g, a, k)))
            for k in range(blocks)
        ]
        downs = [
            pl.BlockSpec((LANES, width), lambda g, a, own, k=k: (column(own, first + stride * g, a, k), 0))
            for k in range(blocks)
        ]
        return ups + downs

    part = ff // (peers * halves)
    here = peers // 2
    columns = (whole((halves, rows, part)), out((halves, rows, part), BF16))
    wide_low = (whole((rows, width)), out((rows, width), BF16))
    wide = (whole((rows, width)), out((rows, width), F32))
    count = blocks
    far = call(
        functools.partial(feed_kernel, count, here),
        (here, halves),
        [whole((rows, width))] * 2 + weights(here, 1),
        [columns] * (2 * here) + [wide, wide],
        vmem=62, prefetch=1, name="feed",
    )(own, ff_low, dy, *([w_up] * count), *([w_down] * count))
    dys = spread({0: after(dy, ff_low), bit: after(dys[bit], far[-1])})
    ffs[peers // 2] = after(ffs[peers // 2], dys[bit])
    ffs = spread(ffs)

    def cross(values):
        return [swap(v, "patch", here + k) for k, v in enumerate(values)]

    act_cross = cross(after(tuple(far[:here]), ffs[peers // 2]))
    near = call(
        functools.partial(feed_end_kernel, per_slot, count, here),
        (here, halves),
        [SMEM] + [whole((rows, width))] * 2 + weights(here - 1, -1)
        + [whole((rows, width))] * 3 + [whole((rows, inner)), whole((HEADS, padded)), whole(w_out.shape), gain_spec],
        [columns] * (2 * here)
        + [wide_low, wide, wide_low]
        + [(whole((rows + 4 * HEADS, inner)), out((rows + 4 * HEADS, inner), BF16)), (whole((2, width)), out((2, width), F32))],
        scratch=[pltpu.VMEM((rows, width), F32), pltpu.VMEM((rows, width), F32)],
        vmem=62, prefetch=1, name="feed_end",
    )(own, counts, after(ff_low, *ffs[1:], *dys[1:]), dy, *([w_up] * count), *([w_down] * count),
      far[2 * here], far[2 * here + 1], hidden, attended, lse, w_out, gains)
    result, dhidden, dhid_low, datt_low, sums_ff = near[2 * here :]
    act_near, dpre_near = list(reversed(near[:here])), list(reversed(near[here : 2 * here]))

    das = {0: datt_low, peers // 2: swap(datt_low, "patch", peers // 2)}
    out_rows = width // shards // 2
    q_rows = inner // shards
    every, ff_bits = digits_of("img") + digits_of("patch"), digits_of("img")
    ff_orders = [ff_bits[::-1], ff_bits[-2:] + ff_bits[:-2][::-1]]
    named = {"c": ("patch", 1), "x": ("patch", 2), "y": ("img", 1), "z": ("img", 2)}

    def order_of(letters):
        head = [named[k] for k in letters]
        return head + [bit for bit in reversed(every) if bit not in head]

    def ff_lanes(rows):
        return [(order, plan_of(rows, ff_bits, order)) for order in ff_orders]

    def near_swaps(values):
        return [values[0]] + [swap(values[j], "patch", j) for j in range(1, here)]

    kv_order, qo_order = order_of(KV_ORDER), order_of(QO_ORDER)
    acts = near_swaps(act_near) + act_cross
    dpre_first = near_swaps(dpre_near)
    got, sums_of = {}, {}

    def out_grad(mark):
        got["out_t"] = call(
            functools.partial(side_by_side_kernel, out_rows),
            (2,),
            [pl.BlockSpec((rows, width // 2), lambda g: (0, g)), whole((rows, inner))],
            [(leading((shards // 2, out_rows, 2 * inner)), out((shards, out_rows, 2 * inner), BF16))],
            name="out_grad",
        )(after(dhid_low, mark), att_low)[0]
        return got["out_t"]

    def begun(letter, scatter):
        sums_of[letter] = scatter
        mark = scatter.both[0]
        scatter.begin()
        return mark

    def down_grad(mark):
        lanes = ff_lanes(width)
        both = outer(own, dys[:-1] + [after(dys[-1], mark)], acts, width // 2, lanes, "down_grad")
        return begun("D", Scatter(own, both, lanes, lambda t: [t.astype(BF16)], name="down_fold"))

    def send_dpre(mark):
        got["dpres"] = dpre_first + cross(after(tuple(far[here : 2 * here]), mark))
        return mark

    def attend_back(mark):
        near_das = spread({0: das[0], peers // 2: after(das[peers // 2], mark)})
        values = call(
            functools.partial(attend_back_kernel, peers, per_slot, scale),
            (slots // pair,),
            [whole((rows, inner))] * peers + [whole((rows + 4 * HEADS, inner))] * peers + [kv_block],
            [(kv_block, out(keyval.shape, BF16))]
            + [(whole((here, rows, inner)), out((here, rows, inner), BF16))] * 2,
            scratch=[pltpu.VMEM((peers, padded, LANES), F32)],
            name="attend_back",
        )(*qs, *near_das, keyval)
        got["dkv"], near_dq, cross_dq = values
        got["pair"] = (near_dq, swap(cross_dq, "patch", 1))
        return got["dkv"]

    def pair_dq(mark):
        near_dq, other = got["pair"]
        mine, sent = call(
            pair_kernel,
            (1,),
            [whole(near_dq.shape)] * 2,
            [(whole((rows, inner)), out((rows, inner), BF16))] * 2,
            name="pair",
        )(after(near_dq, mark), other)
        got["dqs"] = [mine, swap(sent, "patch", here)]
        return mine

    def keyval_back(mark):
        got["media_grad"], got["dlat"], got["sums_media"] = call(
            keyval_back_kernel,
            (slots // group,),
            [
                leading((group, patch_rows, width)), leading((group, keys, 2 * inner)),
                whole(w_keyval.shape), gain_spec,
            ],
            [
                (leading((group, patch_rows, width)), out(media.shape, BF16)),
                (leading((group * per_slot, width)), out((rows, width), F32)),
                (whole((2, width)), out((2, width), F32)),
            ],
            name="keyval_back",
        )(media, after(got["dkv"], mark), w_keyval, gains)
        return got["sums_media"]

    def keyval_grad(mark):
        lanes = [(kv_order, plan_of(2 * inner, every, kv_order))]
        both = outer(
            own, [after(got["dkv"], mark).reshape(-1, 2 * inner)], [key_input.reshape(-1, width)], 2 * inner // 4,
            lanes, "keyval_grad",
        )
        return begun("K", Scatter(own, both, lanes, lambda t: [t], name="keyval_fold"))

    def up_grad(mark):
        lanes, dpres = ff_lanes(halves * part), got["dpres"]
        both = outer(own, dpres[:-1] + [after(dpres[-1], mark)], ffs, part, lanes, "up_grad")
        end = lambda t: [flipped(t)] if strided else [t.astype(BF16)]
        return begun("U", Scatter(own, both, lanes, end, name="up_fold"))

    def latent_back(mark):
        got["dq_low"], got["latent_grad"], got["sums"] = call(
            functools.partial(latent_back_kernel, here),
            (1,),
            [whole((rows, inner))] * here
            + [whole((rows, width))] * 3 + [whole(w_query.shape), gain_spec, whole((2, width)), whole((2, width))],
            [
                (whole((rows, inner)), out((rows, inner), BF16)),
                (whole((rows, width)), out((rows, width), BF16)),
                (whole((HEADS, width)), out((HEADS, width), F32)),
            ],
            name="latent_back",
        )(*got["dqs"], after(got["dlat"], mark), lat, dhidden, w_query, gains, got["sums_media"], sums_ff)
        return got["dq_low"]

    def open_rows(total):
        other = total[q_rows:]
        return [total[:q_rows], jnp.concatenate([other[:, :inner], other[:, inner:]], axis=0)]

    def query_grad(mark):
        q_plan, qo_plan = plan_of(inner, every, qo_order), plan_of(2 * inner, every, qo_order)
        sums = got["sums"]
        tall = 2 * sums.shape[0] + inner
        ins = (after(got["dq_low"], mark), lat_low, got["out_t"], sums)
        both = call(
            functools.partial(query_kernel, qo_order[0], q_plan[0]),
            (1,),
            [whole(v.shape) for v in ins],
            [(whole((inner, width)), out((inner, width), BF16)), (whole((tall, width)), out((tall, width), BF16))],
            prefetch=1, name="query_grad",
        )(own, *ins)
        return begun("Q", Scatter(own, both, [(qo_order, qo_plan)], open_rows, extra=sums, name="query_fold"))

    tasks = dict(
        O=out_grad, G=down_grad, X=send_dpre, B=attend_back, Y=pair_dq, V=keyval_back, W=keyval_grad, P=up_grad, L=latent_back,
        R=query_grad,
    )
    mark = datt_low
    for letter in ORDER:
        if letter in tasks:
            mark = tasks[letter](mark)
        else:
            one = sums_of[letter]
            mark = one.finish(mark)
            if one.at < one.steps:
                one.begin()
    media_grad, latent_grad = got["media_grad"], got["latent_grad"]
    qo_sum = sums_of["Q"]
    (up_sum,), (kv_sum,), (down,), (q_sum, out_sum) = (sums_of[k].run() for k in "UKDQ")
    small = lax.dynamic_slice_in_dim(
        qo_sum.extra, (own[1] * peers + own[0]) * (width // shards), width // shards, axis=1
    )
    if not strided:
        pairs = [((b % n_img) * peers + b // n_img, b) for b in range(shards)]
        up_sum = lax.ppermute(up_sum, ("img", "patch"), pairs).astype(F32).T

    down = lax.all_to_all(down.reshape(peers, -1, halves * part), "patch", 0, 0, tiled=True)
    down_t = call(
        functools.partial(place_kernel, chunk if strided else halves * part),
        (1,),
        [whole(down.shape)],
        [(whole((width // shards, ff)), out((width // shards, ff), F32))],
        name="down_place",
    )(down)[0]

    return (
        result.reshape(slots, per_slot, width),
        media_grad,
        latent_grad.reshape(slots, per_slot, width),
        q_sum.T,
        kv_sum.T,
        out_sum.T,
        up_sum,
        down_t.T,
        small[:3],
        small[3:6],
    )


def solution(mesh):
    rows = P("img", "patch", None)
    shard = P(None, ("img", "patch"))
    return jax.shard_map(
        on_device,
        mesh=mesh,
        in_specs=(rows, rows, P("img"), P(), P(), P(), P(), P(), P(), P(), rows),
        out_specs=(rows, rows, rows) + (shard,) * 7,
        check_vma=False,
    )
```

```python
import functools
import math

import jax
import jax.numpy as jnp
from jax import lax
from jax.experimental import pallas as pl
from jax.experimental.pallas import tpu as pltpu
from jax.sharding import PartitionSpec as P

HEADS = 8
SLOTS_PER = 5
EPS = 1e-05
LANES = 128
F32 = jnp.float32
BF16 = jnp.bfloat16
MIB = 1024 * 1024
TIMES = dict(latent=2.9, media=2.7, attend=3.1, mix=3.8, feed=0.1, feed_end=36.0, down_grad=4.0, attend_back=1.7, keyval_grad=11.4, up_grad=4.0, keyval_back=4.0, latent_back=1.6, query_grad=1.5, pair=0.8, down_fold=0.8, up_fold=0.8, keyval_fold=0.8, query_fold=1.6, out_grad=0.8)
RATE = 2e+09
ORDER = "OGXBVDWYPKDLRUDUKQQKUQKQKQ"
KV_ORDER, QO_ORDER = "cxyz", "cxyz"


def swap(values, axis, bit):
    n = lax.axis_size(axis)
    return lax.ppermute(values, axis, [(k, k ^ bit) for k in range(n)])


def log2(n):
    return n.bit_length() - 1


def after(values, *others):
    return lax.optimization_barrier((values,) + others)[0]


def spread(blocks):
    n = lax.axis_size("patch")
    blocks = dict(blocks)
    bit = n // 4
    while bit:
        for j in list(blocks):
            blocks[j ^ bit] = swap(blocks[j], "patch", bit)
        bit //= 2
    return [blocks[j] for j in range(n)]


def digits_of(axis):
    n = lax.axis_size(axis)
    return [(axis, 1 << k) for k in reversed(range(log2(n)))]


def chosen(own, bit):
    axis, weight = bit
    return (own[("patch", "img").index(axis)] // weight) % 2


def plan_of(rows, digits, order):
    digits, plan = list(digits), []
    for bit in order:
        at = digits.index(bit)
        plan.append(rows // 2 ** (at + 1))
        del digits[at]
        rows //= 2
    return plan


def parted(values, inner, which):
    width = values.shape[-1]
    split = values.reshape(-1, 2, inner, width)
    low, high = split[:, 0].reshape(-1, width), split[:, 1].reshape(-1, width)
    return jnp.where(which == 1, high, low), jnp.where(which == 1, low, high)


class Scatter:
    def __init__(self, own, both, lanes, end, extra=None, name=None):
        self.own, self.both, self.lanes, self.end = own, both, lanes, end
        self.extra, self.name, self.at, self.open = extra, name, 0, False
        self.steps = len(lanes[0][0])

    def begin(self, *others):
        sent = after(tuple(self.both[1::2]), *others)
        self.got = [swap(v, *order[self.at]) for v, (order, _) in zip(sent, self.lanes)]
        self.at, self.open = self.at + 1, True

    def finish(self, *others):
        kept, self.open = tuple(self.both[::2]), False
        if others:
            kept = after(kept, *others)
        nxt = None
        if self.at < self.steps:
            if all(order[self.at :] == self.lanes[0][0][self.at :] for order, _ in self.lanes):
                self.lanes = self.lanes[:1]
            nxt = [(order[self.at], plan[self.at]) for order, plan in self.lanes]
        values = fold(self.own, kept, self.got, self.extra, nxt, self.end, self.name)
        if self.extra is not None:
            self.extra = values[-1]
            values = values[:-1]
        if nxt is not None:
            self.both = values
        else:
            self.values = values
        return values[0]

    def run(self):
        while self.open:
            self.finish()
            if self.at < self.steps:
                self.begin()
        return self.values


def stats(values):
    average = jnp.mean(values, axis=-1, keepdims=True)
    centred = values - average
    spread = jnp.mean(centred * centred, axis=-1, keepdims=True)
    inverse = lax.rsqrt(spread + EPS)
    return centred * inverse, inverse


def pull(hat, inverse, grad, gain):
    scaled = grad * gain
    first = jnp.mean(scaled, axis=-1, keepdims=True)
    second = jnp.mean(scaled * hat, axis=-1, keepdims=True)
    return inverse * (scaled - first - hat * second)


def gelu_parts(values):
    cdf = 0.5 + 0.5 * lax.erf(values * (1.0 / math.sqrt(2.0)))
    density = jnp.exp(-0.5 * values * values) * (1.0 / math.sqrt(2.0 * math.pi))
    return values * cdf, cdf + values * density


def dot(a, b, dims=((1,), (0,))):
    return lax.dot_general(a, b, (dims, ((), ())), preferred_element_type=F32)


NT = ((1,), (1,))
TN = ((0,), (0,))


def low_lanes(shape):
    return lax.broadcasted_iota(jnp.int32, shape, len(shape) - 1) < LANES // 2


def live_rows(counts_ref, rows, per_slot):
    row = lax.broadcasted_iota(jnp.int32, (rows, 1), 0)
    live = jnp.zeros((rows, 1), F32)
    for sample in range(rows // (per_slot * SLOTS_PER)):
        start = sample * SLOTS_PER * per_slot
        inside = jnp.logical_and(row >= start, row < start + counts_ref[sample] * per_slot)
        live = jnp.where(inside, 1.0, live)
    return live


def paired(block):
    low = low_lanes(block.shape)
    zero = jnp.zeros_like(block)
    return jnp.concatenate([jnp.where(low, block, zero), jnp.where(low, zero, block)], axis=0)


def unpaired(block):
    half = block.shape[0] // 2
    return jnp.where(low_lanes((half, block.shape[1])), block[:half], block[half:])


def flipped(values):
    a, b = values.shape
    tall, wide = -a % LANES, -b % LANES
    if wide:
        values = jnp.concatenate([values, jnp.zeros((a, wide), F32)], axis=1)
    if tall:
        values = jnp.concatenate([values, jnp.zeros((tall, b + wide), F32)], axis=0)
    return values.T[:b, :a]


def call(kernel, grid, ins, outs, scratch=(), vmem=40, prefetch=0, name=None):
    return pl.pallas_call(
        kernel,
        grid_spec=pltpu.PrefetchScalarGridSpec(
            num_scalar_prefetch=prefetch,
            grid=grid,
            in_specs=ins,
            out_specs=[spec for spec, _ in outs],
            scratch_shapes=list(scratch),
        ),
        out_shape=[shape for _, shape in outs],
        compiler_params=pltpu.CompilerParams(
            vmem_limit_bytes=vmem * MIB, dimension_semantics=("arbitrary",) * len(grid)
        ),
        cost_estimate=pl.CostEstimate(flops=int(TIMES.get(name, 0.8) * RATE), bytes_accessed=100000, transcendentals=0),
        name=name,
    )


def whole(shape):
    zeros = (0,) * len(shape)
    return pl.BlockSpec(tuple(shape), lambda *_: zeros)


def leading(shape):
    zeros = (0,) * (len(shape) - 1)
    return pl.BlockSpec(tuple(shape), lambda g, *_: (g,) + zeros)


def out(shape, dtype):
    return jax.ShapeDtypeStruct(tuple(shape), dtype)


SMEM = pl.BlockSpec(memory_space=pltpu.SMEM)


def packed(values):
    high = values.astype(BF16)
    left = values - high.astype(F32)
    middle = left.astype(BF16)
    small = left - middle.astype(F32)
    top = jnp.concatenate([high.astype(F32), middle.astype(F32)], axis=1)
    bottom = jnp.concatenate([small, jnp.zeros_like(small)], axis=1)
    return jnp.concatenate([top, bottom], axis=0).astype(BF16)


def unpacked(values):
    values = values.astype(F32)
    n, m = values.shape[0] // 2, values.shape[1] // 2
    return values[:n, :m] + values[:n, m:] + values[n:, :m]


def latent_kernel(per_slot, counts, lat, grad, gain, bias, w_query, lat_low, q_low, dy):
    hat, _ = stats(lat[...].astype(F32))
    low = (hat * gain[1:2] + bias[1:2]).astype(BF16)
    lat_low[...] = low
    q_low[...] = dot(low, w_query[...]).astype(BF16)
    live = live_rows(counts, lat.shape[0], per_slot)
    dy[...] = (live * grad[...].astype(F32)).astype(BF16)


def media_kernel(media, lat_low, gain, bias, w_keyval, key_input, keyval):
    n, rows, width = media.shape
    hat, _ = stats(media[...].reshape(n * rows, width).astype(F32))
    low = (hat * gain[0:1] + bias[0:1]).astype(BF16)
    key_input[:, :rows, :] = low.reshape(n, rows, width)
    key_input[:, rows:, :] = lat_low[...].reshape(n, -1, width)
    every = key_input[...].reshape(-1, width)
    keyval[...] = dot(every, w_keyval[...]).astype(BF16).reshape(keyval.shape)


def attend_kernel(peers, per_slot, scale, *refs):
    qs, kv, parts, held = refs[:peers], refs[peers], refs[peers + 1 : 2 * peers + 1], refs[2 * peers + 1]
    n, keys, inner = kv.shape[0], kv.shape[1], kv.shape[2] // 2
    step = pl.program_id(0)
    items = [(s, t) for s in range(n) for t in range(inner // LANES)]
    cuts = [slice(t * LANES, (t + 1) * LANES) for t in range(2 * inner // LANES)]
    rows = [pl.multiple_of((step * n + s) * per_slot, per_slot) for s in range(n)]
    ones = jnp.ones((keys, LANES), BF16)

    @pl.when(step == 0)
    def _():
        held[...] = jnp.zeros_like(held)

    scores = []
    for s, t in items:
        q = paired(jnp.concatenate([ref[pl.ds(rows[s], per_slot), cuts[t]] for ref in qs], axis=0))
        scores.append(dot(q, kv[s, :, cuts[t]], NT) * scale)
    tops = [jnp.max(score, axis=-1, keepdims=True) for score in scores]
    probs = [jnp.exp(score - top).astype(BF16) for score, top in zip(scores, tops)]
    sums = [
        dot(prob, jnp.concatenate([kv[s, :, cuts[inner // LANES + t]], ones], axis=1))
        for prob, (s, t) in zip(probs, items)
    ]
    lane = lax.broadcasted_iota(jnp.int32, (peers * per_slot, LANES), 1)
    logs = [jnp.zeros((peers * per_slot, LANES), F32) for _ in range(n)]
    for (s, t), both, top in zip(items, sums, tops):
        total = unpaired(both[:, LANES:])
        o = (unpaired(both[:, :LANES]) / total).astype(BF16)
        lse = unpaired(jnp.broadcast_to(top, (top.shape[0], LANES))) + jnp.log(total)
        here = jnp.logical_or(lane == t, lane == LANES // 2 + HEADS // 2 + t)
        logs[s] = jnp.where(here, lse, logs[s])
        for i in range(peers):
            parts[i][pl.ds(rows[s], per_slot), cuts[t]] = o[i * per_slot : (i + 1) * per_slot]
    for s in range(n):
        for i in range(peers):
            held[i, pl.ds(rows[s], per_slot), :] = logs[s][i * per_slot : (i + 1) * per_slot]

    @pl.when(step == pl.num_programs(0) - 1)
    def _():
        for i in range(peers):
            turned = held[i].T
            turned = turned[:HEADS] + turned[LANES // 2 : LANES // 2 + HEADS]
            parts[i][-2 * HEADS :, :] = packed(turned)


def mix_kernel(peers, *refs):
    parts = refs[:peers]
    lat, w_out, gain, bias, attended, att_low, hidden, ff_low, lse_out = refs[peers:]
    rows, inner = attended.shape
    logs = [unpacked(ref[rows:, :]) for ref in parts]
    top = functools.reduce(jnp.maximum, logs)
    lse = top + jnp.log(sum(jnp.exp(v - top) for v in logs))
    lse_out[...] = lse
    weights = flipped(jnp.concatenate([jnp.exp(v - lse) for v in logs], axis=0))[:rows]
    low = low_lanes((rows, LANES))
    for t in range(inner // LANES):
        cut = slice(t * LANES, (t + 1) * LANES)
        total = jnp.zeros((rows, LANES), F32)
        for j in range(peers):
            at = j * HEADS + t
            other = at + HEADS // 2
            weight = jnp.where(low, weights[:, at : at + 1], weights[:, other : other + 1])
            total = total + weight * parts[j][:rows, cut].astype(F32)
        attended[:, cut] = total
        att_low[:, cut] = total.astype(BF16)
    state = lat[...].astype(F32) + dot(att_low[...], w_out[...])
    hidden[...] = state
    hat, _ = stats(state)
    ff_low[...] = (hat * gain[2:3] + bias[2:3]).astype(BF16)


def feed_columns(ff_low, dy, ups, downs, acts, dpres, res, dff):
    half = len(ups) // 2
    a = pl.program_id(1)
    parts = []
    for at in (slice(0, half), slice(half, 2 * half)):
        up = jnp.concatenate([ref[...] for ref in ups[at]], axis=1)
        down = jnp.concatenate([ref[...] for ref in downs[at]], axis=0)
        parts.append((up, down, dot(ff_low[...], up), dot(dy[...], down, NT)))
    done = []
    for up, down, pre, dact in parts:
        value, slope = gelu_parts(pre)
        value = value.astype(BF16)
        back = (slope * dact).astype(BF16)
        res[...] += dot(value, down)
        dff[...] += dot(back, up, NT)
        done.append((value, back))
    for at, (act, dpre) in enumerate(zip(acts, dpres)):

        @pl.when(pl.program_id(0) == at)
        def _():
            width = done[0][0].shape[1]
            for k, (value, back) in enumerate(done):
                act[a, :, k * width : (k + 1) * width] = value
                dpre[a, :, k * width : (k + 1) * width] = back


def first_step():
    return jnp.logical_and(pl.program_id(0) == 0, pl.program_id(1) == 0)


def last_step():
    ends = [pl.program_id(k) == pl.num_programs(k) - 1 for k in range(2)]
    return jnp.logical_and(*ends)


def feed_kernel(count, here, own, ff_low, dy, *refs):
    ups, downs, refs = refs[:count], refs[count : 2 * count], refs[2 * count :]
    acts, dpres, (res, dff) = refs[:here], refs[here : 2 * here], refs[2 * here :]

    @pl.when(first_step())
    def _():
        res[...] = jnp.zeros_like(res)
        dff[...] = jnp.zeros_like(dff)

    feed_columns(ff_low, dy, ups, downs, acts, dpres, res, dff)


def feed_end_kernel(per_slot, count, here, own, counts, ff_low, dy, *refs):
    ups, downs, refs = refs[:count], refs[count : 2 * count], refs[2 * count :]
    res_in, dff_in, hidden, attended, lse, w_out, gain = refs[:7]
    acts, dpres, refs = refs[7 : 7 + here], refs[7 + here : 7 + 2 * here], refs[7 + 2 * here :]
    result, dhidden, dhid_low, datt_low, sums, res, dff = refs

    @pl.when(first_step())
    def _():
        res[...] = res_in[...]
        dff[...] = dff_in[...]

    feed_columns(ff_low, dy, ups, downs, acts, dpres, res, dff)

    @pl.when(last_step())
    def _():
        rows, inner = attended.shape
        live = live_rows(counts, rows, per_slot)
        state = hidden[...]
        result[...] = (live * (state + res[...])).astype(BF16)
        hat, inverse = stats(state)
        grad = dff[...]
        sums[0:1] = jnp.sum(grad * hat, axis=0, keepdims=True)
        sums[1:2] = jnp.sum(grad, axis=0, keepdims=True)
        back = dy[...].astype(F32) + pull(hat, inverse, grad, gain[2:3])
        dhidden[...] = back
        dhid_low[...] = back.astype(BF16)
        datt = dot(dhid_low[...], w_out[...], NT).astype(BF16)
        datt_low[:rows, :] = datt
        product = datt.astype(F32) * attended[...]
        low = low_lanes((rows, LANES))
        lane = lax.broadcasted_iota(jnp.int32, (rows, LANES), 1)
        delta = jnp.zeros((rows, LANES), F32)
        for t in range(inner // LANES):
            both = product[:, t * LANES : (t + 1) * LANES]
            first = jnp.sum(jnp.where(low, both, 0.0), axis=-1, keepdims=True)
            second = jnp.sum(jnp.where(low, 0.0, both), axis=-1, keepdims=True)
            delta = jnp.where(lane == t, first, delta)
            delta = jnp.where(lane == HEADS // 2 + t, second, delta)
        turned = flipped(jnp.concatenate([delta, jnp.zeros((-rows % LANES, LANES), F32)], axis=0))
        datt_low[rows:, :] = packed(jnp.concatenate([lse[...], turned[:HEADS]], axis=0))


def attend_back_kernel(peers, per_slot, scale, *refs):
    qs, das, kv, dkv = refs[:peers], refs[peers : 2 * peers], refs[2 * peers], refs[2 * peers + 1]
    (near, cross), held = refs[2 * peers + 2 : 2 * peers + 4], refs[2 * peers + 4]
    dqs = [(cross if i % 2 else near, i // 2) for i in range(peers)]
    n, inner = kv.shape[0], kv.shape[2] // 2
    step = pl.program_id(0)
    items = [(s, t) for s in range(n) for t in range(inner // LANES)]
    cuts = [slice(t * LANES, (t + 1) * LANES) for t in range(2 * inner // LANES)]
    rows = [pl.multiple_of((step * n + s) * per_slot, per_slot) for s in range(n)]
    later = inner // LANES

    @pl.when(step == 0)
    def _():
        for i in range(peers):
            turned = unpacked(das[i][-4 * HEADS :, :])
            held[i, :, : 2 * HEADS] = flipped(turned)

    def column(block, h):
        other = h + HEADS // 2
        return jnp.concatenate([block[:, h : h + 1], block[:, other : other + 1]], axis=0)

    sts = [
        jnp.concatenate([held[i, pl.ds(row, per_slot), :] for i in range(peers)], axis=0) for row in rows
    ]
    qp = [paired(jnp.concatenate([ref[pl.ds(rows[s], per_slot), cuts[t]] for ref in qs], axis=0)) for s, t in items]
    dp = [paired(jnp.concatenate([ref[pl.ds(rows[s], per_slot), cuts[t]] for ref in das], axis=0)) for s, t in items]
    scores = [dot(q, kv[s, :, cuts[t]], NT) for q, (s, t) in zip(qp, items)]
    dprobs = [dot(d, kv[s, :, cuts[later + t]], NT) for d, (s, t) in zip(dp, items)]
    probs = [jnp.exp(score * scale - column(sts[s], t)) for score, (s, t) in zip(scores, items)]
    dscores = [
        (prob * (dprob - column(sts[s], HEADS + t))).astype(BF16)
        for prob, dprob, (s, t) in zip(probs, dprobs, items)
    ]
    for (s, t), prob, d in zip(items, probs, dp):
        dkv[s, :, cuts[later + t]] = dot(prob.astype(BF16), d, TN).astype(BF16)
    for (s, t), ds, q in zip(items, dscores, qp):
        dkv[s, :, cuts[t]] = (dot(ds, q, TN) * scale).astype(BF16)
    for (s, t), ds in zip(items, dscores):
        dq = (unpaired(dot(ds, kv[s, :, cuts[t]])) * scale).astype(BF16)
        for i in range(peers):
            ref, at = dqs[i]
            ref[at, pl.ds(rows[s], per_slot), cuts[t]] = dq[i * per_slot : (i + 1) * per_slot]


def pair_kernel(near, other, mine, sent):
    total = near[...].astype(F32) + other[...].astype(F32)
    mine[...] = total[0].astype(BF16)
    sent[...] = total[1].astype(BF16)


def keyval_back_kernel(media, dkv, w_keyval, gain, media_grad, dlat, sums):
    n, rows, width = media.shape
    grad = dot(dkv[...].reshape(-1, dkv.shape[2]), w_keyval[...], NT).reshape(n, -1, width)
    dlat[...] = grad[:, rows:].reshape(dlat.shape)
    grad = grad[:, :rows].reshape(n * rows, width)
    hat, inverse = stats(media[...].reshape(n * rows, width).astype(F32))
    media_grad[...] = pull(hat, inverse, grad, gain[0:1]).astype(BF16).reshape(media_grad.shape)

    @pl.when(pl.program_id(0) == 0)
    def _():
        sums[...] = jnp.zeros_like(sums)

    sums[0:1] += jnp.sum(grad * hat, axis=0, keepdims=True)
    sums[1:2] += jnp.sum(grad, axis=0, keepdims=True)


def latent_back_kernel(peers, *refs):
    dqs = refs[:peers]
    dlat, lat, dhidden, w_query, gain, sums_media, sums_ff, dq_low, latent_grad, sums = refs[peers:]
    dq = sum(ref[...].astype(F32) for ref in dqs).astype(BF16)
    dq_low[...] = dq
    grad = dlat[...] + dot(dq, w_query[...], NT)
    hat, inverse = stats(lat[...].astype(F32))
    latent_grad[...] = (dhidden[...] + pull(hat, inverse, grad, gain[1:2])).astype(BF16)
    sums[0:1] = sums_media[0:1]
    sums[1:2] = jnp.sum(grad * hat, axis=0, keepdims=True)
    sums[2:3] = sums_ff[0:1]
    sums[3:4] = sums_media[1:2]
    sums[4:5] = jnp.sum(grad, axis=0, keepdims=True)
    sums[5:6] = sums_ff[1:2]


def halved(values):
    high = values.astype(BF16).astype(F32)
    return jnp.concatenate([high, values - high], axis=0).astype(BF16)


def joined(values):
    values = values.astype(F32)
    half = values.shape[0] // 2
    return values[:half] + values[half:]


def outer_kernel(count, lanes, own, *refs):
    lefts, rights, refs = refs[:count], refs[count : 2 * count], refs[2 * count :]
    results, held = refs[:-1], refs[-1]

    @pl.when(pl.program_id(0) == 0)
    def _():
        at = 0
        for ref in rights:
            rows, width = ref.shape[-2:]
            for k in range(held.shape[1] // width):
                held[at : at + rows, k * width : (k + 1) * width] = ref[k] if len(ref.shape) == 3 else ref[...]
            at += rows

    left = jnp.concatenate([ref[...].reshape(-1, ref.shape[-1]) for ref in lefts], axis=0)
    product = dot(left, held[...], TN)
    width = product.shape[1] // len(lanes)
    for k, (bit, inner) in enumerate(lanes):
        kept, sent = parted(product[:, k * width : (k + 1) * width], inner, chosen(own, bit))
        results[2 * k][...] = kept.astype(BF16)
        results[2 * k + 1][...] = sent.astype(BF16)


def outer(own, lefts, rights, tile, lanes, name):
    count = len(lefts)
    wide = lambda v: v.shape[-1] * (v.shape[0] if v.ndim == 3 else 1)
    a, b = wide(lefts[0]), wide(rights[0])

    def left_spec(v):
        if v.ndim == 3:
            return pl.BlockSpec((1, v.shape[1], tile), lambda g, *_: (g, 0, 0))
        return pl.BlockSpec((v.shape[0], tile), lambda g, *_: (0, g))

    total = sum(v.shape[-2] for v in rights)
    steps, part = a // tile, b // len(lanes)
    spec = pl.BlockSpec((tile // 2, part), lambda g, *_: (g, 0))
    return call(
        functools.partial(outer_kernel, count, [(order[0], plan[0]) for order, plan in lanes]),
        (steps,),
        [left_spec(v) for v in lefts] + [whole(v.shape) for v in rights],
        [(spec, out((a // 2, part), BF16))] * (2 * len(lanes)),
        scratch=[pltpu.VMEM((total, b), BF16)],
        prefetch=1, name=name,
    )(own, *lefts, *rights)


def query_kernel(bit, rows, own, dq, lat_low, out_t, sums, kept, sent):
    width = lat_low.shape[1]
    which = chosen(own, bit)
    other_rows = out_t.shape[1]
    product = dot(dq[...], lat_low[...], TN)
    first = parted(product, rows, which)
    second = parted(out_t[...].astype(F32).reshape(-1, width), other_rows, which)
    both = [
        jnp.concatenate([a.reshape(-1, rows, width), b.reshape(-1, other_rows, width)], axis=1).reshape(-1, width)
        for a, b in zip(first, second)
    ]
    head = 2 * sums.shape[0]
    kept[...] = both[0].astype(BF16)
    sent[:head, :] = halved(sums[...])
    sent[head:, :] = both[1].astype(BF16)


def side_by_side_kernel(rows, left, right, result):
    product = dot(left[...], right[...], TN).astype(BF16)
    split = product.reshape(-1, 2, rows, product.shape[1])
    result[...] = jnp.concatenate([split[:, 0], split[:, 1]], axis=-1)


def fold_kernel(nxt, end, lanes, extra, own, *refs):
    kept, got, refs = refs[:lanes], refs[lanes : 2 * lanes], refs[2 * lanes :]
    head = 0
    if extra:
        more, refs = refs[0], refs[1:]
        head = 2 * more.shape[0]
        small = more[...] + joined(got[0][:head, :])
        refs[-1][...] = small
    totals = [a[...].astype(F32) + b[head:, :].astype(F32) for a, b in zip(kept, got)]
    if nxt is None:
        for ref, values in zip(refs, end(*totals)):
            ref[...] = values.astype(ref.dtype)
        return
    if len(nxt) < len(totals):
        totals = [jnp.concatenate(totals, axis=1)]
    for k, (total, (bit, inner)) in enumerate(zip(totals, nxt)):
        keep, send = parted(total, inner, chosen(own, bit))
        refs[2 * k][...] = keep.astype(BF16)
        refs[2 * k + 1][head:, :] = send.astype(BF16)
    if extra:
        refs[1][:head, :] = halved(small)


def fold(own, kept, got, extra, nxt, end, name):
    ins = list(kept) + list(got)
    if nxt is not None:
        head = 0 if extra is None else 2 * extra.shape[0]
        shapes = []
        for _ in nxt:
            rows, width = kept[0].shape[0], kept[0].shape[1] * len(kept) // len(nxt)
            shapes += [out((rows // 2, width), BF16), out((head + rows // 2, width), BF16)]
    else:
        shapes = list(jax.eval_shape(end, *(out(v.shape, F32) for v in kept)))
    if extra is not None:
        ins.append(extra)
        shapes.append(out(extra.shape, F32))
    return call(
        functools.partial(fold_kernel, nxt, end, len(kept), extra is not None),
        (1,),
        [whole(v.shape) for v in ins],
        [(whole(s.shape), s) for s in shapes],
        prefetch=1, name=name,
    )(own, *ins)


def place_kernel(block, parts, result):
    peers, _, width = parts.shape
    for p in range(peers):
        for k in range(width // block):
            at = (k * peers + p) * block
            result[:, at : at + block] = parts[p, :, k * block : (k + 1) * block].astype(F32)


def on_device(
    media, latents, counts, gains, biases, w_query, w_keyval, w_out, w_up, w_down, out_grad
):
    slots, patch_rows, width = media.shape
    per_slot = latents.shape[1]
    inner = w_query.shape[1]
    ff = w_up.shape[1]
    n_img, peers = lax.axis_size("img"), lax.axis_size("patch")
    shards = n_img * peers
    scale = 1.0 / math.sqrt(inner // HEADS)
    rows = slots * per_slot
    keys = patch_rows + per_slot
    padded = -(-rows // LANES) * LANES
    gain_spec = whole(gains.shape)
    lat = latents.reshape(rows, width)

    own = jnp.stack([lax.axis_index("patch"), lax.axis_index("img")]).astype(jnp.int32)
    fine = width // shards % 16 == 0 and inner // shards % 16 == 0
    lat_low, q_low, dy = call(
        functools.partial(latent_kernel, per_slot),
        (1,),
        [SMEM, whole((rows, width)), whole((rows, width)), gain_spec, gain_spec, whole(w_query.shape)],
        [
            (whole((rows, width)), out((rows, width), BF16)),
            (whole((rows, inner)), out((rows, inner), BF16)),
            (whole((rows, width)), out((rows, width), BF16)),
        ],
        vmem=62, name="latent",
    )(counts, lat, out_grad.reshape(rows, width), gains, biases, w_query)
    qs = {0: q_low}
    bit = peers // 2
    qs[bit] = swap(q_low, "patch", bit)

    group = slots // 2
    key_input, keyval = call(
        media_kernel,
        (slots // group,),
        [
            leading((group, patch_rows, width)), leading((group * per_slot, width)),
            gain_spec, gain_spec, whole(w_keyval.shape),
        ],
        [
            (leading((group, keys, width)), out((slots, keys, width), BF16)),
            (leading((group, keys, 2 * inner)), out((slots, keys, 2 * inner), BF16)),
        ],
        vmem=62, name="media",
    )(media, lat_low, gains, biases, w_keyval)
    first = after(qs[bit], keyval)
    qs[bit] = first
    while bit > 1:
        bit //= 2
        for j in list(qs):
            qs[j ^ bit] = swap(qs[j], "patch", bit)
    qs = [qs[j] for j in range(peers)]

    pair = 2
    kv_block = leading((pair, keys, 2 * inner))
    part_rows = rows + 2 * HEADS
    stat_out = (whole((HEADS, padded)), out((HEADS, padded), F32))
    parts = call(
        functools.partial(attend_kernel, peers, per_slot, scale),
        (slots // pair,),
        [whole((rows, inner))] * peers + [kv_block],
        [(whole((part_rows, inner)), out((part_rows, inner), BF16))] * peers,
        scratch=[pltpu.VMEM((peers, padded, LANES), F32)],
        name="attend",
    )(*qs, keyval)
    parts = [parts[0]] + [swap(parts[j], "patch", j) for j in range(1, peers)]
    dys = {0: dy, peers // 2: swap(after(dy, *parts[1:]), "patch", peers // 2)}

    attended, att_low, hidden, ff_low, lse = call(
        functools.partial(mix_kernel, peers),
        (1,),
        [whole((part_rows, inner))] * peers
        + [whole((rows, width)), whole(w_out.shape), gain_spec, gain_spec],
        [
            (whole((rows, inner)), out((rows, inner), F32)),
            (whole((rows, inner)), out((rows, inner), BF16)),
            (whole((rows, width)), out((rows, width), F32)),
            (whole((rows, width)), out((rows, width), BF16)),
            stat_out,
        ],
        vmem=40, name="mix",
    )(*parts, lat, w_out, gains, biases)
    bit = peers // 2
    ffs = {0: ff_low, bit: swap(ff_low, "patch", bit)}

    halves = 2
    blocks = ff // (peers * halves * LANES)
    chunk = ff // shards
    strided = chunk % LANES == 0

    def column(own, j, a, k):
        p, k = own[0] ^ j, a * blocks + k
        if strided:
            return ((k // (chunk // LANES)) * peers + p) * (chunk // LANES) + k % (chunk // LANES)
        return p * halves * blocks + k

    def weights(first, stride):
        ups = [
            pl.BlockSpec((width, LANES), lambda g, a, own, k=k: (0, column(own, first + stride * g, a, k)))
            for k in range(blocks)
        ]
        downs = [
            pl.BlockSpec((LANES, width), lambda g, a, own, k=k: (column(own, first + stride * g, a, k), 0))
            for k in range(blocks)
        ]
        return ups + downs

    part = ff // (peers * halves)
    here = peers // 2
    columns = (whole((halves, rows, part)), out((halves, rows, part), BF16))
    wide_low = (whole((rows, width)), out((rows, width), BF16))
    wide = (whole((rows, width)), out((rows, width), F32))
    count = blocks
    far = call(
        functools.partial(feed_kernel, count, here),
        (here, halves),
        [whole((rows, width))] * 2 + weights(here, 1),
        [columns] * (2 * here) + [wide, wide],
        vmem=62, prefetch=1, name="feed",
    )(own, ff_low, dy, *([w_up] * count), *([w_down] * count))
    dys = spread({0: after(dy, ff_low), bit: after(dys[bit], far[-1])})
    ffs[peers // 2] = after(ffs[peers // 2], dys[bit])
    ffs = spread(ffs)

    def cross(values):
        return [swap(v, "patch", here + k) for k, v in enumerate(values)]

    act_cross = cross(after(tuple(far[:here]), ffs[peers // 2]))
    near = call(
        functools.partial(feed_end_kernel, per_slot, count, here),
        (here, halves),
        [SMEM] + [whole((rows, width))] * 2 + weights(here - 1, -1)
        + [whole((rows, width))] * 3 + [whole((rows, inner)), whole((HEADS, padded)), whole(w_out.shape), gain_spec],
        [columns] * (2 * here)
        + [wide_low, wide, wide_low]
        + [(whole((rows + 4 * HEADS, inner)), out((rows + 4 * HEADS, inner), BF16)), (whole((2, width)), out((2, width), F32))],
        scratch=[pltpu.VMEM((rows, width), F32), pltpu.VMEM((rows, width), F32)],
        vmem=62, prefetch=1, name="feed_end",
    )(own, counts, after(ff_low, *ffs[1:], *dys[1:]), dy, *([w_up] * count), *([w_down] * count),
      far[2 * here], far[2 * here + 1], hidden, attended, lse, w_out, gains)
    result, dhidden, dhid_low, datt_low, sums_ff = near[2 * here :]
    act_near, dpre_near = list(reversed(near[:here])), list(reversed(near[here : 2 * here]))

    das = {0: datt_low, peers // 2: swap(datt_low, "patch", peers // 2)}
    out_rows = width // shards // 2
    q_rows = inner // shards
    every, ff_bits = digits_of("img") + digits_of("patch"), digits_of("img")
    ff_orders = [ff_bits[::-1], ff_bits[-2:] + ff_bits[:-2][::-1]]
    named = {"c": ("patch", 1), "x": ("patch", 2), "y": ("img", 1), "z": ("img", 2)}

    def order_of(letters):
        head = [named[k] for k in letters]
        return head + [bit for bit in reversed(every) if bit not in head]

    def ff_lanes(rows):
        return [(order, plan_of(rows, ff_bits, order)) for order in ff_orders]

    def near_swaps(values):
        return [values[0]] + [swap(values[j], "patch", j) for j in range(1, here)]

    kv_order, qo_order = order_of(KV_ORDER), order_of(QO_ORDER)
    acts = near_swaps(act_near) + act_cross
    dpre_first = near_swaps(dpre_near)
    got, sums_of = {}, {}

    def out_grad(mark):
        got["out_t"] = call(
            functools.partial(side_by_side_kernel, out_rows),
            (2,),
            [pl.BlockSpec((rows, width // 2), lambda g: (0, g)), whole((rows, inner))],
            [(leading((shards // 2, out_rows, 2 * inner)), out((shards, out_rows, 2 * inner), BF16))],
            name="out_grad",
        )(after(dhid_low, mark), att_low)[0]
        return got["out_t"]

    def begun(letter, scatter):
        sums_of[letter] = scatter
        mark = scatter.both[0]
        scatter.begin()
        return mark

    def down_grad(mark):
        lanes = ff_lanes(width)
        both = outer(own, dys[:-1] + [after(dys[-1], mark)], acts, width // 2, lanes, "down_grad")
        return begun("D", Scatter(own, both, lanes, lambda t: [t.astype(BF16)], name="down_fold"))

    def send_dpre(mark):
        got["dpres"] = dpre_first + cross(after(tuple(far[here : 2 * here]), mark))
        return mark

    def attend_back(mark):
        near_das = spread({0: das[0], peers // 2: after(das[peers // 2], mark)})
        values = call(
            functools.partial(attend_back_kernel, peers, per_slot, scale),
            (slots // pair,),
            [whole((rows, inner))] * peers + [whole((rows + 4 * HEADS, inner))] * peers + [kv_block],
            [(kv_block, out(keyval.shape, BF16))]
            + [(whole((here, rows, inner)), out((here, rows, inner), BF16))] * 2,
            scratch=[pltpu.VMEM((peers, padded, LANES), F32)],
            name="attend_back",
        )(*qs, *near_das, keyval)
        got["dkv"], near_dq, cross_dq = values
        got["pair"] = (near_dq, swap(cross_dq, "patch", 1))
        return got["dkv"]

    def pair_dq(mark):
        near_dq, other = got["pair"]
        mine, sent = call(
            pair_kernel,
            (1,),
            [whole(near_dq.shape)] * 2,
            [(whole((rows, inner)), out((rows, inner), BF16))] * 2,
            name="pair",
        )(after(near_dq, mark), other)
        got["dqs"] = [mine, swap(sent, "patch", here)]
        return mine

    def keyval_back(mark):
        got["media_grad"], got["dlat"], got["sums_media"] = call(
            keyval_back_kernel,
            (slots // group,),
            [
                leading((group, patch_rows, width)), leading((group, keys, 2 * inner)),
                whole(w_keyval.shape), gain_spec,
            ],
            [
                (leading((group, patch_rows, width)), out(media.shape, BF16)),
                (leading((group * per_slot, width)), out((rows, width), F32)),
                (whole((2, width)), out((2, width), F32)),
            ],
            name="keyval_back",
        )(media, after(got["dkv"], mark), w_keyval, gains)
        return got["sums_media"]

    def keyval_grad(mark):
        lanes = [(kv_order, plan_of(2 * inner, every, kv_order))]
        both = outer(
            own, [after(got["dkv"], mark).reshape(-1, 2 * inner)], [key_input.reshape(-1, width)], 2 * inner // 4,
            lanes, "keyval_grad",
        )
        return begun("K", Scatter(own, both, lanes, lambda t: [t], name="keyval_fold"))

    def up_grad(mark):
        lanes, dpres = ff_lanes(halves * part), got["dpres"]
        both = outer(own, dpres[:-1] + [after(dpres[-1], mark)], ffs, part, lanes, "up_grad")
        end = lambda t: [flipped(t)] if strided else [t.astype(BF16)]
        return begun("U", Scatter(own, both, lanes, end, name="up_fold"))

    def latent_back(mark):
        got["dq_low"], got["latent_grad"], got["sums"] = call(
            functools.partial(latent_back_kernel, here),
            (1,),
            [whole((rows, inner))] * here
            + [whole((rows, width))] * 3 + [whole(w_query.shape), gain_spec, whole((2, width)), whole((2, width))],
            [
                (whole((rows, inner)), out((rows, inner), BF16)),
                (whole((rows, width)), out((rows, width), BF16)),
                (whole((HEADS, width)), out((HEADS, width), F32)),
            ],
            name="latent_back",
        )(*got["dqs"], after(got["dlat"], mark), lat, dhidden, w_query, gains, got["sums_media"], sums_ff)
        return got["dq_low"]

    def open_rows(total):
        other = total[q_rows:]
        return [total[:q_rows], jnp.concatenate([other[:, :inner], other[:, inner:]], axis=0)]

    def query_grad(mark):
        q_plan, qo_plan = plan_of(inner, every, qo_order), plan_of(2 * inner, every, qo_order)
        sums = got["sums"]
        tall = 2 * sums.shape[0] + inner
        ins = (after(got["dq_low"], mark), lat_low, got["out_t"], sums)
        both = call(
            functools.partial(query_kernel, qo_order[0], q_plan[0]),
            (1,),
            [whole(v.shape) for v in ins],
            [(whole((inner, width)), out((inner, width), BF16)), (whole((tall, width)), out((tall, width), BF16))],
            prefetch=1, name="query_grad",
        )(own, *ins)
        return begun("Q", Scatter(own, both, [(qo_order, qo_plan)], open_rows, extra=sums, name="query_fold"))

    tasks = dict(
        O=out_grad, G=down_grad, X=send_dpre, B=attend_back, Y=pair_dq, V=keyval_back, W=keyval_grad, P=up_grad, L=latent_back,
        R=query_grad,
    )
    mark = datt_low
    for letter in ORDER:
        if letter in tasks:
            mark = tasks[letter](mark)
        else:
            one = sums_of[letter]
            mark = one.finish(mark)
            if one.at < one.steps:
                one.begin()
    media_grad, latent_grad = got["media_grad"], got["latent_grad"]
    qo_sum = sums_of["Q"]
    (up_sum,), (kv_sum,), (down,), (q_sum, out_sum) = (sums_of[k].run() for k in "UKDQ")
    small = lax.dynamic_slice_in_dim(
        qo_sum.extra, (own[1] * peers + own[0]) * (width // shards), width // shards, axis=1
    )
    if not strided:
        pairs = [((b % n_img) * peers + b // n_img, b) for b in range(shards)]
        up_sum = lax.ppermute(up_sum, ("img", "patch"), pairs).astype(F32).T

    down = lax.all_to_all(down.reshape(peers, -1, halves * part), "patch", 0, 0, tiled=True)
    down_t = call(
        functools.partial(place_kernel, chunk if strided else halves * part),
        (1,),
        [whole(down.shape)],
        [(whole((width // shards, ff)), out((width // shards, ff), F32))],
        name="down_place",
    )(down)[0]

    return (
        result.reshape(slots, per_slot, width),
        media_grad,
        latent_grad.reshape(slots, per_slot, width),
        q_sum.T,
        kv_sum.T,
        out_sum.T,
        up_sum,
        down_t.T,
        small[:3],
        small[3:6],
    )


def solution(mesh):
    rows = P("img", "patch", None)
    shard = P(None, ("img", "patch"))
    return jax.shard_map(
        on_device,
        mesh=mesh,
        in_specs=(rows, rows, P("img"), P(), P(), P(), P(), P(), P(), P(), rows),
        out_specs=(rows, rows, rows) + (shard,) * 7,
        check_vma=False,
    )
```

```python
import functools
import math

import jax
import jax.numpy as jnp
from jax import lax
from jax.experimental import pallas as pl
from jax.experimental.pallas import tpu as pltpu
from jax.sharding import PartitionSpec as P

HEADS = 8
SLOTS_PER = 5
EPS = 1e-05
LANES = 128
F32 = jnp.float32
BF16 = jnp.bfloat16
MIB = 1024 * 1024
TIMES = dict(latent=2.9, media=2.7, attend=3.1, mix=3.8, feed=0.1, feed_end=36.0, down_grad=4.0, attend_back=1.7, keyval_grad=11.4, up_grad=4.0, keyval_back=4.0, latent_back=1.6, query_grad=1.5, pair=0.8, down_fold=0.8, up_fold=0.8, keyval_fold=0.8, query_fold=1.6, out_grad=0.8)
RATE = 2e+09
ORDER = "OGXBVDWYPKDLRUDUKQQKUQKQKQ"
KV_ORDER, QO_ORDER = "cxyz", "cxyz"


def swap(values, axis, bit):
    n = lax.axis_size(axis)
    return lax.ppermute(values, axis, [(k, k ^ bit) for k in range(n)])


def log2(n):
    return n.bit_length() - 1


def after(values, *others):
    return lax.optimization_barrier((values,) + others)[0]


def spread(blocks):
    n = lax.axis_size("patch")
    blocks = dict(blocks)
    bit = n // 4
    while bit:
        for j in list(blocks):
            blocks[j ^ bit] = swap(blocks[j], "patch", bit)
        bit //= 2
    return [blocks[j] for j in range(n)]


def digits_of(axis):
    n = lax.axis_size(axis)
    return [(axis, 1 << k) for k in reversed(range(log2(n)))]


def chosen(own, bit):
    axis, weight = bit
    return (own[("patch", "img").index(axis)] // weight) % 2


def plan_of(rows, digits, order):
    digits, plan = list(digits), []
    for bit in order:
        at = digits.index(bit)
        plan.append(rows // 2 ** (at + 1))
        del digits[at]
        rows //= 2
    return plan


def parted(values, inner, which):
    width = values.shape[-1]
    split = values.reshape(-1, 2, inner, width)
    low, high = split[:, 0].reshape(-1, width), split[:, 1].reshape(-1, width)
    return jnp.where(which == 1, high, low), jnp.where(which == 1, low, high)


class Scatter:
    def __init__(self, own, both, lanes, end, extra=None, name=None):
        self.own, self.both, self.lanes, self.end = own, both, lanes, end
        self.extra, self.name, self.at, self.open = extra, name, 0, False
        self.steps = len(lanes[0][0])

    def begin(self, *others):
        sent = after(tuple(self.both[1::2]), *others)
        self.got = [swap(v, *order[self.at]) for v, (order, _) in zip(sent, self.lanes)]
        self.at, self.open = self.at + 1, True

    def finish(self, *others):
        kept, self.open = tuple(self.both[::2]), False
        if others:
            kept = after(kept, *others)
        nxt = None
        if self.at < self.steps:
            if all(order[self.at :] == self.lanes[0][0][self.at :] for order, _ in self.lanes):
                self.lanes = self.lanes[:1]
            nxt = [(order[self.at], plan[self.at]) for order, plan in self.lanes]
        values = fold(self.own, kept, self.got, self.extra, nxt, self.end, self.name)
        if self.extra is not None:
            self.extra = values[-1]
            values = values[:-1]
        if nxt is not None:
            self.both = values
        else:
            self.values = values
        return values[0]

    def run(self):
        while self.open:
            self.finish()
            if self.at < self.steps:
                self.begin()
        return self.values


def stats(values):
    average = jnp.mean(values, axis=-1, keepdims=True)
    centred = values - average
    spread = jnp.mean(centred * centred, axis=-1, keepdims=True)
    inverse = lax.rsqrt(spread + EPS)
    return centred * inverse, inverse


def pull(hat, inverse, grad, gain):
    scaled = grad * gain
    first = jnp.mean(scaled, axis=-1, keepdims=True)
    second = jnp.mean(scaled * hat, axis=-1, keepdims=True)
    return inverse * (scaled - first - hat * second)


def gelu_parts(values):
    cdf = 0.5 + 0.5 * lax.erf(values * (1.0 / math.sqrt(2.0)))
    density = jnp.exp(-0.5 * values * values) * (1.0 / math.sqrt(2.0 * math.pi))
    return values * cdf, cdf + values * density


def dot(a, b, dims=((1,), (0,))):
    return lax.dot_general(a, b, (dims, ((), ())), preferred_element_type=F32)


NT = ((1,), (1,))
TN = ((0,), (0,))


def low_lanes(shape):
    return lax.broadcasted_iota(jnp.int32, shape, len(shape) - 1) < LANES // 2


def live_rows(counts_ref, rows, per_slot):
    row = lax.broadcasted_iota(jnp.int32, (rows, 1), 0)
    live = jnp.zeros((rows, 1), F32)
    for sample in range(rows // (per_slot * SLOTS_PER)):
        start = sample * SLOTS_PER * per_slot
        inside = jnp.logical_and(row >= start, row < start + counts_ref[sample] * per_slot)
        live = jnp.where(inside, 1.0, live)
    return live


def paired(block):
    low = low_lanes(block.shape)
    zero = jnp.zeros_like(block)
    return jnp.concatenate([jnp.where(low, block, zero), jnp.where(low, zero, block)], axis=0)


def unpaired(block):
    half = block.shape[0] // 2
    return jnp.where(low_lanes((half, block.shape[1])), block[:half], block[half:])


def flipped(values):
    a, b = values.shape
    tall, wide = -a % LANES, -b % LANES
    if wide:
        values = jnp.concatenate([values, jnp.zeros((a, wide), F32)], axis=1)
    if tall:
        values = jnp.concatenate([values, jnp.zeros((tall, b + wide), F32)], axis=0)
    return values.T[:b, :a]


def call(kernel, grid, ins, outs, scratch=(), vmem=40, prefetch=0, name=None):
    return pl.pallas_call(
        kernel,
        grid_spec=pltpu.PrefetchScalarGridSpec(
            num_scalar_prefetch=prefetch,
            grid=grid,
            in_specs=ins,
            out_specs=[spec for spec, _ in outs],
            scratch_shapes=list(scratch),
        ),
        out_shape=[shape for _, shape in outs],
        compiler_params=pltpu.CompilerParams(
            vmem_limit_bytes=vmem * MIB, dimension_semantics=("arbitrary",) * len(grid)
        ),
        cost_estimate=pl.CostEstimate(flops=int(TIMES.get(name, 0.8) * RATE), bytes_accessed=100000, transcendentals=0),
        name=name,
    )


def whole(shape):
    zeros = (0,) * len(shape)
    return pl.BlockSpec(tuple(shape), lambda *_: zeros)


def leading(shape):
    zeros = (0,) * (len(shape) - 1)
    return pl.BlockSpec(tuple(shape), lambda g, *_: (g,) + zeros)


def out(shape, dtype):
    return jax.ShapeDtypeStruct(tuple(shape), dtype)


SMEM = pl.BlockSpec(memory_space=pltpu.SMEM)


def packed(values):
    high = values.astype(BF16)
    left = values - high.astype(F32)
    middle = left.astype(BF16)
    small = left - middle.astype(F32)
    top = jnp.concatenate([high.astype(F32), middle.astype(F32)], axis=1)
    bottom = jnp.concatenate([small, jnp.zeros_like(small)], axis=1)
    return jnp.concatenate([top, bottom], axis=0).astype(BF16)


def unpacked(values):
    values = values.astype(F32)
    n, m = values.shape[0] // 2, values.shape[1] // 2
    return values[:n, :m] + values[:n, m:] + values[n:, :m]


def latent_kernel(per_slot, counts, lat, grad, gain, bias, w_query, lat_low, q_low, dy):
    hat, _ = stats(lat[...].astype(F32))
    low = (hat * gain[1:2] + bias[1:2]).astype(BF16)
    lat_low[...] = low
    q_low[...] = dot(low, w_query[...]).astype(BF16)
    live = live_rows(counts, lat.shape[0], per_slot)
    dy[...] = (live * grad[...].astype(F32)).astype(BF16)


def media_kernel(media, lat_low, gain, bias, w_keyval, key_input, keyval):
    n, rows, width = media.shape
    hat, _ = stats(media[...].reshape(n * rows, width).astype(F32))
    low = (hat * gain[0:1] + bias[0:1]).astype(BF16)
    key_input[:, :rows, :] = low.reshape(n, rows, width)
    key_input[:, rows:, :] = lat_low[...].reshape(n, -1, width)
    every = key_input[...].reshape(-1, width)
    keyval[...] = dot(every, w_keyval[...]).astype(BF16).reshape(keyval.shape)


def attend_kernel(peers, per_slot, scale, *refs):
    qs, kv, parts, held = refs[:peers], refs[peers], refs[peers + 1 : 2 * peers + 1], refs[2 * peers + 1]
    n, keys, inner = kv.shape[0], kv.shape[1], kv.shape[2] // 2
    step = pl.program_id(0)
    items = [(s, t) for s in range(n) for t in range(inner // LANES)]
    cuts = [slice(t * LANES, (t + 1) * LANES) for t in range(2 * inner // LANES)]
    rows = [pl.multiple_of((step * n + s) * per_slot, per_slot) for s in range(n)]
    ones = jnp.ones((keys, LANES), BF16)

    @pl.when(step == 0)
    def _():
        held[...] = jnp.zeros_like(held)

    scores = []
    for s, t in items:
        q = paired(jnp.concatenate([ref[pl.ds(rows[s], per_slot), cuts[t]] for ref in qs], axis=0))
        scores.append(dot(q, kv[s, :, cuts[t]], NT) * scale)
    tops = [jnp.max(score, axis=-1, keepdims=True) for score in scores]
    probs = [jnp.exp(score - top).astype(BF16) for score, top in zip(scores, tops)]
    sums = [
        dot(prob, jnp.concatenate([kv[s, :, cuts[inner // LANES + t]], ones], axis=1))
        for prob, (s, t) in zip(probs, items)
    ]
    lane = lax.broadcasted_iota(jnp.int32, (peers * per_slot, LANES), 1)
    logs = [jnp.zeros((peers * per_slot, LANES), F32) for _ in range(n)]
    for (s, t), both, top in zip(items, sums, tops):
        total = unpaired(both[:, LANES:])
        o = (unpaired(both[:, :LANES]) / total).astype(BF16)
        lse = unpaired(jnp.broadcast_to(top, (top.shape[0], LANES))) + jnp.log(total)
        here = jnp.logical_or(lane == t, lane == LANES // 2 + HEADS // 2 + t)
        logs[s] = jnp.where(here, lse, logs[s])
        for i in range(peers):
            parts[i][pl.ds(rows[s], per_slot), cuts[t]] = o[i * per_slot : (i + 1) * per_slot]
    for s in range(n):
        for i in range(peers):
            held[i, pl.ds(rows[s], per_slot), :] = logs[s][i * per_slot : (i + 1) * per_slot]

    @pl.when(step == pl.num_programs(0) - 1)
    def _():
        for i in range(peers):
            turned = held[i].T
            turned = turned[:HEADS] + turned[LANES // 2 : LANES // 2 + HEADS]
            parts[i][-2 * HEADS :, :] = packed(turned)


def mix_kernel(peers, *refs):
    parts = refs[:peers]
    lat, w_out, gain, bias, attended, att_low, hidden, ff_low, lse_out = refs[peers:]
    rows, inner = attended.shape
    logs = [unpacked(ref[rows:, :]) for ref in parts]
    top = functools.reduce(jnp.maximum, logs)
    lse = top + jnp.log(sum(jnp.exp(v - top) for v in logs))
    lse_out[...] = lse
    weights = flipped(jnp.concatenate([jnp.exp(v - lse) for v in logs], axis=0))[:rows]
    low = low_lanes((rows, LANES))
    for t in range(inner // LANES):
        cut = slice(t * LANES, (t + 1) * LANES)
        total = jnp.zeros((rows, LANES), F32)
        for j in range(peers):
            at = j * HEADS + t
            other = at + HEADS // 2
            weight = jnp.where(low, weights[:, at : at + 1], weights[:, other : other + 1])
            total = total + weight * parts[j][:rows, cut].astype(F32)
        attended[:, cut] = total
        att_low[:, cut] = total.astype(BF16)
    state = lat[...].astype(F32) + dot(att_low[...], w_out[...])
    hidden[...] = state
    hat, _ = stats(state)
    ff_low[...] = (hat * gain[2:3] + bias[2:3]).astype(BF16)


def feed_columns(ff_low, dy, ups, downs, acts, dpres, res, dff):
    half = len(ups) // 2
    a = pl.program_id(1)
    parts = []
    for at in (slice(0, half), slice(half, 2 * half)):
        up = jnp.concatenate([ref[...] for ref in ups[at]], axis=1)
        down = jnp.concatenate([ref[...] for ref in downs[at]], axis=0)
        parts.append((up, down, dot(ff_low[...], up), dot(dy[...], down, NT)))
    done = []
    for up, down, pre, dact in parts:
        value, slope = gelu_parts(pre)
        value = value.astype(BF16)
        back = (slope * dact).astype(BF16)
        res[...] += dot(value, down)
        dff[...] += dot(back, up, NT)
        done.append((value, back))
    for at, (act, dpre) in enumerate(zip(acts, dpres)):

        @pl.when(pl.program_id(0) == at)
        def _():
            width = done[0][0].shape[1]
            for k, (value, back) in enumerate(done):
                act[a, :, k * width : (k + 1) * width] = value
                dpre[a, :, k * width : (k + 1) * width] = back


def first_step():
    return jnp.logical_and(pl.program_id(0) == 0, pl.program_id(1) == 0)


def last_step():
    ends = [pl.program_id(k) == pl.num_programs(k) - 1 for k in range(2)]
    return jnp.logical_and(*ends)


def feed_kernel(count, here, own, ff_low, dy, *refs):
    ups, downs, refs = refs[:count], refs[count : 2 * count], refs[2 * count :]
    acts, dpres, (res, dff) = refs[:here], refs[here : 2 * here], refs[2 * here :]

    @pl.when(first_step())
    def _():
        res[...] = jnp.zeros_like(res)
        dff[...] = jnp.zeros_like(dff)

    feed_columns(ff_low, dy, ups, downs, acts, dpres, res, dff)


def feed_end_kernel(per_slot, count, here, own, counts, ff_low, dy, *refs):
    ups, downs, refs = refs[:count], refs[count : 2 * count], refs[2 * count :]
    res_in, dff_in, hidden, attended, lse, w_out, gain = refs[:7]
    acts, dpres, refs = refs[7 : 7 + here], refs[7 + here : 7 + 2 * here], refs[7 + 2 * here :]
    result, dhidden, dhid_low, datt_low, sums, res, dff = refs

    @pl.when(first_step())
    def _():
        res[...] = res_in[...]
        dff[...] = dff_in[...]

    feed_columns(ff_low, dy, ups, downs, acts, dpres, res, dff)

    @pl.when(last_step())
    def _():
        rows, inner = attended.shape
        live = live_rows(counts, rows, per_slot)
        state = hidden[...]
        result[...] = (live * (state + res[...])).astype(BF16)
        hat, inverse = stats(state)
        grad = dff[...]
        sums[0:1] = jnp.sum(grad * hat, axis=0, keepdims=True)
        sums[1:2] = jnp.sum(grad, axis=0, keepdims=True)
        back = dy[...].astype(F32) + pull(hat, inverse, grad, gain[2:3])
        dhidden[...] = back
        dhid_low[...] = back.astype(BF16)
        datt = dot(dhid_low[...], w_out[...], NT).astype(BF16)
        datt_low[:rows, :] = datt
        product = datt.astype(F32) * attended[...]
        low = low_lanes((rows, LANES))
        lane = lax.broadcasted_iota(jnp.int32, (rows, LANES), 1)
        delta = jnp.zeros((rows, LANES), F32)
        for t in range(inner // LANES):
            both = product[:, t * LANES : (t + 1) * LANES]
            first = jnp.sum(jnp.where(low, both, 0.0), axis=-1, keepdims=True)
            second = jnp.sum(jnp.where(low, 0.0, both), axis=-1, keepdims=True)
            delta = jnp.where(lane == t, first, delta)
            delta = jnp.where(lane == HEADS // 2 + t, second, delta)
        turned = flipped(jnp.concatenate([delta, jnp.zeros((-rows % LANES, LANES), F32)], axis=0))
        datt_low[rows:, :] = packed(jnp.concatenate([lse[...], turned[:HEADS]], axis=0))


def attend_back_kernel(peers, per_slot, scale, *refs):
    qs, das, kv, dkv = refs[:peers], refs[peers : 2 * peers], refs[2 * peers], refs[2 * peers + 1]
    (near, cross), held = refs[2 * peers + 2 : 2 * peers + 4], refs[2 * peers + 4]
    dqs = [(cross if i % 2 else near, i // 2) for i in range(peers)]
    n, inner = kv.shape[0], kv.shape[2] // 2
    step = pl.program_id(0)
    items = [(s, t) for s in range(n) for t in range(inner // LANES)]
    cuts = [slice(t * LANES, (t + 1) * LANES) for t in range(2 * inner // LANES)]
    rows = [pl.multiple_of((step * n + s) * per_slot, per_slot) for s in range(n)]
    later = inner // LANES

    @pl.when(step == 0)
    def _():
        for i in range(peers):
            turned = unpacked(das[i][-4 * HEADS :, :])
            held[i, :, : 2 * HEADS] = flipped(turned)

    def column(block, h):
        other = h + HEADS // 2
        return jnp.concatenate([block[:, h : h + 1], block[:, other : other + 1]], axis=0)

    sts = [
        jnp.concatenate([held[i, pl.ds(row, per_slot), :] for i in range(peers)], axis=0) for row in rows
    ]
    qp = [paired(jnp.concatenate([ref[pl.ds(rows[s], per_slot), cuts[t]] for ref in qs], axis=0)) for s, t in items]
    dp = [paired(jnp.concatenate([ref[pl.ds(rows[s], per_slot), cuts[t]] for ref in das], axis=0)) for s, t in items]
    scores = [dot(q, kv[s, :, cuts[t]], NT) for q, (s, t) in zip(qp, items)]
    dprobs = [dot(d, kv[s, :, cuts[later + t]], NT) for d, (s, t) in zip(dp, items)]
    probs = [jnp.exp(score * scale - column(sts[s], t)) for score, (s, t) in zip(scores, items)]
    dscores = [
        (prob * (dprob - column(sts[s], HEADS + t))).astype(BF16)
        for prob, dprob, (s, t) in zip(probs, dprobs, items)
    ]
    for (s, t), prob, d in zip(items, probs, dp):
        dkv[s, :, cuts[later + t]] = dot(prob.astype(BF16), d, TN).astype(BF16)
    for (s, t), ds, q in zip(items, dscores, qp):
        dkv[s, :, cuts[t]] = (dot(ds, q, TN) * scale).astype(BF16)
    for (s, t), ds in zip(items, dscores):
        dq = (unpaired(dot(ds, kv[s, :, cuts[t]])) * scale).astype(BF16)
        for i in range(peers):
            ref, at = dqs[i]
            ref[at, pl.ds(rows[s], per_slot), cuts[t]] = dq[i * per_slot : (i + 1) * per_slot]


def pair_kernel(near, other, mine, sent):
    total = near[...].astype(F32) + other[...].astype(F32)
    mine[...] = total[0].astype(BF16)
    sent[...] = total[1].astype(BF16)


def keyval_back_kernel(media, dkv, w_keyval, gain, media_grad, dlat, sums):
    n, rows, width = media.shape
    grad = dot(dkv[...].reshape(-1, dkv.shape[2]), w_keyval[...], NT).reshape(n, -1, width)
    dlat[...] = grad[:, rows:].reshape(dlat.shape)
    grad = grad[:, :rows].reshape(n * rows, width)
    hat, inverse = stats(media[...].reshape(n * rows, width).astype(F32))
    media_grad[...] = pull(hat, inverse, grad, gain[0:1]).astype(BF16).reshape(media_grad.shape)

    @pl.when(pl.program_id(0) == 0)
    def _():
        sums[...] = jnp.zeros_like(sums)

    sums[0:1] += jnp.sum(grad * hat, axis=0, keepdims=True)
    sums[1:2] += jnp.sum(grad, axis=0, keepdims=True)


def latent_back_kernel(peers, *refs):
    dqs = refs[:peers]
    dlat, lat, dhidden, w_query, gain, sums_media, sums_ff, dq_low, latent_grad, sums = refs[peers:]
    dq = sum(ref[...].astype(F32) for ref in dqs).astype(BF16)
    dq_low[...] = dq
    grad = dlat[...] + dot(dq, w_query[...], NT)
    hat, inverse = stats(lat[...].astype(F32))
    latent_grad[...] = (dhidden[...] + pull(hat, inverse, grad, gain[1:2])).astype(BF16)
    sums[0:1] = sums_media[0:1]
    sums[1:2] = jnp.sum(grad * hat, axis=0, keepdims=True)
    sums[2:3] = sums_ff[0:1]
    sums[3:4] = sums_media[1:2]
    sums[4:5] = jnp.sum(grad, axis=0, keepdims=True)
    sums[5:6] = sums_ff[1:2]


def halved(values):
    high = values.astype(BF16).astype(F32)
    return jnp.concatenate([high, values - high], axis=0).astype(BF16)


def joined(values):
    values = values.astype(F32)
    half = values.shape[0] // 2
    return values[:half] + values[half:]


def outer_kernel(count, lanes, own, *refs):
    lefts, rights, refs = refs[:count], refs[count : 2 * count], refs[2 * count :]
    results, held = refs[:-1], refs[-1]

    @pl.when(pl.program_id(0) == 0)
    def _():
        at = 0
        for ref in rights:
            rows, width = ref.shape[-2:]
            for k in range(held.shape[1] // width):
                held[at : at + rows, k * width : (k + 1) * width] = ref[k] if len(ref.shape) == 3 else ref[...]
            at += rows

    left = jnp.concatenate([ref[...].reshape(-1, ref.shape[-1]) for ref in lefts], axis=0)
    product = dot(left, held[...], TN)
    width = product.shape[1] // len(lanes)
    for k, (bit, inner) in enumerate(lanes):
        kept, sent = parted(product[:, k * width : (k + 1) * width], inner, chosen(own, bit))
        results[2 * k][...] = kept.astype(BF16)
        results[2 * k + 1][...] = sent.astype(BF16)


def outer(own, lefts, rights, tile, lanes, name):
    count = len(lefts)
    wide = lambda v: v.shape[-1] * (v.shape[0] if v.ndim == 3 else 1)
    a, b = wide(lefts[0]), wide(rights[0])

    def left_spec(v):
        if v.ndim == 3:
            return pl.BlockSpec((1, v.shape[1], tile), lambda g, *_: (g, 0, 0))
        return pl.BlockSpec((v.shape[0], tile), lambda g, *_: (0, g))

    total = sum(v.shape[-2] for v in rights)
    steps, part = a // tile, b // len(lanes)
    spec = pl.BlockSpec((tile // 2, part), lambda g, *_: (g, 0))
    return call(
        functools.partial(outer_kernel, count, [(order[0], plan[0]) for order, plan in lanes]),
        (steps,),
        [left_spec(v) for v in lefts] + [whole(v.shape) for v in rights],
        [(spec, out((a // 2, part), BF16))] * (2 * len(lanes)),
        scratch=[pltpu.VMEM((total, b), BF16)],
        prefetch=1, name=name,
    )(own, *lefts, *rights)


def query_kernel(bit, rows, own, dq, lat_low, out_t, sums, kept, sent):
    width = lat_low.shape[1]
    which = chosen(own, bit)
    other_rows = out_t.shape[1]
    product = dot(dq[...], lat_low[...], TN)
    first = parted(product, rows, which)
    second = parted(out_t[...].astype(F32).reshape(-1, width), other_rows, which)
    both = [
        jnp.concatenate([a.reshape(-1, rows, width), b.reshape(-1, other_rows, width)], axis=1).reshape(-1, width)
        for a, b in zip(first, second)
    ]
    head = 2 * sums.shape[0]
    kept[...] = both[0].astype(BF16)
    sent[:head, :] = halved(sums[...])
    sent[head:, :] = both[1].astype(BF16)


def side_by_side_kernel(rows, left, right, result):
    product = dot(left[...], right[...], TN).astype(BF16)
    split = product.reshape(-1, 2, rows, product.shape[1])
    result[...] = jnp.concatenate([split[:, 0], split[:, 1]], axis=-1)


def fold_kernel(nxt, end, lanes, extra, own, *refs):
    kept, got, refs = refs[:lanes], refs[lanes : 2 * lanes], refs[2 * lanes :]
    head = 0
    if extra:
        more, refs = refs[0], refs[1:]
        head = 2 * more.shape[0]
        small = more[...] + joined(got[0][:head, :])
        refs[-1][...] = small
    totals = [a[...].astype(F32) + b[head:, :].astype(F32) for a, b in zip(kept, got)]
    if nxt is None:
        for ref, values in zip(refs, end(*totals)):
            ref[...] = values.astype(ref.dtype)
        return
    if len(nxt) < len(totals):
        totals = [jnp.concatenate(totals, axis=1)]
    for k, (total, (bit, inner)) in enumerate(zip(totals, nxt)):
        keep, send = parted(total, inner, chosen(own, bit))
        refs[2 * k][...] = keep.astype(BF16)
        refs[2 * k + 1][head:, :] = send.astype(BF16)
    if extra:
        refs[1][:head, :] = halved(small)


def fold(own, kept, got, extra, nxt, end, name):
    ins = list(kept) + list(got)
    if nxt is not None:
        head = 0 if extra is None else 2 * extra.shape[0]
        shapes = []
        for _ in nxt:
            rows, width = kept[0].shape[0], kept[0].shape[1] * len(kept) // len(nxt)
            shapes += [out((rows // 2, width), BF16), out((head + rows // 2, width), BF16)]
    else:
        shapes = list(jax.eval_shape(end, *(out(v.shape, F32) for v in kept)))
    if extra is not None:
        ins.append(extra)
        shapes.append(out(extra.shape, F32))
    return call(
        functools.partial(fold_kernel, nxt, end, len(kept), extra is not None),
        (1,),
        [whole(v.shape) for v in ins],
        [(whole(s.shape), s) for s in shapes],
        prefetch=1, name=name,
    )(own, *ins)


def place_kernel(block, parts, result):
    peers, _, width = parts.shape
    for p in range(peers):
        for k in range(width // block):
            at = (k * peers + p) * block
            result[:, at : at + block] = parts[p, :, k * block : (k + 1) * block].astype(F32)


def on_device(
    media, latents, counts, gains, biases, w_query, w_keyval, w_out, w_up, w_down, out_grad
):
    slots, patch_rows, width = media.shape
    per_slot = latents.shape[1]
    inner = w_query.shape[1]
    ff = w_up.shape[1]
    n_img, peers = lax.axis_size("img"), lax.axis_size("patch")
    shards = n_img * peers
    scale = 1.0 / math.sqrt(inner // HEADS)
    rows = slots * per_slot
    keys = patch_rows + per_slot
    padded = -(-rows // LANES) * LANES
    gain_spec = whole(gains.shape)
    lat = latents.reshape(rows, width)

    own = jnp.stack([lax.axis_index("patch"), lax.axis_index("img")]).astype(jnp.int32)
    fine = width // shards % 16 == 0 and inner // shards % 16 == 0
    lat_low, q_low, dy = call(
        functools.partial(latent_kernel, per_slot),
        (1,),
        [SMEM, whole((rows, width)), whole((rows, width)), gain_spec, gain_spec, whole(w_query.shape)],
        [
            (whole((rows, width)), out((rows, width), BF16)),
            (whole((rows, inner)), out((rows, inner), BF16)),
            (whole((rows, width)), out((rows, width), BF16)),
        ],
        vmem=62, name="latent",
    )(counts, lat, out_grad.reshape(rows, width), gains, biases, w_query)
    qs = {0: q_low}
    bit = peers // 2
    qs[bit] = swap(q_low, "patch", bit)

    group = slots // 2
    key_input, keyval = call(
        media_kernel,
        (slots // group,),
        [
            leading((group, patch_rows, width)), leading((group * per_slot, width)),
            gain_spec, gain_spec, whole(w_keyval.shape),
        ],
        [
            (leading((group, keys, width)), out((slots, keys, width), BF16)),
            (leading((group, keys, 2 * inner)), out((slots, keys, 2 * inner), BF16)),
        ],
        vmem=62, name="media",
    )(media, lat_low, gains, biases, w_keyval)
    first = after(qs[bit], keyval)
    qs[bit] = first
    while bit > 1:
        bit //= 2
        for j in list(qs):
            qs[j ^ bit] = swap(qs[j], "patch", bit)
    qs = [qs[j] for j in range(peers)]

    pair = 2
    kv_block = leading((pair, keys, 2 * inner))
    part_rows = rows + 2 * HEADS
    stat_out = (whole((HEADS, padded)), out((HEADS, padded), F32))
    parts = call(
        functools.partial(attend_kernel, peers, per_slot, scale),
        (slots // pair,),
        [whole((rows, inner))] * peers + [kv_block],
        [(whole((part_rows, inner)), out((part_rows, inner), BF16))] * peers,
        scratch=[pltpu.VMEM((peers, padded, LANES), F32)],
        name="attend",
    )(*qs, keyval)
    parts = [parts[0]] + [swap(parts[j], "patch", j) for j in range(1, peers)]
    dys = {0: dy, peers // 2: swap(after(dy, *parts[1:]), "patch", peers // 2)}

    attended, att_low, hidden, ff_low, lse = call(
        functools.partial(mix_kernel, peers),
        (1,),
        [whole((part_rows, inner))] * peers
        + [whole((rows, width)), whole(w_out.shape), gain_spec, gain_spec],
        [
            (whole((rows, inner)), out((rows, inner), F32)),
            (whole((rows, inner)), out((rows, inner), BF16)),
            (whole((rows, width)), out((rows, width), F32)),
            (whole((rows, width)), out((rows, width), BF16)),
            stat_out,
        ],
        vmem=40, name="mix",
    )(*parts, lat, w_out, gains, biases)
    bit = peers // 2
    ffs = {0: ff_low, bit: swap(ff_low, "patch", bit)}

    halves = 2
    blocks = ff // (peers * halves * LANES)
    chunk = ff // shards
    strided = chunk % LANES == 0

    def column(own, j, a, k):
        p, k = own[0] ^ j, a * blocks + k
        if strided:
            return ((k // (chunk // LANES)) * peers + p) * (chunk // LANES) + k % (chunk // LANES)
        return p * halves * blocks + k

    def weights(first, stride):
        ups = [
            pl.BlockSpec((width, LANES), lambda g, a, own, k=k: (0, column(own, first + stride * g, a, k)))
            for k in range(blocks)
        ]
        downs = [
            pl.BlockSpec((LANES, width), lambda g, a, own, k=k: (column(own, first + stride * g, a, k), 0))
            for k in range(blocks)
        ]
        return ups + downs

    part = ff // (peers * halves)
    here = peers // 2
    columns = (whole((halves, rows, part)), out((halves, rows, part), BF16))
    wide_low = (whole((rows, width)), out((rows, width), BF16))
    wide = (whole((rows, width)), out((rows, width), F32))
    count = blocks
    far = call(
        functools.partial(feed_kernel, count, here),
        (here, halves),
        [whole((rows, width))] * 2 + weights(here, 1),
        [columns] * (2 * here) + [wide, wide],
        vmem=62, prefetch=1, name="feed",
    )(own, ff_low, dy, *([w_up] * count), *([w_down] * count))
    dys = spread({0: after(dy, ff_low), bit: after(dys[bit], far[-1])})
    ffs[peers // 2] = after(ffs[peers // 2], dys[bit])
    ffs = spread(ffs)

    def cross(values):
        return [swap(v, "patch", here + k) for k, v in enumerate(values)]

    act_cross = cross(after(tuple(far[:here]), ffs[peers // 2]))
    near = call(
        functools.partial(feed_end_kernel, per_slot, count, here),
        (here, halves),
        [SMEM] + [whole((rows, width))] * 2 + weights(here - 1, -1)
        + [whole((rows, width))] * 3 + [whole((rows, inner)), whole((HEADS, padded)), whole(w_out.shape), gain_spec],
        [columns] * (2 * here)
        + [wide_low, wide, wide_low]
        + [(whole((rows + 4 * HEADS, inner)), out((rows + 4 * HEADS, inner), BF16)), (whole((2, width)), out((2, width), F32))],
        scratch=[pltpu.VMEM((rows, width), F32), pltpu.VMEM((rows, width), F32)],
        vmem=52, prefetch=1, name="feed_end",
    )(own, counts, after(ff_low, *ffs[1:], *dys[1:]), dy, *([w_up] * count), *([w_down] * count),
      far[2 * here], far[2 * here + 1], hidden, attended, lse, w_out, gains)
    result, dhidden, dhid_low, datt_low, sums_ff = near[2 * here :]
    act_near, dpre_near = list(reversed(near[:here])), list(reversed(near[here : 2 * here]))

    das = {0: datt_low, peers // 2: swap(datt_low, "patch", peers // 2)}
    out_rows = width // shards // 2
    q_rows = inner // shards
    every, ff_bits = digits_of("img") + digits_of("patch"), digits_of("img")
    ff_orders = [ff_bits[::-1], ff_bits[-2:] + ff_bits[:-2][::-1]]
    named = {"c": ("patch", 1), "x": ("patch", 2), "y": ("img", 1), "z": ("img", 2)}

    def order_of(letters):
        head = [named[k] for k in letters]
        return head + [bit for bit in reversed(every) if bit not in head]

    def ff_lanes(rows):
        return [(order, plan_of(rows, ff_bits, order)) for order in ff_orders]

    def near_swaps(values):
        return [values[0]] + [swap(values[j], "patch", j) for j in range(1, here)]

    kv_order, qo_order = order_of(KV_ORDER), order_of(QO_ORDER)
    acts = near_swaps(act_near) + act_cross
    dpre_first = near_swaps(dpre_near)
    got, sums_of = {}, {}

    def out_grad(mark):
        got["out_t"] = call(
            functools.partial(side_by_side_kernel, out_rows),
            (2,),
            [pl.BlockSpec((rows, width // 2), lambda g: (0, g)), whole((rows, inner))],
            [(leading((shards // 2, out_rows, 2 * inner)), out((shards, out_rows, 2 * inner), BF16))],
            name="out_grad",
        )(after(dhid_low, mark), att_low)[0]
        return got["out_t"]

    def begun(letter, scatter):
        sums_of[letter] = scatter
        mark = scatter.both[0]
        scatter.begin()
        return mark

    def down_grad(mark):
        lanes = ff_lanes(width)
        both = outer(own, dys[:-1] + [after(dys[-1], mark)], acts, width // 2, lanes, "down_grad")
        return begun("D", Scatter(own, both, lanes, lambda t: [t.astype(BF16)], name="down_fold"))

    def send_dpre(mark):
        got["dpres"] = dpre_first + cross(after(tuple(far[here : 2 * here]), mark))
        return mark

    def attend_back(mark):
        near_das = spread({0: das[0], peers // 2: after(das[peers // 2], mark)})
        values = call(
            functools.partial(attend_back_kernel, peers, per_slot, scale),
            (slots // pair,),
            [whole((rows, inner))] * peers + [whole((rows + 4 * HEADS, inner))] * peers + [kv_block],
            [(kv_block, out(keyval.shape, BF16))]
            + [(whole((here, rows, inner)), out((here, rows, inner), BF16))] * 2,
            scratch=[pltpu.VMEM((peers, padded, LANES), F32)],
            name="attend_back",
        )(*qs, *near_das, keyval)
        got["dkv"], near_dq, cross_dq = values
        got["pair"] = (near_dq, swap(cross_dq, "patch", 1))
        return got["dkv"]

    def pair_dq(mark):
        near_dq, other = got["pair"]
        mine, sent = call(
            pair_kernel,
            (1,),
            [whole(near_dq.shape)] * 2,
            [(whole((rows, inner)), out((rows, inner), BF16))] * 2,
            name="pair",
        )(after(near_dq, mark), other)
        got["dqs"] = [mine, swap(sent, "patch", here)]
        return mine

    def keyval_back(mark):
        got["media_grad"], got["dlat"], got["sums_media"] = call(
            keyval_back_kernel,
            (slots // group,),
            [
                leading((group, patch_rows, width)), leading((group, keys, 2 * inner)),
                whole(w_keyval.shape), gain_spec,
            ],
            [
                (leading((group, patch_rows, width)), out(media.shape, BF16)),
                (leading((group * per_slot, width)), out((rows, width), F32)),
                (whole((2, width)), out((2, width), F32)),
            ],
            name="keyval_back",
        )(media, after(got["dkv"], mark), w_keyval, gains)
        return got["sums_media"]

    def keyval_grad(mark):
        lanes = [(kv_order, plan_of(2 * inner, every, kv_order))]
        both = outer(
            own, [after(got["dkv"], mark).reshape(-1, 2 * inner)], [key_input.reshape(-1, width)], 2 * inner // 4,
            lanes, "keyval_grad",
        )
        return begun("K", Scatter(own, both, lanes, lambda t: [t], name="keyval_fold"))

    def up_grad(mark):
        lanes, dpres = ff_lanes(halves * part), got["dpres"]
        both = outer(own, dpres[:-1] + [after(dpres[-1], mark)], ffs, part, lanes, "up_grad")
        end = lambda t: [flipped(t)] if strided else [t.astype(BF16)]
        return begun("U", Scatter(own, both, lanes, end, name="up_fold"))

    def latent_back(mark):
        got["dq_low"], got["latent_grad"], got["sums"] = call(
            functools.partial(latent_back_kernel, here),
            (1,),
            [whole((rows, inner))] * here
            + [whole((rows, width))] * 3 + [whole(w_query.shape), gain_spec, whole((2, width)), whole((2, width))],
            [
                (whole((rows, inner)), out((rows, inner), BF16)),
                (whole((rows, width)), out((rows, width), BF16)),
                (whole((HEADS, width)), out((HEADS, width), F32)),
            ],
            name="latent_back",
        )(*got["dqs"], after(got["dlat"], mark), lat, dhidden, w_query, gains, got["sums_media"], sums_ff)
        return got["dq_low"]

    def open_rows(total):
        other = total[q_rows:]
        return [total[:q_rows], jnp.concatenate([other[:, :inner], other[:, inner:]], axis=0)]

    def query_grad(mark):
        q_plan, qo_plan = plan_of(inner, every, qo_order), plan_of(2 * inner, every, qo_order)
        sums = got["sums"]
        tall = 2 * sums.shape[0] + inner
        ins = (after(got["dq_low"], mark), lat_low, got["out_t"], sums)
        both = call(
            functools.partial(query_kernel, qo_order[0], q_plan[0]),
            (1,),
            [whole(v.shape) for v in ins],
            [(whole((inner, width)), out((inner, width), BF16)), (whole((tall, width)), out((tall, width), BF16))],
            prefetch=1, name="query_grad",
        )(own, *ins)
        return begun("Q", Scatter(own, both, [(qo_order, qo_plan)], open_rows, extra=sums, name="query_fold"))

    tasks = dict(
        O=out_grad, G=down_grad, X=send_dpre, B=attend_back, Y=pair_dq, V=keyval_back, W=keyval_grad, P=up_grad, L=latent_back,
        R=query_grad,
    )
    mark = datt_low
    for letter in ORDER:
        if letter in tasks:
            mark = tasks[letter](mark)
        else:
            one = sums_of[letter]
            mark = one.finish(mark)
            if one.at < one.steps:
                one.begin()
    media_grad, latent_grad = got["media_grad"], got["latent_grad"]
    qo_sum = sums_of["Q"]
    (up_sum,), (kv_sum,), (down,), (q_sum, out_sum) = (sums_of[k].run() for k in "UKDQ")
    small = lax.dynamic_slice_in_dim(
        qo_sum.extra, (own[1] * peers + own[0]) * (width // shards), width // shards, axis=1
    )
    if not strided:
        pairs = [((b % n_img) * peers + b // n_img, b) for b in range(shards)]
        up_sum = lax.ppermute(up_sum, ("img", "patch"), pairs).astype(F32).T

    down = lax.all_to_all(down.reshape(peers, -1, halves * part), "patch", 0, 0, tiled=True)
    down_t = call(
        functools.partial(place_kernel, chunk if strided else halves * part),
        (1,),
        [whole(down.shape)],
        [(whole((width // shards, ff)), out((width // shards, ff), F32))],
        name="down_place",
    )(down)[0]

    return (
        result.reshape(slots, per_slot, width),
        media_grad,
        latent_grad.reshape(slots, per_slot, width),
        q_sum.T,
        kv_sum.T,
        out_sum.T,
        up_sum,
        down_t.T,
        small[:3],
        small[3:6],
    )


def solution(mesh):
    rows = P("img", "patch", None)
    shard = P(None, ("img", "patch"))
    return jax.shard_map(
        on_device,
        mesh=mesh,
        in_specs=(rows, rows, P("img"), P(), P(), P(), P(), P(), P(), P(), rows),
        out_specs=(rows, rows, rows) + (shard,) * 7,
        check_vma=False,
    )
```
